32 devices in a mesh: seg: 8 (over z, core), sec: 4 (over y, x).
Axes of the slice: x: 2, y: 2, z: 4, core: 2. Of those that a mesh axis runs over, the one named last changes fastest.
Arguments:
- left_env: bfloat16 [8, 4, 16, 256, 256], P('seg', 'sec'), as said below
- right_env: bfloat16 [8, 4, 16, 256, 256], P('seg', 'sec'), as said below
- left_piece: bfloat16 [8, 4, 256, 256], P('seg', 'sec'), may hold values from -0.375 to 0.375
- right_piece: bfloat16 [8, 4, 256, 256], P('seg', 'sec'), may hold values from -0.375 to 0.375
- guess: bfloat16 [8, 4, 256, 256], P('seg', 'sec'), may hold values from -0.375 to 0.375
- inverse_values: float32 [8, 4, 256], P('seg', 'sec'), may hold values from 0.5 to 4
- precond: bfloat16 [8, 4, 256, 256], P('seg', 'sec'), may hold values from 0.25 to 2
- sector_rows: int32 [8, 4], P('seg', 'sec'), may hold values from 64 to 256, as said below
Outputs:
- polar_factor: float32 [8, 4, 256, 256], P('seg', 'sec')
- next_left: bfloat16 [8, 4, 256, 256], P('seg', 'sec')
- energies: float32 [8], P('seg')
The draws below stay inside these ranges and needn't reach their ends.
Inputs may be any that keep to these rules, and one draw needn't show every extreme that they name: `sector_rows`: some block has 256 live states and some has 64. `left_env`: each channel's block is symmetric. `right_env`: each channel's block is symmetric.
All inputs are finite; a program needn't handle non-finite values.
Results may differ from the reference program's by a relative error of at most 0.006.
Values may be sent and summed in bfloat16 or wider, within the bound.
No kernel may reach another device: no remote copies, remote signals or barrier semaphores. Data moves between devices by JAX's collectives and lax.ppermute only.
A program may use at most 64 MiB of HBM per device.

```python
import math
import jax
import jax.numpy as jnp
from jax import lax

BLOCK = 256
WD = 2
ITERS = 2
NS_STEPS = 3
WT = 16
SEGS = 8
SECTORS = 4


def symmetric_env(key):
    shape = (SEGS, SECTORS, WT, BLOCK, BLOCK)
    base = jax.random.normal(key, shape, jnp.float32)
    sym = (base + jnp.swapaxes(base, -1, -2)) * 0.5 ** 0.5 * BLOCK ** (-0.5)
    return sym.astype(jnp.bfloat16)


def draw_left_env(key, part):
    return symmetric_env(jax.random.fold_in(key, 11))


def draw_right_env(key, part):
    return symmetric_env(jax.random.fold_in(key, 23))


def draw_sector_rows(key, part):
    total = SEGS * SECTORS
    rows = jax.random.randint(jax.random.fold_in(key, 31), (total,), BLOCK // 4, BLOCK + 1)
    first = jax.random.randint(jax.random.fold_in(key, 37), (), 0, total)
    second = (first + 1) % total
    rows = rows.at[first].set(BLOCK)
    rows = rows.at[second].set(BLOCK // 4)
    return rows.reshape(SEGS, SECTORS).astype(jnp.int32)


def level_of(key, extent, cuts, low, high):
    def one(position, shards_of):
        heights = jax.random.uniform(jax.random.fold_in(jax.random.fold_in(key, 6), position), (shards_of,), jnp.float32, low / len(cuts), high / len(cuts))
        return jnp.repeat(jnp.exp(heights), extent[position] // shards_of).reshape((-1,) + (1,) * (len(extent) - position - 1))

    factor_of = one(*cuts[0])
    for cut in cuts[1:]:
        factor_of = factor_of * one(*cut)
    return factor_of


def normal_values(stream_key, extent, spread, reach, cuts=(), held_as=jnp.bfloat16):
    result = jax.random.normal(stream_key, extent, jnp.float32) * spread
    if len(cuts) > 0:
        result = level_of(stream_key, extent, cuts, -0.22, 0.18) * result
    return jnp.clip(result, min=-reach, max=reach).astype(held_as)


def setup_inputs(seed: int = 0) -> dict:
    keys = jax.random.split(jax.random.key(seed), 9)
    return {
        "left_env": draw_left_env(jax.random.fold_in(keys[8], 71), 0),
        "right_env": draw_right_env(jax.random.fold_in(keys[8], 71), 0),
        "left_piece": normal_values(keys[2], (SEGS, SECTORS, BLOCK, BLOCK), BLOCK ** -0.5, 0.375, ((0, 8), (1, 4))),
        "right_piece": normal_values(keys[3], (SEGS, SECTORS, BLOCK, BLOCK), BLOCK ** -0.5, 0.375, ((0, 8), (1, 4))),
        "guess": normal_values(keys[4], (SEGS, SECTORS, BLOCK, BLOCK), BLOCK ** -0.5, 0.375, ((0, 8), (1, 4))),
        "inverse_values": jnp.clip(jnp.exp(math.log(4.0) - 2.0794415 * jax.random.uniform(keys[5], (SEGS, SECTORS, BLOCK), jnp.float32) ** level_of(keys[5], (SEGS, SECTORS, BLOCK), ((0, 8), (1, 4)), -0.2, 0.2)), 0.5, 4.0),
        "precond": jnp.clip(jnp.exp(math.log(2.0) - 2.0794415 * jax.random.uniform(keys[6], (SEGS, SECTORS, BLOCK, BLOCK), jnp.float32) ** level_of(keys[6], (SEGS, SECTORS, BLOCK, BLOCK), ((0, 8), (1, 4)), -0.2, 0.2)), 0.25, 2.0).astype(jnp.bfloat16),
        "sector_rows": draw_sector_rows(jax.random.fold_in(keys[8], 71), 0),
    }


def apply_op(vec, lenv, renv, mask):
    f32 = jnp.float32
    vb = vec.astype(jnp.bfloat16).astype(f32)
    lenv = lenv.astype(f32)
    renv = renv.astype(f32)
    inner = jnp.einsum('swij,sjk->swik', lenv[:, :WD], vb).astype(jnp.bfloat16).astype(f32)
    diag = jnp.einsum('swik,swkl->sil', inner, renv[:, :WD])
    lower = jnp.concatenate([jnp.zeros_like(vb[:1]), vb[:-1]], axis=0)
    up_inner = jnp.einsum('swij,sjk->swik', lenv[:, WD:], lower).astype(jnp.bfloat16).astype(f32)
    up = jnp.einsum('swik,swkl->sil', up_inner, renv[:, WD:])
    dn_inner = jnp.einsum('swji,sjk->swik', lenv[:, WD:], vb).astype(jnp.bfloat16).astype(f32)
    down = jnp.einsum('swik,swlk->sil', dn_inner, renv[:, WD:]).astype(jnp.bfloat16).astype(f32)
    upper = jnp.concatenate([down[1:], jnp.zeros_like(down[:1])], axis=0)
    return mask * (diag + up + upper)

def one_boundary(items):
    lenv, renv, apiece, bnext, guess, invv, precond, rows = items
    f32 = jnp.float32
    idx_r = lax.broadcasted_iota(jnp.int32, (BLOCK, BLOCK), 0)
    idx_c = lax.broadcasted_iota(jnp.int32, (BLOCK, BLOCK), 1)
    mask = ((idx_r[None] < rows[:, None, None]) & (idx_c[None] < rows[:, None, None])).astype(f32)
    scaled = (apiece.astype(f32) * invv[:, None, :]).astype(jnp.bfloat16)
    prod = jnp.einsum('sij,sjk->sik', scaled.astype(f32), bnext.astype(f32))
    start = mask * (prod + guess.astype(f32))
    x = start / jnp.sqrt(jnp.sum(start * start))
    g = apply_op(x, lenv, renv, mask)
    prec = precond.astype(f32)
    lam = jnp.float32(0.0)
    for step in range(ITERS):
        a = jnp.sum(x * g)
        p = prec * (g - a * x)
        s = jnp.sum(x * p)
        q = p - s * x
        t = q / jnp.sqrt(jnp.sum(q * q))
        h = apply_op(t, lenv, renv, mask)
        b = jnp.sum(x * h)
        c = jnp.sum(t * h)
        lam = 0.5 * (a + c) - jnp.sqrt((0.5 * (a - c)) ** 2 + b * b)
        uu = c - lam
        ww = -b
        nrm = jnp.sqrt(uu * uu + ww * ww)
        x = (uu * x + ww * t) / nrm
        g = (uu * g + ww * h) / nrm
    hi = lax.Precision.HIGHEST
    fro = lax.optimization_barrier(jnp.sum(x * x, axis=(1, 2)))
    y = x * lax.rsqrt(fro + 1e-06)[:, None, None]
    for step in range(NS_STEPS):
        gram = jnp.einsum('sij,skj->sik', y, y, precision=hi)
        y = 1.5 * y - 0.5 * jnp.einsum('sik,skj->sij', gram, y, precision=hi)
    weight = jnp.einsum('sji,sjk->sik', y, x, precision=hi).astype(jnp.bfloat16)
    return (y, weight, lam)

def reference(left_env, right_env, left_piece, right_piece, guess, inverse_values, precond, sector_rows):
    bnext = jnp.concatenate([right_piece[1:], jnp.zeros_like(right_piece[:1])], axis=0)
    polar, weight, energies = lax.map(one_boundary, (left_env, right_env, left_piece, bnext, guess, inverse_values, precond, sector_rows))
    next_left = jnp.concatenate([jnp.zeros_like(weight[:1]), weight[:-1]], axis=0)
    return (polar, next_left, energies)
```

```python
import functools

import jax
import jax.numpy as jnp
from jax import lax
from jax.experimental import pallas as pl
from jax.experimental.pallas import tpu as pltpu
from jax.sharding import PartitionSpec as P

WD = 2
NS_STEPS = 3
ROWS = 8
LANES = 128
F32 = jnp.float32
BF16 = jnp.bfloat16
VMEM = pl.BlockSpec(memory_space=pltpu.VMEM)
SMEM = pl.BlockSpec(memory_space=pltpu.SMEM)


def shift(value, axis, steps):
    count = lax.axis_size(axis)
    first, last = max(0, -steps), min(count, count - steps)
    return lax.ppermute(value, axis, [(source, source + steps) for source in range(first, last)])


def exchange(value, axis):
    count = lax.axis_size(axis)
    if count & (count - 1):
        return [lax.psum(value, axis)]
    parts, done = [value], 1
    while done < count:
        if len(parts) > 1:
            parts = [total(parts)]
        radix = 4 if count // done >= 4 else 2
        for digit in range(1, radix):
            pairs = [(source, source ^ (digit * done)) for source in range(count)]
            parts.append(lax.ppermute(parts[0], axis, pairs))
        done *= radix
    return parts


def total(parts):
    while len(parts) > 1:
        parts = [parts[i] + parts[i + 1] for i in range(0, len(parts), 2)]
    return parts[0]


def fold(product):
    row = jnp.sum(product, axis=0, keepdims=True)
    width = row.shape[-1]
    out = row[:, :LANES]
    for start in range(LANES, width, LANES):
        out = out + row[:, start : start + LANES]
    return out


def scalars(refs, count):
    sums = jnp.sum(total([ref[...] for ref in refs]), axis=1, keepdims=True)
    return [sums[i : i + 1] for i in range(count)]


def sandwich(left, right, value, inner, first, last):
    size = value.shape[-1]
    for w in range(first, last):
        product = jnp.dot(left[w], value, preferred_element_type=F32)
        inner[:, w * size : (w + 1) * size] = product.astype(BF16)
    stacked = right[first:last].reshape((last - first) * size, size)
    return jnp.dot(inner[:, first * size : last * size], stacked, preferred_element_type=F32)


def start_kernel(scaled, behind, guess, mask, y_ref, yb_ref):
    size = mask.shape[-1]
    start = jnp.dot(scaled[...], behind[...], preferred_element_type=F32) + guess[...].astype(F32)
    y = mask[...] * start * (1.0 / (1 << (size - 1).bit_length()))
    y_ref[...] = y
    yb_ref[...] = y.astype(BF16)


def lower_kernel(pairs, sends, left, right, vector_b, *refs):
    ops, outs = refs[: len(refs) - 4 - sends], refs[len(refs) - 4 - sends :]
    inner = outs[-1]
    low_ref, diag_ref, stat_ref = outs[:3]
    channels = left.shape[0]
    value = vector_b[...]
    low = sandwich(left, right, value, inner, WD, channels)
    low_ref[...] = low
    if sends:
        outs[3][...] = low.astype(BF16)
    diag = sandwich(left, right, value, inner, 0, WD)
    diag_ref[...] = diag
    stat_ref[...] = jnp.zeros(stat_ref.shape, F32)
    for row, (one, two) in enumerate(pairs):
        other = diag if two is None else ops[two][...]
        stat_ref[row : row + 1] = fold(ops[one][...] * other)


def cross_kernel(row, below, low, stat, out):
    out[...] = stat[...]
    out[row : row + 1] = stat[row : row + 1] + 2.0 * fold(below[...].astype(F32) * low[...])


def raise_kernel(left, right, below, after, up_ref, inner):
    up_ref[...] = sandwich(left, right, below[...], inner, WD, left.shape[0])


def first_kernel(parts, *refs):
    y_ref, diag, up, above, mask, prec = refs[parts : parts + 6]
    g_ref, p_ref, pb_ref = refs[parts + 6 :]
    yy, yhy = scalars(refs[:parts], 2)
    g = mask[...] * (diag[...] + up[...] + above[...].astype(F32))
    g_ref[...] = g
    p = prec[...].astype(F32) * (g - (yhy / yy) * y_ref[...])
    p_ref[...] = p
    pb_ref[...] = p.astype(BF16)


def ritz(a, b, c):
    lam = 0.5 * (a + c) - jnp.sqrt((0.5 * (a - c)) ** 2 + b * b)
    u, w = c - lam, -b
    n = jnp.sqrt(u * u + w * w)
    return lam, u / n, w / n


def second_kernel(parts, *refs):
    y_ref, g_ref, p_ref, diag, up, above, mask, prec = refs[parts : parts + 8]
    x_out, g_out, p_out, pb_out, lam_out = refs[parts + 8 :]
    yy, yg, yp, pp, pg, php = scalars(refs[:parts], 6)
    a = yg / yy
    s = yp / yy
    qq = pp - 2.0 * s * yp + s * s * yy
    b = (pg - s * yg) / jnp.sqrt(qq * yy)
    c = (php - 2.0 * s * pg + s * s * yg) / qq
    lam, u, w = ritz(a, b, c)
    along_p = w / jnp.sqrt(qq)
    along_y = u / jnp.sqrt(yy) - along_p * s
    hp = mask[...] * (diag[...] + up[...] + above[...].astype(F32))
    x = along_y * y_ref[...] + along_p * p_ref[...]
    g = along_y * g_ref[...] + along_p * hp
    p = prec[...].astype(F32) * (g - lam * x)
    x_out[...] = x
    g_out[...] = g
    p_out[...] = p
    pb_out[...] = p.astype(BF16)
    lam_out[...] = jnp.broadcast_to(lam, lam_out.shape)


def split(value):
    high = value.astype(BF16)
    return high, (value - high.astype(F32)).astype(BF16)


def product(one, two, over):
    dims = ((over[:1], over[1:]), ((), ()))
    dot = functools.partial(lax.dot_general, dimension_numbers=dims, preferred_element_type=F32)
    (one_high, one_low), (two_high, two_low) = one, two
    return dot(one_high, two_high) + (dot(one_high, two_low) + dot(one_low, two_high))


def last_kernel(parts, *refs):
    x_ref, p_ref, lam_ref = refs[parts : parts + 3]
    polar_out, weight_out, lam_out = refs[parts + 3 :]
    xp, pp, pg, php = scalars(refs[:parts], 4)
    a = lam_ref[0:1, 0:1]
    qq = pp - xp * xp
    b = (pg - xp * a) / jnp.sqrt(qq)
    c = (php - 2.0 * xp * pg + xp * xp * a) / qq
    lam, u, w = ritz(a, b, c)
    along_p = w / jnp.sqrt(qq)
    along_x = u - along_p * xp
    lam_out[0] = lam[0, 0]
    x = along_x * x_ref[...] + along_p * p_ref[...]
    frob = jnp.sum(jnp.sum(x * x, axis=0, keepdims=True), axis=1, keepdims=True)
    polar = x * lax.rsqrt(frob + 1e-06)
    for _ in range(NS_STEPS):
        halves = split(polar)
        gram = product(halves, halves, (1, 1))
        polar = 1.5 * polar - 0.5 * product(split(gram), halves, (1, 0))
    polar_out[0, 0] = polar
    weight_out[0, 0] = product(split(polar), split(x), (0, 0)).astype(BF16)


def shards(
    left_env, right_env, left_piece, right_piece, guess, inverse_values, precond, sector_rows
):
    left, right = left_env[0, 0], right_env[0, 0]
    channels, size = left.shape[0], left.shape[-1]
    count = sector_rows[0, 0]
    matrix = jax.ShapeDtypeStruct((size, size), F32)
    narrow = jax.ShapeDtypeStruct((size, size), BF16)
    stats = jax.ShapeDtypeStruct((ROWS, LANES), F32)
    inner = pltpu.VMEM((size, channels * size), BF16)

    def call(kernel, name, outs, *operands, scratch=(), out_specs=None):
        return pl.pallas_call(
            kernel,
            name=name,
            out_shape=outs,
            in_specs=[VMEM] * len(operands),
            out_specs=out_specs or [VMEM] * len(outs),
            scratch_shapes=list(scratch),
            compiler_params=pltpu.CompilerParams(vmem_limit_bytes=16 << 20),
        )(*operands)

    behind = shift(right_piece[0, 0], "seg", -1)
    idx_r = lax.broadcasted_iota(jnp.int32, (size, size), 0)
    idx_c = lax.broadcasted_iota(jnp.int32, (size, size), 1)
    mask = ((idx_r < count) & (idx_c < count)).astype(F32)
    scaled = (left_piece[0, 0].astype(F32) * inverse_values[0, 0][None, :]).astype(BF16)
    prec = precond[0, 0]

    y, yb = call(start_kernel, "start", [matrix, narrow], scaled, behind, guess[0, 0], mask)

    def half(name, vector_b, pairs, operands, row, sends):
        below = shift(vector_b, "sec", 1)
        outs = [matrix, matrix, stats] + [narrow] * sends
        kernel = functools.partial(lower_kernel, pairs, sends)
        low, diag, stat, *sent = call(
            kernel, name + "_lower", outs, left, right, vector_b, *operands, scratch=[inner]
        )
        above = shift(sent[0], "sec", -1) if sends else None
        (stat,) = call(functools.partial(cross_kernel, row), name + "_cross", [stats], below, low, stat)
        return below, diag, above, stat

    def raised(name, below, stat):
        return call(raise_kernel, name, [matrix], left, right, below, stat, scratch=[inner])[0]

    below, diag, above, stat = half("one", yb, [(0, 0), (0, None)], [y], 1, 1)
    parts = exchange(stat, "sec")
    up = raised("one_raise", below, stat)
    kernel = functools.partial(first_kernel, len(parts))
    g, p, pb = call(
        kernel, "first", [matrix, matrix, narrow], *parts, y, diag, up, above, mask, prec
    )

    pairs = [(0, 0), (0, 1), (0, 2), (2, 2), (2, 1), (2, None)]
    below, diag, above, stat = half("two", pb, pairs, [y, g, p], 5, 1)
    parts = exchange(stat, "sec")
    up = raised("two_raise", below, stat)
    kernel = functools.partial(second_kernel, len(parts))
    x, g, p, pb, lam = call(
        kernel,
        "second",
        [matrix, matrix, matrix, narrow, stats],
        *parts, y, g, p, diag, up, above, mask, prec,
    )

    pairs = [(0, 2), (2, 2), (2, 1), (2, None)]
    below, diag, above, stat = half("three", pb, pairs, [x, g, p], 3, 0)
    parts = exchange(stat, "sec")
    kernel = functools.partial(last_kernel, len(parts))
    block = (1, 1, size, size)
    polar, weight, energy = call(
        kernel,
        "last",
        [
            jax.ShapeDtypeStruct(block, F32),
            jax.ShapeDtypeStruct(block, BF16),
            jax.ShapeDtypeStruct((1,), F32),
        ],
        *parts, x, p, lam,
        out_specs=[VMEM, VMEM, SMEM],
    )
    return polar, shift(weight, "seg", 1), energy


def solution(mesh):
    placed = (
        P("seg", "sec", None, None, None),
        P("seg", "sec", None, None, None),
        P("seg", "sec", None, None),
        P("seg", "sec", None, None),
        P("seg", "sec", None, None),
        P("seg", "sec", None),
        P("seg", "sec", None, None),
        P("seg", "sec"),
    )
    return jax.shard_map(
        shards,
        mesh=mesh,
        in_specs=placed,
        out_specs=(P("seg", "sec", None, None), P("seg", "sec", None, None), P("seg")),
        check_vma=False,
    )
```

```python
import functools

import jax
import jax.numpy as jnp
from jax import lax
from jax.experimental import pallas as pl
from jax.experimental.pallas import tpu as pltpu
from jax.sharding import PartitionSpec as P

WD = 2
NS_STEPS = 3
ROWS = 8
LANES = 128
F32 = jnp.float32
BF16 = jnp.bfloat16
VMEM = pl.BlockSpec(memory_space=pltpu.VMEM)
SMEM = pl.BlockSpec(memory_space=pltpu.SMEM)
COVER = pl.CostEstimate(flops=10**10, bytes_accessed=1 << 24, transcendentals=0)


def shift(value, axis, steps):
    count = lax.axis_size(axis)
    first, last = max(0, -steps), min(count, count - steps)
    return lax.ppermute(value, axis, [(source, source + steps) for source in range(first, last)])


def rotate(value, axis, steps):
    count = lax.axis_size(axis)
    return lax.ppermute(value, axis, [(source, (source + steps) % count) for source in range(count)])


def from_below(value):
    return jnp.where(lax.axis_index("sec") > 0, value, jnp.zeros_like(value))


def from_above(value):
    last = lax.axis_size("sec") - 1
    return jnp.where(lax.axis_index("sec") < last, value, jnp.zeros_like(value))


def exchange(value, axis):
    count = lax.axis_size(axis)
    if count & (count - 1):
        return [lax.psum(value, axis)]
    parts, done = [value], 1
    while done < count:
        if len(parts) > 1:
            parts = [total(parts)]
        radix = 4 if count // done >= 4 else 2
        for digit in range(1, radix):
            pairs = [(source, source ^ (digit * done)) for source in range(count)]
            parts.append(lax.ppermute(parts[0], axis, pairs))
        done *= radix
    return parts


def total(parts):
    while len(parts) > 1:
        parts = [parts[i] + parts[i + 1] for i in range(0, len(parts), 2)]
    return parts[0]


def fold(product):
    row = jnp.sum(product, axis=0, keepdims=True)
    width = row.shape[-1]
    out = row[:, :LANES]
    for start in range(LANES, width, LANES):
        out = out + row[:, start : start + LANES]
    return out


def scalars(refs, count):
    sums = jnp.sum(total([ref[...] for ref in refs]), axis=1, keepdims=True)
    return [sums[i : i + 1] for i in range(count)]


def sandwich(left, right, value, inner, first, last):
    size = value.shape[-1]
    for w in range(first, last):
        product = jnp.dot(left[w], value, preferred_element_type=F32)
        inner[:, w * size : (w + 1) * size] = product.astype(BF16)
    stacked = right[first:last].reshape((last - first) * size, size)
    return jnp.dot(inner[:, first * size : last * size], stacked, preferred_element_type=F32)


def mask_kernel(rows, mask_out):
    count = rows[0]
    shape = mask_out.shape
    idx_r = lax.broadcasted_iota(jnp.int32, shape, 0)
    idx_c = lax.broadcasted_iota(jnp.int32, shape, 1)
    mask_out[...] = jnp.where((idx_r < count) & (idx_c < count), 1.0, 0.0)


def start_kernel(scaled, behind, guess, mask, y_ref, yb_ref):
    size = mask.shape[-1]
    start = jnp.dot(scaled[...], behind[...], preferred_element_type=F32) + guess[...].astype(F32)
    y = mask[...] * start * (1.0 / (1 << (size - 1).bit_length()))
    y_ref[...] = y
    yb_ref[...] = y.astype(BF16)


def lower_kernel(pairs, sends, left, right, vector_b, *refs):
    ops, outs = refs[: len(refs) - 4 - sends], refs[len(refs) - 4 - sends :]
    inner = outs[-1]
    low_ref, diag_ref, stat_ref = outs[:3]
    channels = left.shape[0]
    value = vector_b[...]
    low = sandwich(left, right, value, inner, WD, channels)
    low_ref[...] = low
    if sends:
        outs[3][...] = low.astype(BF16)
    diag = sandwich(left, right, value, inner, 0, WD)
    diag_ref[...] = diag
    stat_ref[...] = jnp.zeros(stat_ref.shape, F32)
    for row, (one, two) in enumerate(pairs):
        other = diag if two is None else ops[two][...]
        stat_ref[row : row + 1] = fold(ops[one][...] * other)


def cross_kernel(row, below, low, stat, out):
    out[...] = stat[...]
    crossed = fold(from_below(below[...]).astype(F32) * low[...])
    out[row : row + 1] = stat[row : row + 1] + 2.0 * crossed


def raise_kernel(left, right, below, after, up_ref, inner):
    up_ref[...] = from_below(sandwich(left, right, below[...], inner, WD, left.shape[0]))


def first_kernel(parts, *refs):
    y_ref, diag, up, above, mask, prec = refs[parts : parts + 6]
    g_ref, p_ref, pb_ref = refs[parts + 6 :]
    yy, yhy = scalars(refs[:parts], 2)
    g = mask[...] * (diag[...] + up[...] + from_above(above[...].astype(F32)))
    g_ref[...] = g
    p = prec[...].astype(F32) * (g - (yhy / yy) * y_ref[...])
    p_ref[...] = p
    pb_ref[...] = p.astype(BF16)


def ritz(a, b, c):
    lam = 0.5 * (a + c) - jnp.sqrt((0.5 * (a - c)) ** 2 + b * b)
    u, w = c - lam, -b
    n = jnp.sqrt(u * u + w * w)
    return lam, u / n, w / n


def second_kernel(parts, *refs):
    y_ref, g_ref, p_ref, diag, up, above, mask, prec = refs[parts : parts + 8]
    x_out, g_out, p_out, pb_out, lam_out = refs[parts + 8 :]
    yy, yg, yp, pp, pg, php = scalars(refs[:parts], 6)
    a = yg / yy
    s = yp / yy
    qq = pp - 2.0 * s * yp + s * s * yy
    b = (pg - s * yg) / jnp.sqrt(qq * yy)
    c = (php - 2.0 * s * pg + s * s * yg) / qq
    lam, u, w = ritz(a, b, c)
    along_p = w / jnp.sqrt(qq)
    along_y = u / jnp.sqrt(yy) - along_p * s
    hp = mask[...] * (diag[...] + up[...] + from_above(above[...].astype(F32)))
    x = along_y * y_ref[...] + along_p * p_ref[...]
    g = along_y * g_ref[...] + along_p * hp
    p = prec[...].astype(F32) * (g - lam * x)
    x_out[...] = x
    g_out[...] = g
    p_out[...] = p
    pb_out[...] = p.astype(BF16)
    lam_out[...] = jnp.broadcast_to(lam, lam_out.shape)


def dot(one, two, over):
    dims = ((over[:1], over[1:]), ((), ()))
    return lax.dot_general(one, two, dims, preferred_element_type=F32)


def split(value):
    high = value.astype(BF16)
    return high, (value - high.astype(F32)).astype(BF16)


def product(one, two, over):
    (one_high, one_low), (two_high, two_low) = split(one), split(two)
    return dot(one_high, two_high, over) + (
        dot(one_high, two_low, over) + dot(one_low, two_high, over)
    )


def last_kernel(parts, *refs):
    x_ref, p_ref, lam_ref = refs[parts : parts + 3]
    polar_out, weight_out, lam_out = refs[parts + 3 :]
    xp, pp, pg, php = scalars(refs[:parts], 4)
    a = lam_ref[0:1, 0:1]
    qq = pp - xp * xp
    b = (pg - xp * a) / jnp.sqrt(qq)
    c = (php - 2.0 * xp * pg + xp * xp * a) / qq
    lam, u, w = ritz(a, b, c)
    along_p = w / jnp.sqrt(qq)
    along_x = u - along_p * xp
    lam_out[0] = lam[0, 0]
    x = along_x * x_ref[...] + along_p * p_ref[...]
    frob = jnp.sum(jnp.sum(x * x, axis=0, keepdims=True), axis=1, keepdims=True)
    polar = x * lax.rsqrt(frob + 1e-06)
    for _ in range(NS_STEPS):
        narrow = polar.astype(BF16)
        gram = dot(narrow, narrow, (1, 1)).astype(BF16)
        polar = 1.5 * polar - 0.5 * dot(gram, narrow, (1, 0))
    polar_out[0, 0] = polar
    weight_out[0, 0] = product(polar, x, (0, 0)).astype(BF16)


def shards(
    left_env, right_env, left_piece, right_piece, guess, inverse_values, precond, sector_rows
):
    left, right, prec = left_env[0, 0], right_env[0, 0], precond[0, 0]
    channels, size = left.shape[0], left.shape[-1]
    matrix = jax.ShapeDtypeStruct((size, size), F32)
    narrow = jax.ShapeDtypeStruct((size, size), BF16)
    stats = jax.ShapeDtypeStruct((ROWS, LANES), F32)
    inner = pltpu.VMEM((size, channels * size), BF16)

    def call(kernel, name, outs, *operands, scratch=(), in_specs=None, out_specs=None, cost=None, limit=16 << 20):
        return pl.pallas_call(
            kernel,
            name=name,
            out_shape=outs,
            in_specs=in_specs or [VMEM] * len(operands),
            out_specs=out_specs or [VMEM] * len(outs),
            scratch_shapes=list(scratch),
            cost_estimate=cost,
            compiler_params=pltpu.CompilerParams(vmem_limit_bytes=limit),
        )(*operands)

    behind = shift(right_piece[0, 0], "seg", -1)
    (mask,) = call(
        mask_kernel, "mask", [matrix], sector_rows[0], in_specs=[SMEM], cost=COVER
    )
    scaled = (left_piece[0, 0].astype(F32) * inverse_values[0]).astype(BF16)

    y, yb = call(start_kernel, "start", [matrix, narrow], scaled, behind, guess[0, 0], mask)

    def half(name, vector_b, pairs, operands, row, sends):
        below = rotate(vector_b, "sec", 1)
        outs = [matrix, matrix, stats] + [narrow] * sends
        kernel = functools.partial(lower_kernel, pairs, sends)
        low, diag, stat, *sent = call(
            kernel, name + "_lower", outs, left, right, vector_b, *operands, scratch=[inner]
        )
        above = rotate(sent[0], "sec", -1) if sends else None
        (stat,) = call(functools.partial(cross_kernel, row), name + "_cross", [stats], below, low, stat)
        return below, diag, above, stat

    def raised(name, below, stat):
        return call(raise_kernel, name, [matrix], left, right, below, stat, scratch=[inner])[0]

    below, diag, above, stat = half("one", yb, [(0, 0), (0, None)], [y], 1, 1)
    parts = exchange(stat, "sec")
    up = raised("one_raise", below, stat)
    kernel = functools.partial(first_kernel, len(parts))
    g, p, pb = call(
        kernel, "first", [matrix, matrix, narrow], *parts, y, diag, up, above, mask, prec
    )

    pairs = [(0, 0), (0, 1), (0, 2), (2, 2), (2, 1), (2, None)]
    below, diag, above, stat = half("two", pb, pairs, [y, g, p], 5, 1)
    parts = exchange(stat, "sec")
    up = raised("two_raise", below, stat)
    kernel = functools.partial(second_kernel, len(parts))
    x, g, p, pb, lam = call(
        kernel,
        "second",
        [matrix, matrix, matrix, narrow, stats],
        *parts, y, g, p, diag, up, above, mask, prec,
    )

    pairs = [(0, 2), (2, 2), (2, 1), (2, None)]
    below, diag, above, stat = half("three", pb, pairs, [x, g, p], 3, 0)
    parts = exchange(stat, "sec")
    kernel = functools.partial(last_kernel, len(parts))
    block = (1, 1, size, size)
    polar, weight, energy = call(
        kernel,
        "last",
        [
            jax.ShapeDtypeStruct(block, F32),
            jax.ShapeDtypeStruct(block, BF16),
            jax.ShapeDtypeStruct((1,), F32),
        ],
        *parts, x, p, lam,
        out_specs=[VMEM, VMEM, SMEM],
    )
    return polar, shift(weight, "seg", 1), energy


def solution(mesh):
    placed = (
        P("seg", "sec", None, None, None),
        P("seg", "sec", None, None, None),
        P("seg", "sec", None, None),
        P("seg", "sec", None, None),
        P("seg", "sec", None, None),
        P("seg", "sec", None),
        P("seg", "sec", None, None),
        P("seg", "sec"),
    )
    return jax.shard_map(
        shards,
        mesh=mesh,
        in_specs=placed,
        out_specs=(P("seg", "sec", None, None), P("seg", "sec", None, None), P("seg")),
        check_vma=False,
    )
```

```python
import functools

import jax
import jax.numpy as jnp
from jax import lax
from jax.experimental import pallas as pl
from jax.experimental.pallas import tpu as pltpu
from jax.sharding import PartitionSpec as P

WD = 2
NS_STEPS = 3
ROWS = 8
LANES = 128
F32 = jnp.float32
BF16 = jnp.bfloat16
VMEM = pl.BlockSpec(memory_space=pltpu.VMEM)
SMEM = pl.BlockSpec(memory_space=pltpu.SMEM)
COVER = pl.CostEstimate(flops=10**10, bytes_accessed=1 << 24, transcendentals=0)


def shift(value, axis, steps):
    count = lax.axis_size(axis)
    first, last = max(0, -steps), min(count, count - steps)
    return lax.ppermute(value, axis, [(source, source + steps) for source in range(first, last)])


def rotate(value, axis, steps):
    count = lax.axis_size(axis)
    return lax.ppermute(value, axis, [(source, (source + steps) % count) for source in range(count)])


def from_below(value):
    return jnp.where(lax.axis_index("sec") > 0, value, jnp.zeros_like(value))


def from_above(value):
    last = lax.axis_size("sec") - 1
    return jnp.where(lax.axis_index("sec") < last, value, jnp.zeros_like(value))


def exchange(value, axis):
    count = lax.axis_size(axis)
    if count & (count - 1):
        return [lax.psum(value, axis)]
    parts, done = [value], 1
    while done < count:
        if len(parts) > 1:
            parts = [total(parts)]
        radix = 4 if count // done >= 4 else 2
        for digit in range(1, radix):
            pairs = [(source, source ^ (digit * done)) for source in range(count)]
            parts.append(lax.ppermute(parts[0], axis, pairs))
        done *= radix
    return parts


def total(parts):
    while len(parts) > 1:
        parts = [parts[i] + parts[i + 1] for i in range(0, len(parts), 2)]
    return parts[0]


def fold(product):
    row = jnp.sum(product, axis=0, keepdims=True)
    width = row.shape[-1]
    out = row[:, :LANES]
    for start in range(LANES, width, LANES):
        out = out + row[:, start : start + LANES]
    return out


def scalars(refs, count):
    sums = jnp.sum(total([ref[...] for ref in refs]), axis=1, keepdims=True)
    return [sums[i : i + 1] for i in range(count)]


def sandwich(left, right, value, inner, first, last):
    size = value.shape[-1]
    for w in range(first, last):
        product = jnp.dot(left[w], value, preferred_element_type=F32)
        inner[:, w * size : (w + 1) * size] = product.astype(BF16)
    stacked = right[first:last].reshape((last - first) * size, size)
    return jnp.dot(inner[:, first * size : last * size], stacked, preferred_element_type=F32)


def mask_kernel(rows, mask_out):
    count = rows[0]
    shape = mask_out.shape
    idx_r = lax.broadcasted_iota(jnp.int32, shape, 0)
    idx_c = lax.broadcasted_iota(jnp.int32, shape, 1)
    mask_out[...] = jnp.where((idx_r < count) & (idx_c < count), 1.0, 0.0)


def start_kernel(scaled, behind, guess, mask, y_ref, yb_ref):
    size = mask.shape[-1]
    start = jnp.dot(scaled[...], behind[...], preferred_element_type=F32) + guess[...].astype(F32)
    y = mask[...] * start * (1.0 / (1 << (size - 1).bit_length()))
    y_ref[...] = y
    yb_ref[...] = y.astype(BF16)


def lower_kernel(pairs, sends, left, right, vector_b, *refs):
    ops, outs = refs[: len(refs) - 4 - sends], refs[len(refs) - 4 - sends :]
    inner = outs[-1]
    low_ref, diag_ref, stat_ref = outs[:3]
    channels = left.shape[0]
    value = vector_b[...]
    low = sandwich(left, right, value, inner, WD, channels)
    low_ref[...] = low
    if sends:
        outs[3][...] = low.astype(BF16)
    diag = sandwich(left, right, value, inner, 0, WD)
    diag_ref[...] = diag
    stat_ref[...] = jnp.zeros(stat_ref.shape, F32)
    for row, (one, two) in enumerate(pairs):
        other = diag if two is None else ops[two][...]
        stat_ref[row : row + 1] = fold(ops[one][...] * other)


def add_cross(row, below, low, stat, out):
    out[...] = stat[...]
    out[row : row + 1] = stat[row : row + 1] + 2.0 * fold(from_below(below) * low[...])


def cross_kernel(below, low, stat, out):
    add_cross(1, below[...].astype(F32), low, stat, out)


def first_cross_kernel(parts, *refs):
    y, g, prec, low, stat, out, p_out = refs[parts:]
    yy, yhy = scalars(refs[:parts], 2)
    p = prec[...].astype(F32) * (g[...].astype(F32) - (yhy / yy) * y[...].astype(F32))
    p_out[...] = p.astype(BF16)
    add_cross(5, p, low, stat, out)


def second_cross_kernel(y, g, p, hp, prec, coefficients, low, stat, out):
    along_y, along_p, lam = [coefficients[i : i + 1, 0:1] for i in range(3)]
    x = along_y * y[...].astype(F32) + along_p * p[...].astype(F32)
    hx = along_y * g[...].astype(F32) + along_p * hp[...].astype(F32)
    add_cross(3, prec[...].astype(F32) * (hx - lam * x), low, stat, out)


def join_kernel(diag, up, above, mask, out, out_b):
    joined = mask[...] * (diag[...] + up[...] + from_above(above[...].astype(F32)))
    out[...] = joined
    out_b[...] = joined.astype(BF16)


def raise_kernel(left, right, below, after, up_ref, inner):
    up_ref[...] = from_below(sandwich(left, right, below[...], inner, WD, left.shape[0]))


def first_kernel(parts, *refs):
    y_ref, g_ref, prec, p_ref, pb_ref = refs[parts:]
    yy, yhy = scalars(refs[:parts], 2)
    p = prec[...].astype(F32) * (g_ref[...] - (yhy / yy) * y_ref[...])
    p_ref[...] = p
    pb_ref[...] = p.astype(BF16)


def ritz(a, b, c):
    lam = 0.5 * (a + c) - jnp.sqrt((0.5 * (a - c)) ** 2 + b * b)
    u, w = c - lam, -b
    n = jnp.sqrt(u * u + w * w)
    return lam, u / n, w / n


def second_kernel(parts, *refs):
    y_ref, g_ref, p_ref, hp_ref, prec = refs[parts : parts + 5]
    x_out, g_out, p_out, pb_out, coefficients = refs[parts + 5 :]
    yy, yg, yp, pp, pg, php = scalars(refs[:parts], 6)
    a = yg / yy
    s = yp / yy
    qq = pp - 2.0 * s * yp + s * s * yy
    b = (pg - s * yg) / jnp.sqrt(qq * yy)
    c = (php - 2.0 * s * pg + s * s * yg) / qq
    lam, u, w = ritz(a, b, c)
    along_p = w / jnp.sqrt(qq)
    along_y = u / jnp.sqrt(yy) - along_p * s
    x = along_y * y_ref[...] + along_p * p_ref[...]
    g = along_y * g_ref[...] + along_p * hp_ref[...]
    p = prec[...].astype(F32) * (g - lam * x)
    x_out[...] = x
    g_out[...] = g
    p_out[...] = p
    pb_out[...] = p.astype(BF16)
    for i, value in enumerate([along_y, along_p, lam]):
        coefficients[i : i + 1] = jnp.broadcast_to(value, (1, LANES))


def dot(one, two, over):
    dims = ((over[:1], over[1:]), ((), ()))
    return lax.dot_general(one, two, dims, preferred_element_type=F32)


def split(value):
    high = value.astype(BF16)
    return high, (value - high.astype(F32)).astype(BF16)


def product(one, two, over):
    (one_high, one_low), (two_high, two_low) = split(one), split(two)
    return dot(one_high, two_high, over) + (
        dot(one_high, two_low, over) + dot(one_low, two_high, over)
    )


def last_kernel(parts, *refs):
    x_ref, p_ref, coefficients = refs[parts : parts + 3]
    polar_out, weight_out, lam_out = refs[parts + 3 :]
    xp, pp, pg, php = scalars(refs[:parts], 4)
    a = coefficients[2:3, 0:1]
    qq = pp - xp * xp
    b = (pg - xp * a) / jnp.sqrt(qq)
    c = (php - 2.0 * xp * pg + xp * xp * a) / qq
    lam, u, w = ritz(a, b, c)
    along_p = w / jnp.sqrt(qq)
    along_x = u - along_p * xp
    lam_out[0] = lam[0, 0]
    x = along_x * x_ref[...] + along_p * p_ref[...]
    frob = jnp.sum(jnp.sum(x * x, axis=0, keepdims=True), axis=1, keepdims=True)
    polar = x * lax.rsqrt(frob + 1e-06)
    for _ in range(NS_STEPS):
        narrow = polar.astype(BF16)
        gram = dot(narrow, narrow, (1, 1)).astype(BF16)
        polar = 1.5 * polar - 0.5 * dot(gram, narrow, (1, 0))
    polar_out[0, 0] = polar
    weight_out[0, 0] = product(polar, x, (0, 0)).astype(BF16)


def shards(
    left_env, right_env, left_piece, right_piece, guess, inverse_values, precond, sector_rows
):
    left, right, prec = left_env[0, 0], right_env[0, 0], precond[0, 0]
    channels, size = left.shape[0], left.shape[-1]
    matrix = jax.ShapeDtypeStruct((size, size), F32)
    narrow = jax.ShapeDtypeStruct((size, size), BF16)
    stats = jax.ShapeDtypeStruct((ROWS, LANES), F32)
    inner = pltpu.VMEM((size, channels * size), BF16)

    def call(kernel, name, outs, *operands, scratch=(), in_specs=None, out_specs=None, cost=None, limit=16 << 20):
        return pl.pallas_call(
            kernel,
            name=name,
            out_shape=outs,
            in_specs=in_specs or [VMEM] * len(operands),
            out_specs=out_specs or [VMEM] * len(outs),
            scratch_shapes=list(scratch),
            cost_estimate=cost,
            compiler_params=pltpu.CompilerParams(vmem_limit_bytes=limit),
        )(*operands)

    behind = shift(right_piece[0, 0], "seg", -1)
    (mask,) = call(
        mask_kernel, "mask", [matrix], sector_rows[0], in_specs=[SMEM], cost=COVER
    )
    scaled = (left_piece[0, 0].astype(F32) * inverse_values[0]).astype(BF16)

    y, yb = call(start_kernel, "start", [matrix, narrow], scaled, behind, guess[0, 0], mask)

    def half(name, vector_b, pairs, operands, sends):
        outs = [matrix, matrix, stats] + [narrow] * sends
        kernel = functools.partial(lower_kernel, pairs, sends)
        low, diag, stat, *sent = call(
            kernel, name, outs, left, right, vector_b, *operands, scratch=[inner]
        )
        return low, diag, stat, rotate(sent[0], "sec", -1) if sends else None

    def joined(name, below, after, diag, above):
        (up,) = call(
            raise_kernel, name + "_raise", [matrix], left, right, below, after, scratch=[inner]
        )
        return call(join_kernel, name + "_join", [matrix, narrow], diag, up, above, mask)

    y_below = rotate(yb, "sec", 1)
    low, diag, stat, above = half("one_lower", yb, [(0, 0), (0, None)], [y], 1)
    prec_below = rotate(prec, "sec", 1)
    (stat,) = call(cross_kernel, "one_cross", [stats], y_below, low, stat)
    parts = exchange(stat, "sec")
    g, gb = joined("one", y_below, stat, diag, above)
    g_below = rotate(gb, "sec", 1)
    kernel = functools.partial(first_kernel, len(parts))
    p, pb = call(kernel, "first", [matrix, narrow], *parts, y, g, prec)

    pairs = [(0, 0), (0, 1), (0, 2), (2, 2), (2, 1), (2, None)]
    low, diag, stat, above = half("two_lower", pb, pairs, [y, g, p], 1)
    kernel = functools.partial(first_cross_kernel, len(parts))
    stat, p_below = call(
        kernel, "two_cross", [stats, narrow], *parts, y_below, g_below, prec_below, low, stat
    )
    parts = exchange(stat, "sec")
    hp, hpb = joined("two", p_below, stat, diag, above)
    hp_below = rotate(hpb, "sec", 1)
    kernel = functools.partial(second_kernel, len(parts))
    x, g, p, pb, coefficients = call(
        kernel, "second", [matrix, matrix, matrix, narrow, stats], *parts, y, g, p, hp, prec
    )

    pairs = [(0, 2), (2, 2), (2, 1), (2, None)]
    low, diag, stat, _ = half("three_lower", pb, pairs, [x, g, p], 0)
    (stat,) = call(
        second_cross_kernel,
        "three_cross",
        [stats],
        y_below, g_below, p_below, hp_below, prec_below, coefficients, low, stat,
    )
    parts = exchange(stat, "sec")
    kernel = functools.partial(last_kernel, len(parts))
    block = (1, 1, size, size)
    polar, weight, energy = call(
        kernel,
        "last",
        [
            jax.ShapeDtypeStruct(block, F32),
            jax.ShapeDtypeStruct(block, BF16),
            jax.ShapeDtypeStruct((1,), F32),
        ],
        *parts, x, p, coefficients,
        out_specs=[VMEM, VMEM, SMEM],
    )
    return polar, shift(weight, "seg", 1), energy


def solution(mesh):
    placed = (
        P("seg", "sec", None, None, None),
        P("seg", "sec", None, None, None),
        P("seg", "sec", None, None),
        P("seg", "sec", None, None),
        P("seg", "sec", None, None),
        P("seg", "sec", None),
        P("seg", "sec", None, None),
        P("seg", "sec"),
    )
    return jax.shard_map(
        shards,
        mesh=mesh,
        in_specs=placed,
        out_specs=(P("seg", "sec", None, None), P("seg", "sec", None, None), P("seg")),
        check_vma=False,
    )
```

```python
import functools

import jax
import jax.numpy as jnp
from jax import lax
from jax.experimental import pallas as pl
from jax.experimental.pallas import tpu as pltpu
from jax.sharding import PartitionSpec as P


WD = 2
NS_STEPS = 3
ROWS = 8
LANES = 128
F32 = jnp.float32
BF16 = jnp.bfloat16
VMEM = pl.BlockSpec(memory_space=pltpu.VMEM)
SMEM = pl.BlockSpec(memory_space=pltpu.SMEM)
COVER = pl.CostEstimate(flops=10**10, bytes_accessed=1 << 24, transcendentals=0)


def shift(value, axis, steps):
    count = lax.axis_size(axis)
    first, last = max(0, -steps), min(count, count - steps)
    return lax.ppermute(value, axis, [(source, source + steps) for source in range(first, last)])


def rotate(value, axis, steps):
    count = lax.axis_size(axis)
    return lax.ppermute(value, axis, [(source, (source + steps) % count) for source in range(count)])


def from_below(value):
    return jnp.where(lax.axis_index("sec") > 0, value, jnp.zeros_like(value))


def from_above(value):
    last = lax.axis_size("sec") - 1
    return jnp.where(lax.axis_index("sec") < last, value, jnp.zeros_like(value))


def exchange(value, axis):
    count = lax.axis_size(axis)
    if count & (count - 1):
        return [lax.psum(value, axis)]
    parts, done = [value], 1
    while done < count:
        if len(parts) > 1:
            parts = [total(parts)]
        radix = 4 if count // done >= 4 else 2
        for digit in range(1, radix):
            pairs = [(source, source ^ (digit * done)) for source in range(count)]
            parts.append(lax.ppermute(parts[0], axis, pairs))
        done *= radix
    return parts


def total(parts):
    while len(parts) > 1:
        parts = [parts[i] + parts[i + 1] for i in range(0, len(parts), 2)]
    return parts[0]


def fold(product):
    row = jnp.sum(product, axis=0, keepdims=True)
    width = row.shape[-1]
    out = row[:, :LANES]
    for start in range(LANES, width, LANES):
        out = out + row[:, start : start + LANES]
    return out


def scalars(refs, count):
    sums = jnp.sum(total([ref[...] for ref in refs]), axis=1, keepdims=True)
    return [sums[i : i + 1] for i in range(count)]


def sandwich(left, right, value, inner, first, last):
    size = value.shape[-1]
    for w in range(first, last):
        product = jnp.dot(left[w], value, preferred_element_type=F32)
        inner[:, w * size : (w + 1) * size] = product.astype(BF16)
    stacked = right[first:last].reshape((last - first) * size, size)
    return jnp.dot(inner[:, first * size : last * size], stacked, preferred_element_type=F32)


def mask_kernel(rows, mask_out):
    count = rows[0]
    shape = mask_out.shape
    idx_r = lax.broadcasted_iota(jnp.int32, shape, 0)
    idx_c = lax.broadcasted_iota(jnp.int32, shape, 1)
    mask_out[...] = jnp.where((idx_r < count) & (idx_c < count), 1.0, 0.0)


def start_kernel(scaled, behind, guess, mask, y_ref, yb_ref):
    size = mask.shape[-1]
    start = jnp.dot(scaled[...], behind[...], preferred_element_type=F32) + guess[...].astype(F32)
    y = mask[...] * start * (1.0 / (1 << (size - 1).bit_length()))
    y_ref[...] = y
    yb_ref[...] = y.astype(BF16)


def lower_kernel(pairs, sends, left, right, vector_b, *refs):
    ops, outs = refs[: len(refs) - 4 - sends], refs[len(refs) - 4 - sends :]
    inner = outs[-1]
    low_ref, diag_ref, stat_ref = outs[:3]
    channels = left.shape[0]
    value = vector_b[...]
    low = sandwich(left, right, value, inner, WD, channels)
    low_ref[...] = low
    if sends:
        outs[3][...] = low.astype(BF16)
    diag = sandwich(left, right, value, inner, 0, WD)
    diag_ref[...] = diag
    stat_ref[...] = jnp.zeros(stat_ref.shape, F32)
    for row, (one, two) in enumerate(pairs):
        other = diag if two is None else ops[two][...]
        stat_ref[row : row + 1] = fold(ops[one][...] * other)


def add_cross(row, below, low, stat, out):
    out[...] = stat[...]
    out[row : row + 1] = stat[row : row + 1] + 2.0 * fold(from_below(below) * low[...])


def cross_kernel(below, low, stat, out):
    add_cross(1, below[...].astype(F32), low, stat, out)


def first_cross_kernel(parts, *refs):
    y, g, prec, low, stat, out, p_out = refs[parts:]
    yy, yhy = scalars(refs[:parts], 2)
    p = prec[...].astype(F32) * (g[...].astype(F32) - (yhy / yy) * y[...].astype(F32))
    p_out[...] = p.astype(BF16)
    add_cross(5, p, low, stat, out)


def second_cross_kernel(y, g, p, hp, prec, coefficients, low, stat, out):
    along_y, along_p, lam = [coefficients[i : i + 1, 0:1] for i in range(3)]
    x = along_y * y[...].astype(F32) + along_p * p[...].astype(F32)
    hx = along_y * g[...].astype(F32) + along_p * hp[...].astype(F32)
    add_cross(3, prec[...].astype(F32) * (hx - lam * x), low, stat, out)


def join_kernel(diag, up, above, mask, out, out_b):
    joined = mask[...] * (diag[...] + up[...] + from_above(above[...].astype(F32)))
    out[...] = joined
    out_b[...] = joined.astype(BF16)


def raise_kernel(left, right, below, after, up_ref, inner):
    up_ref[...] = from_below(sandwich(left, right, below[...], inner, WD, left.shape[0]))


def first_kernel(parts, *refs):
    y_ref, g_ref, prec, p_ref, pb_ref = refs[parts:]
    yy, yhy = scalars(refs[:parts], 2)
    p = prec[...].astype(F32) * (g_ref[...] - (yhy / yy) * y_ref[...])
    p_ref[...] = p
    pb_ref[...] = p.astype(BF16)


def ritz(a, b, c):
    lam = 0.5 * (a + c) - jnp.sqrt((0.5 * (a - c)) ** 2 + b * b)
    u, w = c - lam, -b
    n = jnp.sqrt(u * u + w * w)
    return lam, u / n, w / n


def second_kernel(parts, *refs):
    y_ref, g_ref, p_ref, hp_ref, prec = refs[parts : parts + 5]
    x_out, g_out, p_out, pb_out, coefficients = refs[parts + 5 :]
    yy, yg, yp, pp, pg, php = scalars(refs[:parts], 6)
    a = yg / yy
    s = yp / yy
    qq = pp - 2.0 * s * yp + s * s * yy
    b = (pg - s * yg) / jnp.sqrt(qq * yy)
    c = (php - 2.0 * s * pg + s * s * yg) / qq
    lam, u, w = ritz(a, b, c)
    along_p = w / jnp.sqrt(qq)
    along_y = u / jnp.sqrt(yy) - along_p * s
    x = along_y * y_ref[...] + along_p * p_ref[...]
    g = along_y * g_ref[...] + along_p * hp_ref[...]
    p = prec[...].astype(F32) * (g - lam * x)
    x_out[...] = x
    g_out[...] = g
    p_out[...] = p
    pb_out[...] = p.astype(BF16)
    for i, value in enumerate([along_y, along_p, lam]):
        coefficients[i : i + 1] = jnp.broadcast_to(value, (1, LANES))


def dot(one, two, over):
    dims = ((over[:1], over[1:]), ((), ()))
    return lax.dot_general(one, two, dims, preferred_element_type=F32)


def split(value):
    high = value.astype(BF16)
    return high, (value - high.astype(F32)).astype(BF16)


def product(one, two, over):
    (one_high, one_low), (two_high, two_low) = split(one), split(two)
    return dot(one_high, two_high, over) + (
        dot(one_high, two_low, over) + dot(one_low, two_high, over)
    )


def last_kernel(parts, *refs):
    x_ref, p_ref, coefficients = refs[parts : parts + 3]
    polar_out, weight_out, lam_out = refs[parts + 3 :]
    xp, pp, pg, php = scalars(refs[:parts], 4)
    a = coefficients[2:3, 0:1]
    qq = pp - xp * xp
    b = (pg - xp * a) / jnp.sqrt(qq)
    c = (php - 2.0 * xp * pg + xp * xp * a) / qq
    lam, u, w = ritz(a, b, c)
    along_p = w / jnp.sqrt(qq)
    along_x = u - along_p * xp
    lam_out[0] = lam[0, 0]
    x = along_x * x_ref[...] + along_p * p_ref[...]
    frob = jnp.sum(jnp.sum(x * x, axis=0, keepdims=True), axis=1, keepdims=True)
    polar = x * lax.rsqrt(frob + 1e-06)
    for _ in range(NS_STEPS):
        narrow = polar.astype(BF16)
        gram = dot(narrow, narrow, (1, 1)).astype(BF16)
        polar = 1.5 * polar - 0.5 * dot(gram, narrow, (1, 0))
    polar_out[0, 0] = polar
    weight_out[0, 0] = product(polar, x, (0, 0)).astype(BF16)


def inner_shards(
    left_env, right_env, left_piece, right_piece, guess, inverse_values, precond, sector_rows
):
    left, right, prec = left_env[0, 0], right_env[0, 0], precond[0, 0]
    channels, size = left.shape[0], left.shape[-1]
    matrix = jax.ShapeDtypeStruct((size, size), F32)
    narrow = jax.ShapeDtypeStruct((size, size), BF16)
    stats = jax.ShapeDtypeStruct((ROWS, LANES), F32)
    inner = pltpu.VMEM((size, channels * size), BF16)

    def call(kernel, outs, *operands, scratch=(), in_specs=None, out_specs=None, cost=None, limit=16 << 20):
        return pl.pallas_call(
            kernel,
            out_shape=outs,
            in_specs=in_specs or [VMEM] * len(operands),
            out_specs=out_specs or [VMEM] * len(outs),
            scratch_shapes=list(scratch),
            cost_estimate=cost,
            compiler_params=pltpu.CompilerParams(vmem_limit_bytes=limit),
        )(*operands)

    behind = shift(right_piece[0, 0], "seg", -1)
    prec_below = rotate(prec, "sec", 1)
    (mask,) = call(mask_kernel, [matrix], sector_rows[0], in_specs=[SMEM], cost=COVER)
    scaled = (left_piece[0, 0].astype(F32) * inverse_values[0]).astype(BF16)

    y, yb = call(start_kernel, [matrix, narrow], scaled, behind, guess[0, 0], mask)

    def half(vector_b, pairs, operands, sends):
        outs = [matrix, matrix, stats] + [narrow] * sends
        kernel = functools.partial(lower_kernel, pairs, sends)
        low, diag, stat, *sent = call(
            kernel, outs, left, right, vector_b, *operands, scratch=[inner]
        )
        return low, diag, stat, rotate(sent[0], "sec", -1) if sends else None

    def joined(below, after, diag, above):
        (up,) = call(raise_kernel, [matrix], left, right, below, after, scratch=[inner])
        return call(join_kernel, [matrix, narrow], diag, up, above, mask)

    y_below = rotate(yb, "sec", 1)
    low, diag, stat, above = half(yb, [(0, 0), (0, None)], [y], 1)
    (stat,) = call(cross_kernel, [stats], y_below, low, stat)
    parts = exchange(stat, "sec")
    g, gb = joined(y_below, stat, diag, above)
    g_below = rotate(gb, "sec", 1)
    kernel = functools.partial(first_kernel, len(parts))
    p, pb = call(kernel, [matrix, narrow], *parts, y, g, prec)

    pairs = [(0, 0), (0, 1), (0, 2), (2, 2), (2, 1), (2, None)]
    low, diag, stat, above = half(pb, pairs, [y, g, p], 1)
    kernel = functools.partial(first_cross_kernel, len(parts))
    stat, p_below = call(kernel, [stats, narrow], *parts, y_below, g_below, prec_below, low, stat)
    parts = exchange(stat, "sec")
    hp, hpb = joined(p_below, stat, diag, above)
    hp_below = rotate(hpb, "sec", 1)
    kernel = functools.partial(second_kernel, len(parts))
    x, g, p, pb, coefficients = call(
        kernel, [matrix, matrix, matrix, narrow, stats], *parts, y, g, p, hp, prec
    )

    pairs = [(0, 2), (2, 2), (2, 1), (2, None)]
    low, diag, stat, _ = half(pb, pairs, [x, g, p], 0)
    (stat,) = call(
        second_cross_kernel,
        [stats],
        y_below, g_below, p_below, hp_below, prec_below, coefficients, low, stat,
    )
    parts = exchange(stat, "sec")
    kernel = functools.partial(last_kernel, len(parts))
    block = (1, 1, size, size)
    polar, weight, energy = call(
        kernel,
        [
            jax.ShapeDtypeStruct(block, F32),
            jax.ShapeDtypeStruct(block, BF16),
            jax.ShapeDtypeStruct((1,), F32),
        ],
        *parts, x, p, coefficients,
        out_specs=[VMEM, VMEM, SMEM],
    )
    return polar, shift(weight, "seg", 1), energy


def solution(mesh):
    placed = (
        P("seg", "sec", None, None, None),
        P("seg", "sec", None, None, None),
        P("seg", "sec", None, None),
        P("seg", "sec", None, None),
        P("seg", "sec", None, None),
        P("seg", "sec", None),
        P("seg", "sec", None, None),
        P("seg", "sec"),
    )
    return jax.shard_map(
        inner_shards,
        mesh=mesh,
        in_specs=placed,
        out_specs=(P("seg", "sec", None, None), P("seg", "sec", None, None), P("seg")),
        check_vma=False,
    )
```

```python
import functools

import jax
import jax.numpy as jnp
from jax import lax
from jax.experimental import pallas as pl
from jax.experimental.pallas import tpu as pltpu
from jax.sharding import PartitionSpec as P


WD = 2
NS_STEPS = 3
ROWS = 8
LANES = 128
F32 = jnp.float32
BF16 = jnp.bfloat16
VMEM = pl.BlockSpec(memory_space=pltpu.VMEM)
SMEM = pl.BlockSpec(memory_space=pltpu.SMEM)
SHORT = pl.CostEstimate(flops=0, bytes_accessed=1 << 20, transcendentals=0)
COVER = pl.CostEstimate(flops=10**10, bytes_accessed=1 << 24, transcendentals=0)


def swaps(value, axis):
    count = lax.axis_size(axis)

    def partners(first):
        pairs = {i: i for i in range(count)}
        for i in range(first, count - 1, 2):
            pairs[i], pairs[i + 1] = i + 1, i
        return list(pairs.items())

    far = lax.ppermute(value, axis, partners(1))
    near = lax.ppermute(value, axis, partners(0))
    return near, far


def pick(near, far, axis, step):
    place = lax.axis_index(axis)
    inside = (place + step >= 0) & (place + step < lax.axis_size(axis))
    paired = lax.rem(place, 2) == (0 if step > 0 else 1)
    return jnp.where(inside, jnp.where(paired, near, far), jnp.zeros_like(near))


def rotate(value, axis, steps):
    count = lax.axis_size(axis)
    return lax.ppermute(value, axis, [(source, (source + steps) % count) for source in range(count)])


def from_below(value):
    return jnp.where(lax.axis_index("sec") > 0, value, jnp.zeros_like(value))


def from_above(value):
    last = lax.axis_size("sec") - 1
    return jnp.where(lax.axis_index("sec") < last, value, jnp.zeros_like(value))


def exchange(value, axis):
    count = lax.axis_size(axis)
    if count & (count - 1):
        return [lax.psum(value, axis)]
    parts, done = [value], 1
    while done < count:
        if len(parts) > 1:
            parts = [total(parts)]
        radix = 4 if count // done >= 4 else 2
        for digit in range(1, radix):
            pairs = [(source, source ^ (digit * done)) for source in range(count)]
            parts.append(lax.ppermute(parts[0], axis, pairs))
        done *= radix
    return parts


def total(parts):
    while len(parts) > 1:
        parts = [parts[i] + parts[i + 1] for i in range(0, len(parts), 2)]
    return parts[0]


def fold(product):
    row = jnp.sum(product, axis=0, keepdims=True)
    width = row.shape[-1]
    out = row[:, :LANES]
    for start in range(LANES, width, LANES):
        out = out + row[:, start : start + LANES]
    return out


def scalars(refs, count):
    sums = jnp.sum(total([ref[...] for ref in refs]), axis=1, keepdims=True)
    return [sums[i : i + 1] for i in range(count)]


def sandwich(left, right, value, inner, first, last):
    size = value.shape[-1]
    for w in range(first, last):
        product = jnp.dot(left[w], value, preferred_element_type=F32)
        inner[:, w * size : (w + 1) * size] = product.astype(BF16)
    stacked = right[first:last].reshape((last - first) * size, size)
    return jnp.dot(inner[:, first * size : last * size], stacked, preferred_element_type=F32)


def mask_kernel(rows, mask_out):
    count = rows[0]
    shape = mask_out.shape
    idx_r = lax.broadcasted_iota(jnp.int32, shape, 0)
    idx_c = lax.broadcasted_iota(jnp.int32, shape, 1)
    mask_out[...] = jnp.where((idx_r < count) & (idx_c < count), 1.0, 0.0)


def start_kernel(scaled, near, far, guess, mask, y_ref, yb_ref):
    size = mask.shape[-1]
    behind = pick(near[...], far[...], "seg", 1)
    start = jnp.dot(scaled[...], behind, preferred_element_type=F32) + guess[...].astype(F32)
    y = mask[...] * start * (1.0 / (1 << (size - 1).bit_length()))
    y_ref[...] = y
    yb_ref[...] = y.astype(BF16)


def lower_kernel(pairs, sends, left, right, vector_b, *refs):
    ops, outs = refs[: len(refs) - 4 - sends], refs[len(refs) - 4 - sends :]
    inner = outs[-1]
    low_ref, diag_ref, stat_ref = outs[:3]
    channels = left.shape[0]
    value = vector_b[...]
    low = sandwich(left, right, value, inner, WD, channels)
    low_ref[...] = low
    if sends:
        outs[3][...] = low.astype(BF16)
    diag = sandwich(left, right, value, inner, 0, WD)
    diag_ref[...] = diag
    stat_ref[...] = jnp.zeros(stat_ref.shape, F32)
    for row, (one, two) in enumerate(pairs):
        other = diag if two is None else ops[two][...]
        stat_ref[row : row + 1] = fold(ops[one][...] * other)


def add_cross(row, below, low, stat, out):
    out[...] = stat[...]
    out[row : row + 1] = stat[row : row + 1] + 2.0 * fold(from_below(below) * low[...])


def cross_kernel(below, low, stat, out):
    add_cross(1, below[...].astype(F32), low, stat, out)


def first_cross_kernel(parts, *refs):
    y, g, prec, low, stat, out, p_out = refs[parts:]
    yy, yhy = scalars(refs[:parts], 2)
    p = prec[...].astype(F32) * (g[...].astype(F32) - (yhy / yy) * y[...].astype(F32))
    p_out[...] = p.astype(BF16)
    add_cross(5, p, low, stat, out)


def second_cross_kernel(y, g, p, hp, prec, coefficients, low, stat, out):
    along_y, along_p, lam = [coefficients[i : i + 1, 0:1] for i in range(3)]
    x = along_y * y[...].astype(F32) + along_p * p[...].astype(F32)
    hx = along_y * g[...].astype(F32) + along_p * hp[...].astype(F32)
    add_cross(3, prec[...].astype(F32) * (hx - lam * x), low, stat, out)


def join_kernel(diag, up, above, mask, out, out_b):
    joined = mask[...] * (diag[...] + up[...] + from_above(above[...].astype(F32)))
    out[...] = joined
    out_b[...] = joined.astype(BF16)


def raise_kernel(left, right, below, after, up_ref, inner):
    up_ref[...] = from_below(sandwich(left, right, below[...], inner, WD, left.shape[0]))


def first_kernel(parts, *refs):
    y_ref, g_ref, prec, p_ref, pb_ref = refs[parts:]
    yy, yhy = scalars(refs[:parts], 2)
    p = prec[...].astype(F32) * (g_ref[...] - (yhy / yy) * y_ref[...])
    p_ref[...] = p
    pb_ref[...] = p.astype(BF16)


def ritz(a, b, c):
    lam = 0.5 * (a + c) - jnp.sqrt((0.5 * (a - c)) ** 2 + b * b)
    u, w = c - lam, -b
    n = jnp.sqrt(u * u + w * w)
    return lam, u / n, w / n


def second_kernel(parts, *refs):
    y_ref, g_ref, p_ref, hp_ref, prec = refs[parts : parts + 5]
    x_out, g_out, p_out, pb_out, coefficients = refs[parts + 5 :]
    yy, yg, yp, pp, pg, php = scalars(refs[:parts], 6)
    a = yg / yy
    s = yp / yy
    qq = pp - 2.0 * s * yp + s * s * yy
    b = (pg - s * yg) / jnp.sqrt(qq * yy)
    c = (php - 2.0 * s * pg + s * s * yg) / qq
    lam, u, w = ritz(a, b, c)
    along_p = w / jnp.sqrt(qq)
    along_y = u / jnp.sqrt(yy) - along_p * s
    x = along_y * y_ref[...] + along_p * p_ref[...]
    g = along_y * g_ref[...] + along_p * hp_ref[...]
    p = prec[...].astype(F32) * (g - lam * x)
    x_out[...] = x
    g_out[...] = g
    p_out[...] = p
    pb_out[...] = p.astype(BF16)
    for i, value in enumerate([along_y, along_p, lam]):
        coefficients[i : i + 1] = jnp.broadcast_to(value, (1, LANES))


def dot(one, two, over):
    dims = ((over[:1], over[1:]), ((), ()))
    return lax.dot_general(one, two, dims, preferred_element_type=F32)


def split(value):
    high = value.astype(BF16)
    return high, (value - high.astype(F32)).astype(BF16)


def product(one, two, over):
    (one_high, one_low), (two_high, two_low) = split(one), split(two)
    return dot(one_high, two_high, over) + (
        dot(one_high, two_low, over) + dot(one_low, two_high, over)
    )


def last_kernel(parts, *refs):
    x_ref, p_ref, coefficients = refs[parts : parts + 3]
    polar_out, weight_out, lam_out = refs[parts + 3 :]
    xp, pp, pg, php = scalars(refs[:parts], 4)
    a = coefficients[2:3, 0:1]
    qq = pp - xp * xp
    b = (pg - xp * a) / jnp.sqrt(qq)
    c = (php - 2.0 * xp * pg + xp * xp * a) / qq
    lam, u, w = ritz(a, b, c)
    along_p = w / jnp.sqrt(qq)
    along_x = u - along_p * xp
    lam_out[0] = lam[0, 0]
    x = along_x * x_ref[...] + along_p * p_ref[...]
    frob = jnp.sum(jnp.sum(x * x, axis=0, keepdims=True), axis=1, keepdims=True)
    polar = x * lax.rsqrt(frob + 1e-06)
    for _ in range(NS_STEPS):
        narrow = polar.astype(BF16)
        gram = dot(narrow, narrow, (1, 1)).astype(BF16)
        polar = 1.5 * polar - 0.5 * dot(gram, narrow, (1, 0))
    polar_out[...] = polar
    weight_out[0, 0] = product(polar, x, (0, 0)).astype(BF16)


def hand_kernel(near, far, out):
    out[...] = pick(near[...], far[...], "seg", -1)


def store_kernel(value, out):
    out[0, 0] = value[...]


def inner_shards(
    left_env, right_env, left_piece, right_piece, guess, inverse_values, precond, sector_rows
):
    left, right, prec = left_env[0, 0], right_env[0, 0], precond[0, 0]
    channels, size = left.shape[0], left.shape[-1]
    matrix = jax.ShapeDtypeStruct((size, size), F32)
    narrow = jax.ShapeDtypeStruct((size, size), BF16)
    stats = jax.ShapeDtypeStruct((ROWS, LANES), F32)
    inner = pltpu.VMEM((size, channels * size), BF16)

    def call(kernel, outs, *operands, scratch=(), in_specs=None, out_specs=None, cost=None, limit=16 << 20):
        return pl.pallas_call(
            kernel,
            out_shape=outs,
            in_specs=in_specs or [VMEM] * len(operands),
            out_specs=out_specs or [VMEM] * len(outs),
            scratch_shapes=list(scratch),
            cost_estimate=cost,
            compiler_params=pltpu.CompilerParams(vmem_limit_bytes=limit),
        )(*operands)

    near, far = swaps(right_piece[0, 0], "seg")
    prec_below = rotate(prec, "sec", 1)
    (mask,) = call(mask_kernel, [matrix], sector_rows[0], in_specs=[SMEM], cost=COVER)
    scaled = (left_piece[0, 0].astype(F32) * inverse_values[0]).astype(BF16)

    y, yb = call(start_kernel, [matrix, narrow], scaled, near, far, guess[0, 0], mask)

    def half(vector_b, pairs, operands, sends):
        outs = [matrix, matrix, stats] + [narrow] * sends
        kernel = functools.partial(lower_kernel, pairs, sends)
        low, diag, stat, *sent = call(
            kernel, outs, left, right, vector_b, *operands, scratch=[inner]
        )
        return low, diag, stat, rotate(sent[0], "sec", -1) if sends else None

    def joined(below, after, diag, above):
        (up,) = call(raise_kernel, [matrix], left, right, below, after, scratch=[inner])
        return call(join_kernel, [matrix, narrow], diag, up, above, mask)

    y_below = rotate(yb, "sec", 1)
    low, diag, stat, above = half(yb, [(0, 0), (0, None)], [y], 1)
    (stat,) = call(cross_kernel, [stats], y_below, low, stat)
    parts = exchange(stat, "sec")
    g, gb = joined(y_below, stat, diag, above)
    g_below = rotate(gb, "sec", 1)
    kernel = functools.partial(first_kernel, len(parts))
    p, pb = call(kernel, [matrix, narrow], *parts, y, g, prec)

    pairs = [(0, 0), (0, 1), (0, 2), (2, 2), (2, 1), (2, None)]
    low, diag, stat, above = half(pb, pairs, [y, g, p], 1)
    kernel = functools.partial(first_cross_kernel, len(parts))
    stat, p_below = call(kernel, [stats, narrow], *parts, y_below, g_below, prec_below, low, stat)
    parts = exchange(stat, "sec")
    hp, hpb = joined(p_below, stat, diag, above)
    hp_below = rotate(hpb, "sec", 1)
    kernel = functools.partial(second_kernel, len(parts))
    x, g, p, pb, coefficients = call(
        kernel, [matrix, matrix, matrix, narrow, stats], *parts, y, g, p, hp, prec
    )

    pairs = [(0, 2), (2, 2), (2, 1), (2, None)]
    low, diag, stat, _ = half(pb, pairs, [x, g, p], 0)
    (stat,) = call(
        second_cross_kernel,
        [stats],
        y_below, g_below, p_below, hp_below, prec_below, coefficients, low, stat,
    )
    parts = exchange(stat, "sec")
    kernel = functools.partial(last_kernel, len(parts))
    block = (1, 1, size, size)
    polar, weight, energy = call(
        kernel,
        [
            matrix,
            jax.ShapeDtypeStruct(block, BF16),
            jax.ShapeDtypeStruct((1,), F32),
        ],
        *parts, x, p, coefficients,
        out_specs=[VMEM, VMEM, SMEM],
    )
    near, far = swaps(weight, "seg")
    (handed,) = call(hand_kernel, [jax.ShapeDtypeStruct(block, BF16)], near, far)
    (polar,) = call(store_kernel, [jax.ShapeDtypeStruct(block, F32)], polar, cost=SHORT)
    return polar, handed, energy


def solution(mesh):
    placed = (
        P("seg", "sec", None, None, None),
        P("seg", "sec", None, None, None),
        P("seg", "sec", None, None),
        P("seg", "sec", None, None),
        P("seg", "sec", None, None),
        P("seg", "sec", None),
        P("seg", "sec", None, None),
        P("seg", "sec"),
    )
    return jax.shard_map(
        inner_shards,
        mesh=mesh,
        in_specs=placed,
        out_specs=(P("seg", "sec", None, None), P("seg", "sec", None, None), P("seg")),
        check_vma=False,
    )
```

```python
import functools

import jax
import jax.numpy as jnp
from jax import lax
from jax.experimental import pallas as pl
from jax.experimental.pallas import tpu as pltpu
from jax.sharding import PartitionSpec as P


WD = 2
NS_STEPS = 3
ROWS = 8
LANES = 128
F32 = jnp.float32
BF16 = jnp.bfloat16
VMEM = pl.BlockSpec(memory_space=pltpu.VMEM)
SMEM = pl.BlockSpec(memory_space=pltpu.SMEM)
SHORT = pl.CostEstimate(flops=0, bytes_accessed=1 << 20, transcendentals=0)
COVER = pl.CostEstimate(flops=10**10, bytes_accessed=1 << 24, transcendentals=0)


def shift(value, axis, steps):
    count = lax.axis_size(axis)
    first, last = max(0, -steps), min(count, count - steps)
    return lax.ppermute(value, axis, [(source, source + steps) for source in range(first, last)])


def swap(value, axis, first):
    count = lax.axis_size(axis)
    pairs = {i: i for i in range(count)}
    for i in range(first, count - 1, 2):
        pairs[i], pairs[i + 1] = i + 1, i
    return lax.ppermute(value, axis, list(pairs.items()))


def rotate(value, axis, steps):
    count = lax.axis_size(axis)
    return lax.ppermute(value, axis, [(source, (source + steps) % count) for source in range(count)])


def from_below(value):
    return jnp.where(lax.axis_index("sec") > 0, value, jnp.zeros_like(value))


def from_above(value):
    last = lax.axis_size("sec") - 1
    return jnp.where(lax.axis_index("sec") < last, value, jnp.zeros_like(value))


def exchange(value, axis):
    count = lax.axis_size(axis)
    if count & (count - 1):
        return [lax.psum(value, axis)]
    parts, done = [value], 1
    while done < count:
        if len(parts) > 1:
            parts = [total(parts)]
        radix = 4 if count // done >= 4 else 2
        for digit in range(1, radix):
            pairs = [(source, source ^ (digit * done)) for source in range(count)]
            parts.append(lax.ppermute(parts[0], axis, pairs))
        done *= radix
    return parts


def total(parts):
    while len(parts) > 1:
        parts = [parts[i] + parts[i + 1] for i in range(0, len(parts), 2)]
    return parts[0]


def fold(product):
    row = jnp.sum(product, axis=0, keepdims=True)
    width = row.shape[-1]
    out = row[:, :LANES]
    for start in range(LANES, width, LANES):
        out = out + row[:, start : start + LANES]
    return out


def scalars(refs, count):
    sums = jnp.sum(total([ref[...] for ref in refs]), axis=1, keepdims=True)
    return [sums[i : i + 1] for i in range(count)]


def sandwich(left, right, value, inner, first, last):
    size = value.shape[-1]
    for w in range(first, last):
        product = jnp.dot(left[w], value, preferred_element_type=F32)
        inner[:, w * size : (w + 1) * size] = product.astype(BF16)
    stacked = right[first:last].reshape((last - first) * size, size)
    return jnp.dot(inner[:, first * size : last * size], stacked, preferred_element_type=F32)


def mask_kernel(rows, mask_out):
    count = rows[0]
    shape = mask_out.shape
    idx_r = lax.broadcasted_iota(jnp.int32, shape, 0)
    idx_c = lax.broadcasted_iota(jnp.int32, shape, 1)
    mask_out[...] = jnp.where((idx_r < count) & (idx_c < count), 1.0, 0.0)


def start_kernel(scaled, behind, guess, mask, y_ref, yb_ref):
    size = mask.shape[-1]
    start = jnp.dot(scaled[...], behind[...], preferred_element_type=F32) + guess[...].astype(F32)
    y = mask[...] * start * (1.0 / (1 << (size - 1).bit_length()))
    y_ref[...] = y
    yb_ref[...] = y.astype(BF16)


def lower_kernel(pairs, sends, left, right, vector_b, *refs):
    outs = refs[-5 if sends else -3 :]
    ops, inner = refs[: len(refs) - len(outs)], refs[-1]
    low_ref, stat_ref = outs[:2]
    channels = left.shape[0]
    value = vector_b[...]
    low = sandwich(left, right, value, inner, WD, channels)
    low_ref[...] = low
    diag = sandwich(left, right, value, inner, 0, WD)
    if sends:
        outs[2][...] = diag
        outs[3][...] = low.astype(BF16)
    stat_ref[...] = jnp.zeros(stat_ref.shape, F32)
    for row, (one, two) in enumerate(pairs):
        other = diag if two is None else ops[two][...]
        stat_ref[row : row + 1] = fold(ops[one][...] * other)


def add_cross(row, below, low, stat, out):
    out[...] = stat[...]
    out[row : row + 1] = stat[row : row + 1] + 2.0 * fold(from_below(below) * low[...])


def cross_kernel(below, low, stat, out):
    add_cross(1, below[...].astype(F32), low, stat, out)


def first_cross_kernel(parts, *refs):
    y, g, prec, low, stat, out, p_out = refs[parts:]
    yy, yhy = scalars(refs[:parts], 2)
    p = prec[...].astype(F32) * (g[...].astype(F32) - (yhy / yy) * y[...].astype(F32))
    p_out[...] = p.astype(BF16)
    add_cross(5, p, low, stat, out)


def second_cross_kernel(y, g, p, hp, prec, coefficients, low, stat, out):
    along_y, along_p, lam = [coefficients[i : i + 1, 0:1] for i in range(3)]
    x = along_y * y[...].astype(F32) + along_p * p[...].astype(F32)
    hx = along_y * g[...].astype(F32) + along_p * hp[...].astype(F32)
    add_cross(3, prec[...].astype(F32) * (hx - lam * x), low, stat, out)


def join_kernel(diag, up, above, mask, out, out_b):
    joined = mask[...] * (diag[...] + up[...] + from_above(above[...].astype(F32)))
    out[...] = joined
    out_b[...] = joined.astype(BF16)


def raise_kernel(left, right, below, after, up_ref, inner):
    up_ref[...] = from_below(sandwich(left, right, below[...], inner, WD, left.shape[0]))


def first_kernel(parts, *refs):
    y_ref, g_ref, prec, p_ref, pb_ref = refs[parts:]
    yy, yhy = scalars(refs[:parts], 2)
    p = prec[...].astype(F32) * (g_ref[...] - (yhy / yy) * y_ref[...])
    p_ref[...] = p
    pb_ref[...] = p.astype(BF16)


def ritz(a, b, c):
    lam = 0.5 * (a + c) - jnp.sqrt((0.5 * (a - c)) ** 2 + b * b)
    u, w = c - lam, -b
    n = jnp.sqrt(u * u + w * w)
    return lam, u / n, w / n


def second_kernel(parts, *refs):
    y_ref, g_ref, p_ref, hp_ref, prec = refs[parts : parts + 5]
    x_out, g_out, p_out, pb_out, coefficients = refs[parts + 5 :]
    yy, yg, yp, pp, pg, php = scalars(refs[:parts], 6)
    a = yg / yy
    s = yp / yy
    qq = pp - 2.0 * s * yp + s * s * yy
    b = (pg - s * yg) / jnp.sqrt(qq * yy)
    c = (php - 2.0 * s * pg + s * s * yg) / qq
    lam, u, w = ritz(a, b, c)
    along_p = w / jnp.sqrt(qq)
    along_y = u / jnp.sqrt(yy) - along_p * s
    x = along_y * y_ref[...] + along_p * p_ref[...]
    g = along_y * g_ref[...] + along_p * hp_ref[...]
    p = prec[...].astype(F32) * (g - lam * x)
    x_out[...] = x
    g_out[...] = g
    p_out[...] = p
    pb_out[...] = p.astype(BF16)
    for i, value in enumerate([along_y, along_p, lam]):
        coefficients[i : i + 1] = jnp.broadcast_to(value, (1, LANES))


def dot(one, two, over):
    dims = ((over[:1], over[1:]), ((), ()))
    return lax.dot_general(one, two, dims, preferred_element_type=F32)


def split(value):
    high = value.astype(BF16)
    return high, (value - high.astype(F32)).astype(BF16)


def product(one, two, over):
    (one_high, one_low), (two_high, two_low) = split(one), split(two)
    return dot(one_high, two_high, over) + (
        dot(one_high, two_low, over) + dot(one_low, two_high, over)
    )


def finish(sums, x_ref, p_ref, coefficients):
    xp, pp, pg, php = sums
    a = coefficients[2:3, 0:1]
    qq = pp - xp * xp
    b = (pg - xp * a) / jnp.sqrt(qq)
    c = (php - 2.0 * xp * pg + xp * xp * a) / qq
    lam, u, w = ritz(a, b, c)
    along_p = w / jnp.sqrt(qq)
    along_x = u - along_p * xp
    return lam, along_x * x_ref[...] + along_p * p_ref[...]


def polarise(x, polar_out, weight_out):
    frob = jnp.sum(jnp.sum(x * x, axis=0, keepdims=True), axis=1, keepdims=True)
    polar = x * lax.rsqrt(frob + 1e-06)
    for _ in range(NS_STEPS):
        narrow = polar.astype(BF16)
        gram = dot(narrow, narrow, (1, 1)).astype(BF16)
        polar = 1.5 * polar - 0.5 * dot(gram, narrow, (1, 0))
    polar_out[...] = polar
    weight_out[0, 0] = product(polar, x, (0, 0)).astype(BF16)


def odd_segment():
    return lax.rem(lax.axis_index("seg"), 2) == 1


def odd_kernel(parts, *refs):
    x_ref, p_ref, coefficients, polar_out, weight_out = refs[parts:]

    @pl.when(odd_segment())
    def _():
        _, x = finish(scalars(refs[:parts], 4), x_ref, p_ref, coefficients)
        polarise(x, polar_out, weight_out)

    @pl.when(jnp.logical_not(odd_segment()))
    def _():
        weight_out[...] = jnp.zeros_like(weight_out)


def even_kernel(parts, *refs):
    x_ref, p_ref, coefficients, _, polar_out, weight_out, lam_out = refs[parts:]

    @pl.when(jnp.logical_not(odd_segment()))
    def _():
        lam, x = finish(scalars(refs[:parts], 4), x_ref, p_ref, coefficients)
        lam_out[0] = lam[0, 0]
        polarise(x, polar_out, weight_out)

    @pl.when(odd_segment())
    def _():
        lam, _ = finish(scalars(refs[:parts], 4), x_ref, p_ref, coefficients)
        lam_out[0] = lam[0, 0]
        weight_out[...] = jnp.zeros_like(weight_out)


def hand_kernel(near, far, out):
    value = jnp.where(odd_segment(), near[...], far[...])
    out[...] = jnp.where(lax.axis_index("seg") > 0, value, jnp.zeros_like(value))


def store_kernel(value, out):
    out[0, 0] = value[...]


def inner_shards(
    left_env, right_env, left_piece, right_piece, guess, inverse_values, precond, sector_rows
):
    left, right, prec = left_env[0, 0], right_env[0, 0], precond[0, 0]
    channels, size = left.shape[0], left.shape[-1]
    matrix = jax.ShapeDtypeStruct((size, size), F32)
    narrow = jax.ShapeDtypeStruct((size, size), BF16)
    stats = jax.ShapeDtypeStruct((ROWS, LANES), F32)
    inner = pltpu.VMEM((size, channels * size), BF16)

    def call(kernel, outs, *operands, scratch=(), in_specs=None, out_specs=None, cost=None, aliases=None):
        return pl.pallas_call(
            kernel,
            out_shape=outs,
            in_specs=in_specs or [VMEM] * len(operands),
            out_specs=out_specs or [VMEM] * len(outs),
            scratch_shapes=list(scratch),
            cost_estimate=cost,
            input_output_aliases=aliases or {},
            compiler_params=pltpu.CompilerParams(vmem_limit_bytes=16 << 20),
        )(*operands)

    behind = shift(right_piece[0, 0], "seg", -1)
    prec_below = rotate(prec, "sec", 1)
    (mask,) = call(mask_kernel, [matrix], sector_rows[0], in_specs=[SMEM], cost=COVER)
    scaled = (left_piece[0, 0].astype(F32) * inverse_values[0]).astype(BF16)

    y, yb = call(start_kernel, [matrix, narrow], scaled, behind, guess[0, 0], mask)

    def half(vector_b, pairs, operands, sends):
        outs = [matrix, stats] + [matrix, narrow] * sends
        kernel = functools.partial(lower_kernel, pairs, sends)
        low, stat, *rest = call(kernel, outs, left, right, vector_b, *operands, scratch=[inner])
        if not sends:
            return low, stat
        diag, sent = rest
        return low, stat, diag, rotate(sent, "sec", -1)

    def joined(below, after, diag, above):
        (up,) = call(raise_kernel, [matrix], left, right, below, after, scratch=[inner])
        return call(join_kernel, [matrix, narrow], diag, up, above, mask)

    y_below = rotate(yb, "sec", 1)
    low, stat, diag, above = half(yb, [(0, 0), (0, None)], [y], 1)
    (stat,) = call(cross_kernel, [stats], y_below, low, stat)
    parts = exchange(stat, "sec")
    g, gb = joined(y_below, stat, diag, above)
    g_below = rotate(gb, "sec", 1)
    kernel = functools.partial(first_kernel, len(parts))
    p, pb = call(kernel, [matrix, narrow], *parts, y, g, prec)

    pairs = [(0, 0), (0, 1), (0, 2), (2, 2), (2, 1), (2, None)]
    low, stat, diag, above = half(pb, pairs, [y, g, p], 1)
    kernel = functools.partial(first_cross_kernel, len(parts))
    stat, p_below = call(kernel, [stats, narrow], *parts, y_below, g_below, prec_below, low, stat)
    parts = exchange(stat, "sec")
    hp, hpb = joined(p_below, stat, diag, above)
    hp_below = rotate(hpb, "sec", 1)
    kernel = functools.partial(second_kernel, len(parts))
    x, g, p, pb, coefficients = call(
        kernel, [matrix, matrix, matrix, narrow, stats], *parts, y, g, p, hp, prec
    )

    pairs = [(0, 2), (2, 2), (2, 1), (2, None)]
    low, stat = half(pb, pairs, [x, g, p], 0)
    (stat,) = call(
        second_cross_kernel,
        [stats],
        y_below, g_below, p_below, hp_below, prec_below, coefficients, low, stat,
    )
    parts = exchange(stat, "sec")
    block = (1, 1, size, size)
    weight = jax.ShapeDtypeStruct(block, BF16)
    energy = jax.ShapeDtypeStruct((1,), F32)
    operands = (*parts, x, p, coefficients)
    polar, far = call(functools.partial(odd_kernel, len(parts)), [matrix, weight], *operands)
    far = swap(far, "seg", 1)
    polar, near, energy = call(
        functools.partial(even_kernel, len(parts)),
        [matrix, weight, energy],
        *operands, polar,
        out_specs=[VMEM, VMEM, SMEM],
        aliases={len(operands): 0},
    )
    near = swap(near, "seg", 0)
    (handed,) = call(hand_kernel, [jax.ShapeDtypeStruct(block, BF16)], near, far)
    (polar,) = call(store_kernel, [jax.ShapeDtypeStruct(block, F32)], polar, cost=SHORT)
    return polar, handed, energy


def solution(mesh):
    placed = (
        P("seg", "sec", None, None, None),
        P("seg", "sec", None, None, None),
        P("seg", "sec", None, None),
        P("seg", "sec", None, None),
        P("seg", "sec", None, None),
        P("seg", "sec", None),
        P("seg", "sec", None, None),
        P("seg", "sec"),
    )
    return jax.shard_map(
        inner_shards,
        mesh=mesh,
        in_specs=placed,
        out_specs=(P("seg", "sec", None, None), P("seg", "sec", None, None), P("seg")),
        check_vma=False,
    )
```

```python
import functools

import jax
import jax.numpy as jnp
from jax import lax
from jax.experimental import pallas as pl
from jax.experimental.pallas import tpu as pltpu
from jax.sharding import PartitionSpec as P


WD = 2
NS_STEPS = 3
ROWS = 8
LANES = 128
F32 = jnp.float32
BF16 = jnp.bfloat16
VMEM = pl.BlockSpec(memory_space=pltpu.VMEM)
SMEM = pl.BlockSpec(memory_space=pltpu.SMEM)
SHORT = pl.CostEstimate(flops=0, bytes_accessed=1 << 20, transcendentals=0)
COVER = pl.CostEstimate(flops=10**10, bytes_accessed=1 << 24, transcendentals=0)


def shift(value, axis, steps):
    count = lax.axis_size(axis)
    first, last = max(0, -steps), min(count, count - steps)
    return lax.ppermute(value, axis, [(source, source + steps) for source in range(first, last)])


def swap(value, axis, first):
    count = lax.axis_size(axis)
    pairs = {i: i for i in range(count)}
    for i in range(first, count - 1, 2):
        pairs[i], pairs[i + 1] = i + 1, i
    return lax.ppermute(value, axis, list(pairs.items()))


def rotate(value, axis, steps):
    count = lax.axis_size(axis)
    return lax.ppermute(value, axis, [(source, (source + steps) % count) for source in range(count)])


def from_below(value):
    return jnp.where(lax.axis_index("sec") > 0, value, jnp.zeros_like(value))


def from_above(value):
    last = lax.axis_size("sec") - 1
    return jnp.where(lax.axis_index("sec") < last, value, jnp.zeros_like(value))


def exchange(value, axis):
    count = lax.axis_size(axis)
    if count & (count - 1):
        return [lax.psum(value, axis)]
    parts, done = [value], 1
    while done < count:
        if len(parts) > 1:
            parts = [total(parts)]
        radix = 4 if count // done >= 4 else 2
        for digit in range(1, radix):
            pairs = [(source, source ^ (digit * done)) for source in range(count)]
            parts.append(lax.ppermute(parts[0], axis, pairs))
        done *= radix
    return parts


def total(parts):
    while len(parts) > 1:
        parts = [parts[i] + parts[i + 1] for i in range(0, len(parts), 2)]
    return parts[0]


def fold(product):
    row = jnp.sum(product, axis=0, keepdims=True)
    width = row.shape[-1]
    out = row[:, :LANES]
    for start in range(LANES, width, LANES):
        out = out + row[:, start : start + LANES]
    return out


def scalars(refs, count):
    sums = jnp.sum(total([ref[...] for ref in refs]), axis=1, keepdims=True)
    return [sums[i : i + 1] for i in range(count)]


def sandwich(left, right, value, inner, first, last):
    size = value.shape[-1]
    for w in range(first, last):
        product = jnp.dot(left[w], value, preferred_element_type=F32)
        inner[:, w * size : (w + 1) * size] = product.astype(BF16)
    stacked = right[first:last].reshape((last - first) * size, size)
    return jnp.dot(inner[:, first * size : last * size], stacked, preferred_element_type=F32)


def cover_kernel(out):
    out[...] = jnp.zeros(out.shape, F32)


def mask_kernel(rows, _, mask_out):
    count = rows[...]
    shape = mask_out.shape
    idx_r = lax.broadcasted_iota(jnp.int32, shape, 0)
    idx_c = lax.broadcasted_iota(jnp.int32, shape, 1)
    mask_out[...] = jnp.where((idx_r < count) & (idx_c < count), 1.0, 0.0)


def start_kernel(scaled, behind, guess, mask, y_ref, yb_ref):
    size = mask.shape[-1]
    start = jnp.dot(scaled[...], behind[...], preferred_element_type=F32) + guess[...].astype(F32)
    y = mask[...] * start * (1.0 / (1 << (size - 1).bit_length()))
    y_ref[...] = y
    yb_ref[...] = y.astype(BF16)


def lower_kernel(pairs, sends, left, right, vector_b, *refs):
    outs = refs[-5 if sends else -3 :]
    ops, inner = refs[: len(refs) - len(outs)], refs[-1]
    low_ref, stat_ref = outs[:2]
    channels = left.shape[0]
    value = vector_b[...]
    low = sandwich(left, right, value, inner, WD, channels)
    low_ref[...] = low
    diag = sandwich(left, right, value, inner, 0, WD)
    if sends:
        outs[2][...] = diag
        outs[3][...] = low.astype(BF16)
    stat_ref[...] = jnp.zeros(stat_ref.shape, F32)
    for row, (one, two) in enumerate(pairs):
        other = diag if two is None else ops[two][...]
        stat_ref[row : row + 1] = fold(ops[one][...] * other)


def add_cross(row, below, low, stat, out):
    out[...] = stat[...]
    out[row : row + 1] = stat[row : row + 1] + 2.0 * fold(from_below(below) * low[...])


def cross_kernel(below, low, stat, out):
    add_cross(1, below[...].astype(F32), low, stat, out)


def first_cross_kernel(parts, *refs):
    y, g, prec, low, stat, out, p_out = refs[parts:]
    yy, yhy = scalars(refs[:parts], 2)
    p = prec[...].astype(F32) * (g[...].astype(F32) - (yhy / yy) * y[...].astype(F32))
    p_out[...] = p.astype(BF16)
    add_cross(5, p, low, stat, out)


def second_cross_kernel(y, g, p, hp, prec, coefficients, low, stat, out):
    along_y, along_p, lam = [coefficients[i : i + 1, 0:1] for i in range(3)]
    x = along_y * y[...].astype(F32) + along_p * p[...].astype(F32)
    hx = along_y * g[...].astype(F32) + along_p * hp[...].astype(F32)
    add_cross(3, prec[...].astype(F32) * (hx - lam * x), low, stat, out)


def join_kernel(diag, up, above, mask, out, out_b):
    joined = mask[...] * (diag[...] + up[...] + from_above(above[...].astype(F32)))
    out[...] = joined
    out_b[...] = joined.astype(BF16)


def raise_kernel(left, right, below, after, up_ref, inner):
    up_ref[...] = from_below(sandwich(left, right, below[...], inner, WD, left.shape[0]))


def first_kernel(parts, *refs):
    y_ref, g_ref, prec, p_ref, pb_ref = refs[parts:]
    yy, yhy = scalars(refs[:parts], 2)
    p = prec[...].astype(F32) * (g_ref[...] - (yhy / yy) * y_ref[...])
    p_ref[...] = p
    pb_ref[...] = p.astype(BF16)


def ritz(a, b, c):
    lam = 0.5 * (a + c) - jnp.sqrt((0.5 * (a - c)) ** 2 + b * b)
    u, w = c - lam, -b
    n = jnp.sqrt(u * u + w * w)
    return lam, u / n, w / n


def second_kernel(parts, *refs):
    y_ref, g_ref, p_ref, hp_ref, prec = refs[parts : parts + 5]
    x_out, g_out, p_out, pb_out, coefficients = refs[parts + 5 :]
    yy, yg, yp, pp, pg, php = scalars(refs[:parts], 6)
    a = yg / yy
    s = yp / yy
    qq = pp - 2.0 * s * yp + s * s * yy
    b = (pg - s * yg) / jnp.sqrt(qq * yy)
    c = (php - 2.0 * s * pg + s * s * yg) / qq
    lam, u, w = ritz(a, b, c)
    along_p = w / jnp.sqrt(qq)
    along_y = u / jnp.sqrt(yy) - along_p * s
    x = along_y * y_ref[...] + along_p * p_ref[...]
    g = along_y * g_ref[...] + along_p * hp_ref[...]
    p = prec[...].astype(F32) * (g - lam * x)
    x_out[...] = x
    g_out[...] = g
    p_out[...] = p
    pb_out[...] = p.astype(BF16)
    for i, value in enumerate([along_y, along_p, lam]):
        coefficients[i : i + 1] = jnp.broadcast_to(value, (1, LANES))


def dot(one, two, over):
    dims = ((over[:1], over[1:]), ((), ()))
    return lax.dot_general(one, two, dims, preferred_element_type=F32)


def split(value):
    high = value.astype(BF16)
    return high, (value - high.astype(F32)).astype(BF16)


def product(one, two, over):
    (one_high, one_low), (two_high, two_low) = split(one), split(two)
    return dot(one_high, two_high, over) + (
        dot(one_high, two_low, over) + dot(one_low, two_high, over)
    )


def finish(sums, x_ref, p_ref, coefficients):
    xp, pp, pg, php = sums
    a = coefficients[2:3, 0:1]
    qq = pp - xp * xp
    b = (pg - xp * a) / jnp.sqrt(qq)
    c = (php - 2.0 * xp * pg + xp * xp * a) / qq
    lam, u, w = ritz(a, b, c)
    along_p = w / jnp.sqrt(qq)
    along_x = u - along_p * xp
    return lam, along_x * x_ref[...] + along_p * p_ref[...]


def polarise(x, polar_out, weight_out):
    frob = jnp.sum(jnp.sum(x * x, axis=0, keepdims=True), axis=1, keepdims=True)
    polar = x * lax.rsqrt(frob + 1e-06)
    for _ in range(NS_STEPS):
        narrow = polar.astype(BF16)
        gram = dot(narrow, narrow, (1, 1)).astype(BF16)
        polar = 1.5 * polar - 0.5 * dot(gram, narrow, (1, 0))
    polar_out[...] = polar
    weight_out[0, 0] = product(polar, x, (0, 0)).astype(BF16)


def odd_segment():
    return lax.rem(lax.axis_index("seg"), 2) == 1


def odd_kernel(parts, *refs):
    x_ref, p_ref, coefficients, polar_out, weight_out = refs[parts:]

    @pl.when(odd_segment())
    def _():
        _, x = finish(scalars(refs[:parts], 4), x_ref, p_ref, coefficients)
        polarise(x, polar_out, weight_out)

    @pl.when(jnp.logical_not(odd_segment()))
    def _():
        weight_out[...] = jnp.zeros_like(weight_out)


def even_kernel(parts, *refs):
    x_ref, p_ref, coefficients, _, polar_out, weight_out, lam_out = refs[parts:]

    @pl.when(jnp.logical_not(odd_segment()))
    def _():
        lam, x = finish(scalars(refs[:parts], 4), x_ref, p_ref, coefficients)
        lam_out[0] = lam[0, 0]
        polarise(x, polar_out, weight_out)

    @pl.when(odd_segment())
    def _():
        lam, _ = finish(scalars(refs[:parts], 4), x_ref, p_ref, coefficients)
        lam_out[0] = lam[0, 0]
        weight_out[...] = jnp.zeros_like(weight_out)


def hand_kernel(near, far, out):
    value = jnp.where(odd_segment(), near[...], far[...])
    out[...] = jnp.where(lax.axis_index("seg") > 0, value, jnp.zeros_like(value))


def store_kernel(value, out):
    out[0, 0] = value[...]


def inner_shards(
    left_env, right_env, left_piece, right_piece, guess, inverse_values, precond, sector_rows
):
    left, right, prec = left_env[0, 0], right_env[0, 0], precond[0, 0]
    channels, size = left.shape[0], left.shape[-1]
    matrix = jax.ShapeDtypeStruct((size, size), F32)
    narrow = jax.ShapeDtypeStruct((size, size), BF16)
    stats = jax.ShapeDtypeStruct((ROWS, LANES), F32)
    inner = pltpu.VMEM((size, channels * size), BF16)

    def call(kernel, outs, *operands, scratch=(), in_specs=None, out_specs=None, cost=None, aliases=None):
        return pl.pallas_call(
            kernel,
            out_shape=outs,
            in_specs=in_specs or [VMEM] * len(operands),
            out_specs=out_specs or [VMEM] * len(outs),
            scratch_shapes=list(scratch),
            cost_estimate=cost,
            input_output_aliases=aliases or {},
            compiler_params=pltpu.CompilerParams(vmem_limit_bytes=16 << 20),
        )(*operands)

    (cover,) = call(cover_kernel, [stats], cost=COVER)
    behind = shift(right_piece[0, 0], "seg", -1)
    prec_below = rotate(prec, "sec", 1)
    (mask,) = call(mask_kernel, [matrix], sector_rows, cover)
    scaled = (left_piece[0, 0].astype(F32) * inverse_values[0]).astype(BF16)

    y, yb = call(start_kernel, [matrix, narrow], scaled, behind, guess[0, 0], mask)

    def half(vector_b, pairs, operands, sends):
        outs = [matrix, stats] + [matrix, narrow] * sends
        kernel = functools.partial(lower_kernel, pairs, sends)
        low, stat, *rest = call(kernel, outs, left, right, vector_b, *operands, scratch=[inner])
        if not sends:
            return low, stat
        diag, sent = rest
        return low, stat, diag, rotate(sent, "sec", -1)

    def joined(below, after, diag, above):
        (up,) = call(raise_kernel, [matrix], left, right, below, after, scratch=[inner])
        return call(join_kernel, [matrix, narrow], diag, up, above, mask)

    y_below = rotate(yb, "sec", 1)
    low, stat, diag, above = half(yb, [(0, 0), (0, None)], [y], 1)
    (stat,) = call(cross_kernel, [stats], y_below, low, stat)
    parts = exchange(stat, "sec")
    g, gb = joined(y_below, stat, diag, above)
    g_below = rotate(gb, "sec", 1)
    kernel = functools.partial(first_kernel, len(parts))
    p, pb = call(kernel, [matrix, narrow], *parts, y, g, prec)

    pairs = [(0, 0), (0, 1), (0, 2), (2, 2), (2, 1), (2, None)]
    low, stat, diag, above = half(pb, pairs, [y, g, p], 1)
    kernel = functools.partial(first_cross_kernel, len(parts))
    stat, p_below = call(kernel, [stats, narrow], *parts, y_below, g_below, prec_below, low, stat)
    parts = exchange(stat, "sec")
    hp, hpb = joined(p_below, stat, diag, above)
    hp_below = rotate(hpb, "sec", 1)
    kernel = functools.partial(second_kernel, len(parts))
    x, g, p, pb, coefficients = call(
        kernel, [matrix, matrix, matrix, narrow, stats], *parts, y, g, p, hp, prec
    )

    pairs = [(0, 2), (2, 2), (2, 1), (2, None)]
    low, stat = half(pb, pairs, [x, g, p], 0)
    (stat,) = call(
        second_cross_kernel,
        [stats],
        y_below, g_below, p_below, hp_below, prec_below, coefficients, low, stat,
    )
    parts = exchange(stat, "sec")
    block = (1, 1, size, size)
    weight = jax.ShapeDtypeStruct(block, BF16)
    energy = jax.ShapeDtypeStruct((1,), F32)
    operands = (*parts, x, p, coefficients)
    polar, far = call(functools.partial(odd_kernel, len(parts)), [matrix, weight], *operands)
    far = swap(far, "seg", 1)
    polar, near, energy = call(
        functools.partial(even_kernel, len(parts)),
        [matrix, weight, energy],
        *operands, polar,
        out_specs=[VMEM, VMEM, SMEM],
        aliases={len(operands): 0},
    )
    near = swap(near, "seg", 0)
    (handed,) = call(hand_kernel, [jax.ShapeDtypeStruct(block, BF16)], near, far)
    (polar,) = call(store_kernel, [jax.ShapeDtypeStruct(block, F32)], polar, cost=SHORT)
    return polar, handed, energy


def solution(mesh):
    placed = (
        P("seg", "sec", None, None, None),
        P("seg", "sec", None, None, None),
        P("seg", "sec", None, None),
        P("seg", "sec", None, None),
        P("seg", "sec", None, None),
        P("seg", "sec", None),
        P("seg", "sec", None, None),
        P("seg", "sec"),
    )
    return jax.shard_map(
        inner_shards,
        mesh=mesh,
        in_specs=placed,
        out_specs=(P("seg", "sec", None, None), P("seg", "sec", None, None), P("seg")),
        check_vma=False,
    )
```

```python
import functools

import jax
import jax.numpy as jnp
from jax import lax
from jax.experimental import pallas as pl
from jax.experimental.pallas import tpu as pltpu
from jax.sharding import PartitionSpec as P


WD = 2
NS_STEPS = 3
ROWS = 8
LANES = 128
F32 = jnp.float32
BF16 = jnp.bfloat16
VMEM = pl.BlockSpec(memory_space=pltpu.VMEM)
SMEM = pl.BlockSpec(memory_space=pltpu.SMEM)
SHORT = pl.CostEstimate(flops=0, bytes_accessed=1 << 20, transcendentals=0)
COVER = pl.CostEstimate(flops=10**10, bytes_accessed=1 << 24, transcendentals=0)


def shift(value, axis, steps):
    count = lax.axis_size(axis)
    first, last = max(0, -steps), min(count, count - steps)
    return lax.ppermute(value, axis, [(source, source + steps) for source in range(first, last)])


def swap(value, axis, first):
    count = lax.axis_size(axis)
    pairs = {i: i for i in range(count)}
    for i in range(first, count - 1, 2):
        pairs[i], pairs[i + 1] = i + 1, i
    return lax.ppermute(value, axis, list(pairs.items()))


def rotate(value, axis, steps):
    count = lax.axis_size(axis)
    return lax.ppermute(value, axis, [(source, (source + steps) % count) for source in range(count)])


def from_below(value):
    return jnp.where(lax.axis_index("sec") > 0, value, jnp.zeros_like(value))


def from_above(value):
    last = lax.axis_size("sec") - 1
    return jnp.where(lax.axis_index("sec") < last, value, jnp.zeros_like(value))


def exchange(value, axis):
    count = lax.axis_size(axis)
    if count & (count - 1):
        return [lax.psum(value, axis)]
    parts, done = [value], 1
    while done < count:
        if len(parts) > 1:
            parts = [total(parts)]
        radix = 4 if count // done >= 4 else 2
        for digit in range(1, radix):
            pairs = [(source, source ^ (digit * done)) for source in range(count)]
            parts.append(lax.ppermute(parts[0], axis, pairs))
        done *= radix
    return parts


def total(parts):
    while len(parts) > 1:
        parts = [parts[i] + parts[i + 1] for i in range(0, len(parts), 2)]
    return parts[0]


def fold(product):
    row = jnp.sum(product, axis=0, keepdims=True)
    width = row.shape[-1]
    out = row[:, :LANES]
    for start in range(LANES, width, LANES):
        out = out + row[:, start : start + LANES]
    return out


def scalars(refs, count):
    sums = jnp.sum(total([ref[...] for ref in refs]), axis=1, keepdims=True)
    return [sums[i : i + 1] for i in range(count)]


def sandwich(left, right, value, inner, first, last):
    size = value.shape[-1]
    for w in range(first, last):
        product = jnp.dot(left[w], value, preferred_element_type=F32)
        inner[:, w * size : (w + 1) * size] = product.astype(BF16)
    stacked = right[first:last].reshape((last - first) * size, size)
    return jnp.dot(inner[:, first * size : last * size], stacked, preferred_element_type=F32)


def cover_kernel(out):
    out[...] = jnp.zeros(out.shape, F32)


def mask_kernel(rows, _, mask_out):
    count = rows[...]
    shape = mask_out.shape
    idx_r = lax.broadcasted_iota(jnp.int32, shape, 0)
    idx_c = lax.broadcasted_iota(jnp.int32, shape, 1)
    mask_out[...] = jnp.where((idx_r < count) & (idx_c < count), 1.0, 0.0)


def start_kernel(scaled, behind, guess, mask, y_ref, yb_ref):
    size = mask.shape[-1]
    start = jnp.dot(scaled[...], behind[...], preferred_element_type=F32) + guess[...].astype(F32)
    y = mask[...] * start * (1.0 / (1 << (size - 1).bit_length()))
    y_ref[...] = y
    yb_ref[...] = y.astype(BF16)


def lower_kernel(pairs, sends, left, right, vector_b, *refs):
    outs = refs[-5 if sends else -3 :]
    ops, inner = refs[: len(refs) - len(outs)], refs[-1]
    low_ref, stat_ref = outs[:2]
    channels = left.shape[0]
    value = vector_b[...]
    low = sandwich(left, right, value, inner, WD, channels)
    low_ref[...] = low
    diag = sandwich(left, right, value, inner, 0, WD)
    if sends:
        outs[2][...] = diag
        outs[3][...] = low.astype(BF16)
    stat_ref[...] = jnp.zeros(stat_ref.shape, F32)
    for row, (one, two) in enumerate(pairs):
        other = diag if two is None else ops[two][...]
        stat_ref[row : row + 1] = fold(ops[one][...] * other)


def add_cross(row, below, low, stat, out):
    out[...] = stat[...]
    out[row : row + 1] = stat[row : row + 1] + 2.0 * fold(from_below(below) * low[...])


def cross_kernel(below, low, stat, out):
    add_cross(1, below[...].astype(F32), low, stat, out)


def first_cross_kernel(parts, *refs):
    y, g, prec, low, stat, out, p_out = refs[parts:]
    yy, yhy = scalars(refs[:parts], 2)
    p = prec[...].astype(F32) * (g[...].astype(F32) - (yhy / yy) * y[...].astype(F32))
    p_out[...] = p.astype(BF16)
    add_cross(5, p, low, stat, out)


def second_cross_kernel(y, g, p, hp, prec, coefficients, low, stat, out):
    along_y, along_p, lam = [coefficients[i : i + 1, 0:1] for i in range(3)]
    x = along_y * y[...].astype(F32) + along_p * p[...].astype(F32)
    hx = along_y * g[...].astype(F32) + along_p * hp[...].astype(F32)
    add_cross(3, prec[...].astype(F32) * (hx - lam * x), low, stat, out)


def join_kernel(diag, up, above, mask, out, out_b):
    joined = mask[...] * (diag[...] + up[...] + from_above(above[...].astype(F32)))
    out[...] = joined
    out_b[...] = joined.astype(BF16)


def raise_kernel(left, right, below, after, up_ref, inner):
    up_ref[...] = from_below(sandwich(left, right, below[...], inner, WD, left.shape[0]))


def first_kernel(parts, *refs):
    y_ref, g_ref, prec, p_ref, pb_ref = refs[parts:]
    yy, yhy = scalars(refs[:parts], 2)
    p = prec[...].astype(F32) * (g_ref[...] - (yhy / yy) * y_ref[...])
    p_ref[...] = p
    pb_ref[...] = p.astype(BF16)


def ritz(a, b, c):
    lam = 0.5 * (a + c) - jnp.sqrt((0.5 * (a - c)) ** 2 + b * b)
    u, w = c - lam, -b
    n = jnp.sqrt(u * u + w * w)
    return lam, u / n, w / n


def second_kernel(parts, *refs):
    y_ref, g_ref, p_ref, hp_ref, prec = refs[parts : parts + 5]
    x_out, g_out, p_out, pb_out, coefficients = refs[parts + 5 :]
    yy, yg, yp, pp, pg, php = scalars(refs[:parts], 6)
    a = yg / yy
    s = yp / yy
    qq = pp - 2.0 * s * yp + s * s * yy
    b = (pg - s * yg) / jnp.sqrt(qq * yy)
    c = (php - 2.0 * s * pg + s * s * yg) / qq
    lam, u, w = ritz(a, b, c)
    along_p = w / jnp.sqrt(qq)
    along_y = u / jnp.sqrt(yy) - along_p * s
    x = along_y * y_ref[...] + along_p * p_ref[...]
    g = along_y * g_ref[...] + along_p * hp_ref[...]
    p = prec[...].astype(F32) * (g - lam * x)
    x_out[...] = x
    g_out[...] = g
    p_out[...] = p
    pb_out[...] = p.astype(BF16)
    for i, value in enumerate([along_y, along_p, lam]):
        coefficients[i : i + 1] = jnp.broadcast_to(value, (1, LANES))


def dot(one, two, over):
    dims = ((over[:1], over[1:]), ((), ()))
    return lax.dot_general(one, two, dims, preferred_element_type=F32)


def split(value):
    high = value.astype(BF16)
    return high, (value - high.astype(F32)).astype(BF16)


def product(one, two, over):
    (one_high, one_low), (two_high, two_low) = split(one), split(two)
    return dot(one_high, two_high, over) + (
        dot(one_high, two_low, over) + dot(one_low, two_high, over)
    )


def finish(sums, x_ref, p_ref, coefficients):
    xp, pp, pg, php = sums
    a = coefficients[2:3, 0:1]
    qq = pp - xp * xp
    b = (pg - xp * a) / jnp.sqrt(qq)
    c = (php - 2.0 * xp * pg + xp * xp * a) / qq
    lam, u, w = ritz(a, b, c)
    along_p = w / jnp.sqrt(qq)
    along_x = u - along_p * xp
    return lam, along_x * x_ref[...] + along_p * p_ref[...]


def polarise(x, polar_out, weight_out):
    frob = jnp.sum(jnp.sum(x * x, axis=0, keepdims=True), axis=1, keepdims=True)
    polar = x * lax.rsqrt(frob + 1e-06)
    for _ in range(NS_STEPS):
        narrow = polar.astype(BF16)
        gram = dot(narrow, narrow, (1, 1)).astype(BF16)
        polar = 1.5 * polar - 0.5 * dot(gram, narrow, (1, 0))
    polar_out[...] = polar
    weight_out[0, 0] = product(polar, x, (0, 0)).astype(BF16)


def odd_segment():
    return lax.rem(lax.axis_index("seg"), 2) == 1


def odd_kernel(parts, *refs):
    x_ref, p_ref, coefficients, polar_out, weight_out = refs[parts:]

    @pl.when(odd_segment())
    def _():
        _, x = finish(scalars(refs[:parts], 4), x_ref, p_ref, coefficients)
        polarise(x, polar_out, weight_out)

    @pl.when(jnp.logical_not(odd_segment()))
    def _():
        weight_out[...] = jnp.zeros_like(weight_out)


def even_kernel(parts, *refs):
    x_ref, p_ref, coefficients, _, polar_out, weight_out, lam_out = refs[parts:]

    @pl.when(jnp.logical_not(odd_segment()))
    def _():
        lam, x = finish(scalars(refs[:parts], 4), x_ref, p_ref, coefficients)
        lam_out[0] = lam[0, 0]
        polarise(x, polar_out, weight_out)

    @pl.when(odd_segment())
    def _():
        lam, _ = finish(scalars(refs[:parts], 4), x_ref, p_ref, coefficients)
        lam_out[0] = lam[0, 0]
        weight_out[...] = jnp.zeros_like(weight_out)


def hand_kernel(near, far, target, out, sems):
    value = jnp.where(odd_segment(), near[...], far[...])
    out[...] = jnp.where(lax.axis_index("seg") > 0, value, jnp.zeros_like(value))
    count = sems.shape[0]
    step = out.shape[2] // count
    copies = []
    for i in range(count):
        part = (0, 0, pl.ds(i * step, step))
        copies.append(pltpu.make_async_copy(out.at[part], target.at[part], sems.at[i]))
        copies[-1].start()
    for copy in copies:
        copy.wait()


def store_kernel(value, out):
    out[0, 0] = value[...]


def inner_shards(
    left_env, right_env, left_piece, right_piece, guess, inverse_values, precond, sector_rows
):
    left, right, prec = left_env[0, 0], right_env[0, 0], precond[0, 0]
    channels, size = left.shape[0], left.shape[-1]
    matrix = jax.ShapeDtypeStruct((size, size), F32)
    narrow = jax.ShapeDtypeStruct((size, size), BF16)
    stats = jax.ShapeDtypeStruct((ROWS, LANES), F32)
    inner = pltpu.VMEM((size, channels * size), BF16)

    def call(kernel, outs, *operands, scratch=(), in_specs=None, out_specs=None, cost=None, aliases=None):
        return pl.pallas_call(
            kernel,
            out_shape=outs,
            in_specs=in_specs or [VMEM] * len(operands),
            out_specs=out_specs or [VMEM] * len(outs),
            scratch_shapes=list(scratch),
            cost_estimate=cost,
            input_output_aliases=aliases or {},
            compiler_params=pltpu.CompilerParams(vmem_limit_bytes=16 << 20),
        )(*operands)

    (cover,) = call(cover_kernel, [stats], cost=COVER)
    behind = shift(right_piece[0, 0], "seg", -1)
    prec_below = rotate(prec, "sec", 1)
    (mask,) = call(mask_kernel, [matrix], sector_rows, cover)
    scaled = (left_piece[0, 0].astype(F32) * inverse_values[0]).astype(BF16)

    y, yb = call(start_kernel, [matrix, narrow], scaled, behind, guess[0, 0], mask)

    def half(vector_b, pairs, operands, sends):
        outs = [matrix, stats] + [matrix, narrow] * sends
        kernel = functools.partial(lower_kernel, pairs, sends)
        low, stat, *rest = call(kernel, outs, left, right, vector_b, *operands, scratch=[inner])
        if not sends:
            return low, stat
        diag, sent = rest
        return low, stat, diag, rotate(sent, "sec", -1)

    def joined(below, after, diag, above):
        (up,) = call(raise_kernel, [matrix], left, right, below, after, scratch=[inner])
        return call(join_kernel, [matrix, narrow], diag, up, above, mask)

    y_below = rotate(yb, "sec", 1)
    low, stat, diag, above = half(yb, [(0, 0), (0, None)], [y], 1)
    (stat,) = call(cross_kernel, [stats], y_below, low, stat)
    parts = exchange(stat, "sec")
    g, gb = joined(y_below, stat, diag, above)
    g_below = rotate(gb, "sec", 1)
    kernel = functools.partial(first_kernel, len(parts))
    p, pb = call(kernel, [matrix, narrow], *parts, y, g, prec)

    pairs = [(0, 0), (0, 1), (0, 2), (2, 2), (2, 1), (2, None)]
    low, stat, diag, above = half(pb, pairs, [y, g, p], 1)
    kernel = functools.partial(first_cross_kernel, len(parts))
    stat, p_below = call(kernel, [stats, narrow], *parts, y_below, g_below, prec_below, low, stat)
    parts = exchange(stat, "sec")
    hp, hpb = joined(p_below, stat, diag, above)
    hp_below = rotate(hpb, "sec", 1)
    kernel = functools.partial(second_kernel, len(parts))
    x, g, p, pb, coefficients = call(
        kernel, [matrix, matrix, matrix, narrow, stats], *parts, y, g, p, hp, prec
    )

    pairs = [(0, 2), (2, 2), (2, 1), (2, None)]
    low, stat = half(pb, pairs, [x, g, p], 0)
    (stat,) = call(
        second_cross_kernel,
        [stats],
        y_below, g_below, p_below, hp_below, prec_below, coefficients, low, stat,
    )
    parts = exchange(stat, "sec")
    block = (1, 1, size, size)
    weight = jax.ShapeDtypeStruct(block, BF16)
    energy = jax.ShapeDtypeStruct((1,), F32)
    operands = (*parts, x, p, coefficients)
    polar, far = call(functools.partial(odd_kernel, len(parts)), [matrix, weight], *operands)
    far = swap(far, "seg", 1)
    polar, near, energy = call(
        functools.partial(even_kernel, len(parts)),
        [matrix, weight, energy],
        *operands, polar,
        out_specs=[VMEM, VMEM, SMEM],
        aliases={len(operands): 0},
    )
    near = swap(near, "seg", 0)
    (handed,) = call(
        hand_kernel,
        [weight],
        near, far,
        scratch=[pltpu.VMEM(block, BF16), pltpu.SemaphoreType.DMA((4,))],
        out_specs=[pl.BlockSpec(memory_space=pltpu.HBM)],
    )
    (polar,) = call(store_kernel, [jax.ShapeDtypeStruct(block, F32)], polar, cost=SHORT)
    return polar, handed, energy


def solution(mesh):
    placed = (
        P("seg", "sec", None, None, None),
        P("seg", "sec", None, None, None),
        P("seg", "sec", None, None),
        P("seg", "sec", None, None),
        P("seg", "sec", None, None),
        P("seg", "sec", None),
        P("seg", "sec", None, None),
        P("seg", "sec"),
    )
    return jax.shard_map(
        inner_shards,
        mesh=mesh,
        in_specs=placed,
        out_specs=(P("seg", "sec", None, None), P("seg", "sec", None, None), P("seg")),
        check_vma=False,
    )
```

```python
import functools

import jax
import jax.numpy as jnp
from jax import lax
from jax.experimental import pallas as pl
from jax.experimental.pallas import tpu as pltpu
from jax.sharding import PartitionSpec as P


WD = 2
NS_STEPS = 3
ROWS = 8
LANES = 128
F32 = jnp.float32
BF16 = jnp.bfloat16
VMEM = pl.BlockSpec(memory_space=pltpu.VMEM)
SMEM = pl.BlockSpec(memory_space=pltpu.SMEM)
SHORT = pl.CostEstimate(flops=0, bytes_accessed=1 << 20, transcendentals=0)
COVER = pl.CostEstimate(flops=10**10, bytes_accessed=1 << 24, transcendentals=0)


def shift(value, axis, steps):
    count = lax.axis_size(axis)
    first, last = max(0, -steps), min(count, count - steps)
    return lax.ppermute(value, axis, [(source, source + steps) for source in range(first, last)])


def swap(value, axis, first):
    count = lax.axis_size(axis)
    pairs = {i: i for i in range(count)}
    for i in range(first, count - 1, 2):
        pairs[i], pairs[i + 1] = i + 1, i
    return lax.ppermute(value, axis, list(pairs.items()))


def rotate(value, axis, steps):
    count = lax.axis_size(axis)
    return lax.ppermute(value, axis, [(source, (source + steps) % count) for source in range(count)])


def from_below(value):
    return jnp.where(lax.axis_index("sec") > 0, value, jnp.zeros_like(value))


def from_above(value):
    last = lax.axis_size("sec") - 1
    return jnp.where(lax.axis_index("sec") < last, value, jnp.zeros_like(value))


def exchange(value, axis):
    count = lax.axis_size(axis)
    if count & (count - 1):
        return [lax.psum(value, axis)]
    parts, done = [value], 1
    while done < count:
        if len(parts) > 1:
            parts = [total(parts)]
        radix = 4 if count // done >= 4 else 2
        for digit in range(1, radix):
            pairs = [(source, source ^ (digit * done)) for source in range(count)]
            parts.append(lax.ppermute(parts[0], axis, pairs))
        done *= radix
    return parts


def pairwise(value, axis):
    count = lax.axis_size(axis)
    if count & (count - 1) or count == 1:
        return exchange(value, axis)
    stride, parts = count // 2, [value]
    while stride:
        if len(parts) > 1:
            parts = [total(parts)]
        pairs = [(source, source ^ stride) for source in range(count)]
        parts.append(lax.ppermute(parts[0], axis, pairs))
        stride //= 2
    return parts


def total(parts):
    while len(parts) > 1:
        parts = [parts[i] + parts[i + 1] for i in range(0, len(parts), 2)]
    return parts[0]


def fold(product):
    row = jnp.sum(product, axis=0, keepdims=True)
    width = row.shape[-1]
    out = row[:, :LANES]
    for start in range(LANES, width, LANES):
        out = out + row[:, start : start + LANES]
    return out


def scalars(refs, count):
    sums = jnp.sum(total([ref[...] for ref in refs]), axis=1, keepdims=True)
    return [sums[i : i + 1] for i in range(count)]


def sandwich(left, right, value, inner, first, last):
    size = value.shape[-1]
    for w in range(first, last):
        product = jnp.dot(left[w], value, preferred_element_type=F32)
        inner[:, w * size : (w + 1) * size] = product.astype(BF16)
    stacked = right[first:last].reshape((last - first) * size, size)
    return jnp.dot(inner[:, first * size : last * size], stacked, preferred_element_type=F32)


def cover_kernel(out):
    out[...] = jnp.zeros(out.shape, F32)


def mask_kernel(rows, _, mask_out):
    count = rows[...]
    shape = mask_out.shape
    idx_r = lax.broadcasted_iota(jnp.int32, shape, 0)
    idx_c = lax.broadcasted_iota(jnp.int32, shape, 1)
    mask_out[...] = jnp.where((idx_r < count) & (idx_c < count), 1.0, 0.0)


def start_kernel(scaled, behind, guess, mask, y_ref, yb_ref):
    size = mask.shape[-1]
    start = jnp.dot(scaled[...], behind[...], preferred_element_type=F32) + guess[...].astype(F32)
    y = mask[...] * start * (1.0 / (1 << (size - 1).bit_length()))
    y_ref[...] = y
    yb_ref[...] = y.astype(BF16)


def lower_kernel(pairs, sends, left, right, vector_b, *refs):
    outs = refs[-5 if sends else -3 :]
    ops, inner = refs[: len(refs) - len(outs)], refs[-1]
    low_ref, stat_ref = outs[:2]
    channels = left.shape[0]
    value = vector_b[...]
    low = sandwich(left, right, value, inner, WD, channels)
    low_ref[...] = low
    diag = sandwich(left, right, value, inner, 0, WD)
    if sends:
        outs[2][...] = diag
        outs[3][...] = low.astype(BF16)
    stat_ref[...] = jnp.zeros(stat_ref.shape, F32)
    for row, (one, two) in enumerate(pairs):
        other = diag if two is None else ops[two][...]
        stat_ref[row : row + 1] = fold(ops[one][...] * other)


def add_cross(row, below, low, stat, out):
    out[...] = stat[...]
    out[row : row + 1] = stat[row : row + 1] + 2.0 * fold(from_below(below) * low[...])


def cross_kernel(below, low, stat, out):
    add_cross(1, below[...].astype(F32), low, stat, out)


def first_cross_kernel(parts, *refs):
    y, g, prec, low, stat, out, p_out = refs[parts:]
    yy, yhy = scalars(refs[:parts], 2)
    p = prec[...].astype(F32) * (g[...].astype(F32) - (yhy / yy) * y[...].astype(F32))
    p_out[...] = p.astype(BF16)
    add_cross(5, p, low, stat, out)


def second_cross_kernel(y, g, p, hp, prec, coefficients, low, stat, out):
    along_y, along_p, lam = [coefficients[i : i + 1, 0:1] for i in range(3)]
    x = along_y * y[...].astype(F32) + along_p * p[...].astype(F32)
    hx = along_y * g[...].astype(F32) + along_p * hp[...].astype(F32)
    add_cross(3, prec[...].astype(F32) * (hx - lam * x), low, stat, out)


def join_kernel(diag, up, above, mask, out, out_b):
    joined = mask[...] * (diag[...] + up[...] + from_above(above[...].astype(F32)))
    out[...] = joined
    out_b[...] = joined.astype(BF16)


def raise_kernel(left, right, below, after, up_ref, inner):
    up_ref[...] = from_below(sandwich(left, right, below[...], inner, WD, left.shape[0]))


def first_kernel(parts, *refs):
    y_ref, g_ref, prec, p_ref, pb_ref = refs[parts:]
    yy, yhy = scalars(refs[:parts], 2)
    p = prec[...].astype(F32) * (g_ref[...] - (yhy / yy) * y_ref[...])
    p_ref[...] = p
    pb_ref[...] = p.astype(BF16)


def ritz(a, b, c):
    lam = 0.5 * (a + c) - jnp.sqrt((0.5 * (a - c)) ** 2 + b * b)
    u, w = c - lam, -b
    n = jnp.sqrt(u * u + w * w)
    return lam, u / n, w / n


def second_kernel(parts, *refs):
    y_ref, g_ref, p_ref, hp_ref, prec = refs[parts : parts + 5]
    x_out, g_out, p_out, pb_out, coefficients = refs[parts + 5 :]
    yy, yg, yp, pp, pg, php = scalars(refs[:parts], 6)
    a = yg / yy
    s = yp / yy
    qq = pp - 2.0 * s * yp + s * s * yy
    b = (pg - s * yg) / jnp.sqrt(qq * yy)
    c = (php - 2.0 * s * pg + s * s * yg) / qq
    lam, u, w = ritz(a, b, c)
    along_p = w / jnp.sqrt(qq)
    along_y = u / jnp.sqrt(yy) - along_p * s
    x = along_y * y_ref[...] + along_p * p_ref[...]
    g = along_y * g_ref[...] + along_p * hp_ref[...]
    p = prec[...].astype(F32) * (g - lam * x)
    x_out[...] = x
    g_out[...] = g
    p_out[...] = p
    pb_out[...] = p.astype(BF16)
    for i, value in enumerate([along_y, along_p, lam]):
        coefficients[i : i + 1] = jnp.broadcast_to(value, (1, LANES))


def dot(one, two, over):
    dims = ((over[:1], over[1:]), ((), ()))
    return lax.dot_general(one, two, dims, preferred_element_type=F32)


def split(value):
    high = value.astype(BF16)
    return high, (value - high.astype(F32)).astype(BF16)


def product(one, two, over):
    (one_high, one_low), (two_high, two_low) = split(one), split(two)
    return dot(one_high, two_high, over) + (
        dot(one_high, two_low, over) + dot(one_low, two_high, over)
    )


def finish(sums, x_ref, p_ref, coefficients):
    xp, pp, pg, php = sums
    a = coefficients[2:3, 0:1]
    qq = pp - xp * xp
    b = (pg - xp * a) / jnp.sqrt(qq)
    c = (php - 2.0 * xp * pg + xp * xp * a) / qq
    lam, u, w = ritz(a, b, c)
    along_p = w / jnp.sqrt(qq)
    along_x = u - along_p * xp
    return lam, along_x * x_ref[...] + along_p * p_ref[...]


def polarise(x, polar_out, weight_out):
    frob = jnp.sum(jnp.sum(x * x, axis=0, keepdims=True), axis=1, keepdims=True)
    polar = x * lax.rsqrt(frob + 1e-06)
    for _ in range(NS_STEPS):
        narrow = polar.astype(BF16)
        gram = dot(narrow, narrow, (1, 1)).astype(BF16)
        polar = 1.5 * polar - 0.5 * dot(gram, narrow, (1, 0))
    polar_out[...] = polar
    weight_out[0, 0] = product(polar, x, (0, 0)).astype(BF16)


def odd_segment():
    return lax.rem(lax.axis_index("seg"), 2) == 1


def odd_kernel(parts, *refs):
    x_ref, p_ref, coefficients, polar_out, weight_out = refs[parts:]

    @pl.when(odd_segment())
    def _():
        _, x = finish(scalars(refs[:parts], 4), x_ref, p_ref, coefficients)
        polarise(x, polar_out, weight_out)

    @pl.when(jnp.logical_not(odd_segment()))
    def _():
        weight_out[...] = jnp.zeros_like(weight_out)


def even_kernel(parts, *refs):
    x_ref, p_ref, coefficients, _, polar_out, weight_out, lam_out = refs[parts:]

    @pl.when(jnp.logical_not(odd_segment()))
    def _():
        lam, x = finish(scalars(refs[:parts], 4), x_ref, p_ref, coefficients)
        lam_out[0] = lam[0, 0]
        polarise(x, polar_out, weight_out)

    @pl.when(odd_segment())
    def _():
        lam, _ = finish(scalars(refs[:parts], 4), x_ref, p_ref, coefficients)
        lam_out[0] = lam[0, 0]
        weight_out[...] = jnp.zeros_like(weight_out)


def hand_kernel(near, far, out):
    value = jnp.where(odd_segment(), near[...], far[...])
    out[...] = jnp.where(lax.axis_index("seg") > 0, value, jnp.zeros_like(value))


def store_kernel(value, out):
    out[0, 0] = value[...]


def inner_shards(
    left_env, right_env, left_piece, right_piece, guess, inverse_values, precond, sector_rows
):
    left, right, prec = left_env[0, 0], right_env[0, 0], precond[0, 0]
    channels, size = left.shape[0], left.shape[-1]
    matrix = jax.ShapeDtypeStruct((size, size), F32)
    narrow = jax.ShapeDtypeStruct((size, size), BF16)
    stats = jax.ShapeDtypeStruct((ROWS, LANES), F32)
    inner = pltpu.VMEM((size, channels * size), BF16)

    def call(kernel, outs, *operands, scratch=(), in_specs=None, out_specs=None, cost=None, aliases=None):
        return pl.pallas_call(
            kernel,
            out_shape=outs,
            in_specs=in_specs or [VMEM] * len(operands),
            out_specs=out_specs or [VMEM] * len(outs),
            scratch_shapes=list(scratch),
            cost_estimate=cost,
            input_output_aliases=aliases or {},
            compiler_params=pltpu.CompilerParams(vmem_limit_bytes=16 << 20),
        )(*operands)

    (cover,) = call(cover_kernel, [stats], cost=COVER)
    behind = shift(right_piece[0, 0], "seg", -1)
    prec_below = rotate(prec, "sec", 1)
    (mask,) = call(mask_kernel, [matrix], sector_rows, cover)
    scaled = (left_piece[0, 0].astype(F32) * inverse_values[0]).astype(BF16)

    y, yb = call(start_kernel, [matrix, narrow], scaled, behind, guess[0, 0], mask)

    def half(vector_b, pairs, operands, sends):
        outs = [matrix, stats] + [matrix, narrow] * sends
        kernel = functools.partial(lower_kernel, pairs, sends)
        low, stat, *rest = call(kernel, outs, left, right, vector_b, *operands, scratch=[inner])
        if not sends:
            return low, stat
        diag, sent = rest
        return low, stat, diag, rotate(sent, "sec", -1)

    def joined(below, after, diag, above):
        (up,) = call(raise_kernel, [matrix], left, right, below, after, scratch=[inner])
        return call(join_kernel, [matrix, narrow], diag, up, above, mask)

    y_below = rotate(yb, "sec", 1)
    low, stat, diag, above = half(yb, [(0, 0), (0, None)], [y], 1)
    (stat,) = call(cross_kernel, [stats], y_below, low, stat)
    parts = pairwise(stat, "sec")
    g, gb = joined(y_below, stat, diag, above)
    g_below = rotate(gb, "sec", 1)
    kernel = functools.partial(first_kernel, len(parts))
    p, pb = call(kernel, [matrix, narrow], *parts, y, g, prec)

    pairs = [(0, 0), (0, 1), (0, 2), (2, 2), (2, 1), (2, None)]
    low, stat, diag, above = half(pb, pairs, [y, g, p], 1)
    kernel = functools.partial(first_cross_kernel, len(parts))
    stat, p_below = call(kernel, [stats, narrow], *parts, y_below, g_below, prec_below, low, stat)
    parts = pairwise(stat, "sec")
    hp, hpb = joined(p_below, stat, diag, above)
    hp_below = rotate(hpb, "sec", 1)
    kernel = functools.partial(second_kernel, len(parts))
    x, g, p, pb, coefficients = call(
        kernel, [matrix, matrix, matrix, narrow, stats], *parts, y, g, p, hp, prec
    )

    pairs = [(0, 2), (2, 2), (2, 1), (2, None)]
    low, stat = half(pb, pairs, [x, g, p], 0)
    (stat,) = call(
        second_cross_kernel,
        [stats],
        y_below, g_below, p_below, hp_below, prec_below, coefficients, low, stat,
    )
    parts = exchange(stat, "sec")
    block = (1, 1, size, size)
    weight = jax.ShapeDtypeStruct(block, BF16)
    energy = jax.ShapeDtypeStruct((1,), F32)
    operands = (*parts, x, p, coefficients)
    polar, far = call(functools.partial(odd_kernel, len(parts)), [matrix, weight], *operands)
    far = swap(far, "seg", 1)
    polar, near, energy = call(
        functools.partial(even_kernel, len(parts)),
        [matrix, weight, energy],
        *operands, polar,
        out_specs=[VMEM, VMEM, SMEM],
        aliases={len(operands): 0},
    )
    near = swap(near, "seg", 0)
    (handed,) = call(hand_kernel, [weight], near, far)
    (polar,) = call(store_kernel, [jax.ShapeDtypeStruct(block, F32)], polar, cost=SHORT)
    return polar, handed, energy


def solution(mesh):
    placed = (
        P("seg", "sec", None, None, None),
        P("seg", "sec", None, None, None),
        P("seg", "sec", None, None),
        P("seg", "sec", None, None),
        P("seg", "sec", None, None),
        P("seg", "sec", None),
        P("seg", "sec", None, None),
        P("seg", "sec"),
    )
    return jax.shard_map(
        inner_shards,
        mesh=mesh,
        in_specs=placed,
        out_specs=(P("seg", "sec", None, None), P("seg", "sec", None, None), P("seg")),
        check_vma=False,
    )
```

```python
import functools

import jax
import jax.numpy as jnp
from jax import lax
from jax.experimental import pallas as pl
from jax.experimental.pallas import tpu as pltpu
from jax.sharding import PartitionSpec as P


WD = 2
NS_STEPS = 3
ROWS = 8
LANES = 128
F32 = jnp.float32
BF16 = jnp.bfloat16
VMEM = pl.BlockSpec(memory_space=pltpu.VMEM)
SMEM = pl.BlockSpec(memory_space=pltpu.SMEM)
SHORT = pl.CostEstimate(flops=0, bytes_accessed=1 << 20, transcendentals=0)
COVER = pl.CostEstimate(flops=10**10, bytes_accessed=1 << 24, transcendentals=0)


def shift(value, axis, steps):
    count = lax.axis_size(axis)
    first, last = max(0, -steps), min(count, count - steps)
    return lax.ppermute(value, axis, [(source, source + steps) for source in range(first, last)])


def swap(value, axis, first):
    count = lax.axis_size(axis)
    pairs = {i: i for i in range(count)}
    for i in range(first, count - 1, 2):
        pairs[i], pairs[i + 1] = i + 1, i
    return lax.ppermute(value, axis, list(pairs.items()))


def rotate(value, axis, steps):
    count = lax.axis_size(axis)
    return lax.ppermute(value, axis, [(source, (source + steps) % count) for source in range(count)])


def from_below(value):
    return jnp.where(lax.axis_index("sec") > 0, value, jnp.zeros_like(value))


def from_above(value):
    last = lax.axis_size("sec") - 1
    return jnp.where(lax.axis_index("sec") < last, value, jnp.zeros_like(value))


def exchange(value, axis):
    count = lax.axis_size(axis)
    if count & (count - 1):
        return [lax.psum(value, axis)]
    parts, done = [value], 1
    while done < count:
        if len(parts) > 1:
            parts = [total(parts)]
        radix = 4 if count // done >= 4 else 2
        for digit in range(1, radix):
            pairs = [(source, source ^ (digit * done)) for source in range(count)]
            parts.append(lax.ppermute(parts[0], axis, pairs))
        done *= radix
    return parts


def pairwise(value, axis):
    count = lax.axis_size(axis)
    if count & (count - 1) or count == 1:
        return exchange(value, axis)
    stride, parts = 1, [value]
    while stride < count:
        if len(parts) > 1:
            parts = [total(parts)]
        pairs = [(source, source ^ stride) for source in range(count)]
        parts.append(lax.ppermute(parts[0], axis, pairs))
        stride *= 2
    return parts


def total(parts):
    while len(parts) > 1:
        parts = [parts[i] + parts[i + 1] for i in range(0, len(parts), 2)]
    return parts[0]


def fold(product):
    row = jnp.sum(product, axis=0, keepdims=True)
    width = row.shape[-1]
    out = row[:, :LANES]
    for start in range(LANES, width, LANES):
        out = out + row[:, start : start + LANES]
    return out


def scalars(refs, count):
    sums = jnp.sum(total([ref[...] for ref in refs]), axis=1, keepdims=True)
    return [sums[i : i + 1] for i in range(count)]


def sandwich(left, right, value, inner, first, last):
    size = value.shape[-1]
    for w in range(first, last):
        product = jnp.dot(left[w], value, preferred_element_type=F32)
        inner[:, w * size : (w + 1) * size] = product.astype(BF16)
    stacked = right[first:last].reshape((last - first) * size, size)
    return jnp.dot(inner[:, first * size : last * size], stacked, preferred_element_type=F32)


def cover_kernel(out):
    out[...] = jnp.zeros(out.shape, F32)


def mask_kernel(rows, _, mask_out):
    count = rows[...]
    shape = mask_out.shape
    idx_r = lax.broadcasted_iota(jnp.int32, shape, 0)
    idx_c = lax.broadcasted_iota(jnp.int32, shape, 1)
    mask_out[...] = jnp.where((idx_r < count) & (idx_c < count), 1.0, 0.0)


def start_kernel(scaled, behind, guess, mask, y_ref, yb_ref):
    size = mask.shape[-1]
    start = jnp.dot(scaled[...], behind[...], preferred_element_type=F32) + guess[...].astype(F32)
    y = mask[...] * start * (1.0 / (1 << (size - 1).bit_length()))
    y_ref[...] = y
    yb_ref[...] = y.astype(BF16)


def lower_kernel(pairs, sends, left, right, vector_b, *refs):
    outs = refs[-5 if sends else -3 :]
    ops, inner = refs[: len(refs) - len(outs)], refs[-1]
    low_ref, stat_ref = outs[:2]
    channels = left.shape[0]
    value = vector_b[...]
    low = sandwich(left, right, value, inner, WD, channels)
    low_ref[...] = low
    diag = sandwich(left, right, value, inner, 0, WD)
    if sends:
        outs[2][...] = diag
        outs[3][...] = low.astype(BF16)
    stat_ref[...] = jnp.zeros(stat_ref.shape, F32)
    for row, (one, two) in enumerate(pairs):
        other = diag if two is None else ops[two][...]
        stat_ref[row : row + 1] = fold(ops[one][...] * other)


def add_cross(row, below, low, stat, out):
    out[...] = stat[...]
    out[row : row + 1] = stat[row : row + 1] + 2.0 * fold(from_below(below) * low[...])


def cross_kernel(below, low, stat, out):
    add_cross(1, below[...].astype(F32), low, stat, out)


def first_cross_kernel(parts, *refs):
    y, g, prec, low, stat, out, p_out = refs[parts:]
    yy, yhy = scalars(refs[:parts], 2)
    p = prec[...].astype(F32) * (g[...].astype(F32) - (yhy / yy) * y[...].astype(F32))
    p_out[...] = p.astype(BF16)
    add_cross(5, p, low, stat, out)


def second_cross_kernel(y, g, p, hp, prec, coefficients, low, stat, out):
    along_y, along_p, lam = [coefficients[i : i + 1, 0:1] for i in range(3)]
    x = along_y * y[...].astype(F32) + along_p * p[...].astype(F32)
    hx = along_y * g[...].astype(F32) + along_p * hp[...].astype(F32)
    add_cross(3, prec[...].astype(F32) * (hx - lam * x), low, stat, out)


def join_kernel(diag, up, above, mask, out, out_b):
    joined = mask[...] * (diag[...] + up[...] + from_above(above[...].astype(F32)))
    out[...] = joined
    out_b[...] = joined.astype(BF16)


def raise_kernel(left, right, below, after, up_ref, inner):
    up_ref[...] = from_below(sandwich(left, right, below[...], inner, WD, left.shape[0]))


def first_kernel(parts, *refs):
    y_ref, g_ref, prec, p_ref, pb_ref = refs[parts:]
    yy, yhy = scalars(refs[:parts], 2)
    p = prec[...].astype(F32) * (g_ref[...] - (yhy / yy) * y_ref[...])
    p_ref[...] = p
    pb_ref[...] = p.astype(BF16)


def ritz(a, b, c):
    lam = 0.5 * (a + c) - jnp.sqrt((0.5 * (a - c)) ** 2 + b * b)
    u, w = c - lam, -b
    n = jnp.sqrt(u * u + w * w)
    return lam, u / n, w / n


def second_kernel(parts, *refs):
    y_ref, g_ref, p_ref, hp_ref, prec = refs[parts : parts + 5]
    x_out, g_out, p_out, pb_out, coefficients = refs[parts + 5 :]
    yy, yg, yp, pp, pg, php = scalars(refs[:parts], 6)
    a = yg / yy
    s = yp / yy
    qq = pp - 2.0 * s * yp + s * s * yy
    b = (pg - s * yg) / jnp.sqrt(qq * yy)
    c = (php - 2.0 * s * pg + s * s * yg) / qq
    lam, u, w = ritz(a, b, c)
    along_p = w / jnp.sqrt(qq)
    along_y = u / jnp.sqrt(yy) - along_p * s
    x = along_y * y_ref[...] + along_p * p_ref[...]
    g = along_y * g_ref[...] + along_p * hp_ref[...]
    p = prec[...].astype(F32) * (g - lam * x)
    x_out[...] = x
    g_out[...] = g
    p_out[...] = p
    pb_out[...] = p.astype(BF16)
    for i, value in enumerate([along_y, along_p, lam]):
        coefficients[i : i + 1] = jnp.broadcast_to(value, (1, LANES))


def dot(one, two, over):
    dims = ((over[:1], over[1:]), ((), ()))
    return lax.dot_general(one, two, dims, preferred_element_type=F32)


def split(value):
    high = value.astype(BF16)
    return high, (value - high.astype(F32)).astype(BF16)


def product(one, two, over):
    (one_high, one_low), (two_high, two_low) = split(one), split(two)
    return dot(one_high, two_high, over) + (
        dot(one_high, two_low, over) + dot(one_low, two_high, over)
    )


def finish(sums, x_ref, p_ref, coefficients):
    xp, pp, pg, php = sums
    a = coefficients[2:3, 0:1]
    qq = pp - xp * xp
    b = (pg - xp * a) / jnp.sqrt(qq)
    c = (php - 2.0 * xp * pg + xp * xp * a) / qq
    lam, u, w = ritz(a, b, c)
    along_p = w / jnp.sqrt(qq)
    along_x = u - along_p * xp
    return lam, along_x * x_ref[...] + along_p * p_ref[...]


def polarise(x, polar_out, weight_out):
    frob = jnp.sum(jnp.sum(x * x, axis=0, keepdims=True), axis=1, keepdims=True)
    polar = x * lax.rsqrt(frob + 1e-06)
    for _ in range(NS_STEPS):
        narrow = polar.astype(BF16)
        gram = dot(narrow, narrow, (1, 1)).astype(BF16)
        polar = 1.5 * polar - 0.5 * dot(gram, narrow, (1, 0))
    polar_out[...] = polar
    weight_out[0, 0] = product(polar, x, (0, 0)).astype(BF16)


def odd_segment():
    return lax.rem(lax.axis_index("seg"), 2) == 1


def odd_kernel(parts, *refs):
    x_ref, p_ref, coefficients, polar_out, weight_out = refs[parts:]

    @pl.when(odd_segment())
    def _():
        _, x = finish(scalars(refs[:parts], 4), x_ref, p_ref, coefficients)
        polarise(x, polar_out, weight_out)

    @pl.when(jnp.logical_not(odd_segment()))
    def _():
        weight_out[...] = jnp.zeros_like(weight_out)


def even_kernel(parts, *refs):
    x_ref, p_ref, coefficients, _, polar_out, weight_out, lam_out = refs[parts:]

    @pl.when(jnp.logical_not(odd_segment()))
    def _():
        lam, x = finish(scalars(refs[:parts], 4), x_ref, p_ref, coefficients)
        lam_out[0] = lam[0, 0]
        polarise(x, polar_out, weight_out)

    @pl.when(odd_segment())
    def _():
        lam, _ = finish(scalars(refs[:parts], 4), x_ref, p_ref, coefficients)
        lam_out[0] = lam[0, 0]
        weight_out[...] = jnp.zeros_like(weight_out)


def hand_kernel(near, far, out):
    value = jnp.where(odd_segment(), near[...], far[...])
    out[...] = jnp.where(lax.axis_index("seg") > 0, value, jnp.zeros_like(value))


def store_kernel(value, out):
    out[0, 0] = value[...]


def inner_shards(
    left_env, right_env, left_piece, right_piece, guess, inverse_values, precond, sector_rows
):
    left, right, prec = left_env[0, 0], right_env[0, 0], precond[0, 0]
    channels, size = left.shape[0], left.shape[-1]
    matrix = jax.ShapeDtypeStruct((size, size), F32)
    narrow = jax.ShapeDtypeStruct((size, size), BF16)
    stats = jax.ShapeDtypeStruct((ROWS, LANES), F32)
    inner = pltpu.VMEM((size, channels * size), BF16)

    def call(kernel, outs, *operands, scratch=(), in_specs=None, out_specs=None, cost=None, aliases=None):
        return pl.pallas_call(
            kernel,
            out_shape=outs,
            in_specs=in_specs or [VMEM] * len(operands),
            out_specs=out_specs or [VMEM] * len(outs),
            scratch_shapes=list(scratch),
            cost_estimate=cost,
            input_output_aliases=aliases or {},
            compiler_params=pltpu.CompilerParams(vmem_limit_bytes=16 << 20),
        )(*operands)

    (cover,) = call(cover_kernel, [stats], cost=COVER)
    behind = shift(right_piece[0, 0], "seg", -1)
    prec_below = rotate(prec, "sec", 1)
    (mask,) = call(mask_kernel, [matrix], sector_rows, cover)
    scaled = (left_piece[0, 0].astype(F32) * inverse_values[0]).astype(BF16)

    y, yb = call(start_kernel, [matrix, narrow], scaled, behind, guess[0, 0], mask)

    def half(vector_b, pairs, operands, sends):
        outs = [matrix, stats] + [matrix, narrow] * sends
        kernel = functools.partial(lower_kernel, pairs, sends)
        low, stat, *rest = call(kernel, outs, left, right, vector_b, *operands, scratch=[inner])
        if not sends:
            return low, stat
        diag, sent = rest
        return low, stat, diag, rotate(sent, "sec", -1)

    def joined(below, after, diag, above):
        (up,) = call(raise_kernel, [matrix], left, right, below, after, scratch=[inner])
        return call(join_kernel, [matrix, narrow], diag, up, above, mask)

    y_below = rotate(yb, "sec", 1)
    low, stat, diag, above = half(yb, [(0, 0), (0, None)], [y], 1)
    (stat,) = call(cross_kernel, [stats], y_below, low, stat)
    parts = pairwise(stat, "sec")
    g, gb = joined(y_below, stat, diag, above)
    g_below = rotate(gb, "sec", 1)
    kernel = functools.partial(first_kernel, len(parts))
    p, pb = call(kernel, [matrix, narrow], *parts, y, g, prec)

    pairs = [(0, 0), (0, 1), (0, 2), (2, 2), (2, 1), (2, None)]
    low, stat, diag, above = half(pb, pairs, [y, g, p], 1)
    kernel = functools.partial(first_cross_kernel, len(parts))
    stat, p_below = call(kernel, [stats, narrow], *parts, y_below, g_below, prec_below, low, stat)
    parts = pairwise(stat, "sec")
    hp, hpb = joined(p_below, stat, diag, above)
    hp_below = rotate(hpb, "sec", 1)
    kernel = functools.partial(second_kernel, len(parts))
    x, g, p, pb, coefficients = call(
        kernel, [matrix, matrix, matrix, narrow, stats], *parts, y, g, p, hp, prec
    )

    pairs = [(0, 2), (2, 2), (2, 1), (2, None)]
    low, stat = half(pb, pairs, [x, g, p], 0)
    (stat,) = call(
        second_cross_kernel,
        [stats],
        y_below, g_below, p_below, hp_below, prec_below, coefficients, low, stat,
    )
    parts = exchange(stat, "sec")
    block = (1, 1, size, size)
    weight = jax.ShapeDtypeStruct(block, BF16)
    energy = jax.ShapeDtypeStruct((1,), F32)
    operands = (*parts, x, p, coefficients)
    polar, far = call(functools.partial(odd_kernel, len(parts)), [matrix, weight], *operands)
    far = swap(far, "seg", 1)
    polar, near, energy = call(
        functools.partial(even_kernel, len(parts)),
        [matrix, weight, energy],
        *operands, polar,
        out_specs=[VMEM, VMEM, SMEM],
        aliases={len(operands): 0},
    )
    near = swap(near, "seg", 0)
    (handed,) = call(hand_kernel, [weight], near, far)
    (polar,) = call(store_kernel, [jax.ShapeDtypeStruct(block, F32)], polar, cost=SHORT)
    return polar, handed, energy


def solution(mesh):
    placed = (
        P("seg", "sec", None, None, None),
        P("seg", "sec", None, None, None),
        P("seg", "sec", None, None),
        P("seg", "sec", None, None),
        P("seg", "sec", None, None),
        P("seg", "sec", None),
        P("seg", "sec", None, None),
        P("seg", "sec"),
    )
    return jax.shard_map(
        inner_shards,
        mesh=mesh,
        in_specs=placed,
        out_specs=(P("seg", "sec", None, None), P("seg", "sec", None, None), P("seg")),
        check_vma=False,
    )
```

```python
import functools

import jax
import jax.numpy as jnp
from jax import lax
from jax.experimental import pallas as pl
from jax.experimental.pallas import tpu as pltpu
from jax.sharding import PartitionSpec as P


WD = 2
NS_STEPS = 3
ROWS = 8
LANES = 128
F32 = jnp.float32
BF16 = jnp.bfloat16
VMEM = pl.BlockSpec(memory_space=pltpu.VMEM)
SMEM = pl.BlockSpec(memory_space=pltpu.SMEM)
SHORT = pl.CostEstimate(flops=0, bytes_accessed=1 << 20, transcendentals=0)
COVER = pl.CostEstimate(flops=10**10, bytes_accessed=1 << 24, transcendentals=0)


def shift(value, axis, steps):
    count = lax.axis_size(axis)
    first, last = max(0, -steps), min(count, count - steps)
    return lax.ppermute(value, axis, [(source, source + steps) for source in range(first, last)])


def swap(value, axis, first):
    count = lax.axis_size(axis)
    pairs = {i: i for i in range(count)}
    for i in range(first, count - 1, 2):
        pairs[i], pairs[i + 1] = i + 1, i
    return lax.ppermute(value, axis, list(pairs.items()))


def rotate(value, axis, steps):
    count = lax.axis_size(axis)
    return lax.ppermute(value, axis, [(source, (source + steps) % count) for source in range(count)])


def from_below(value):
    return jnp.where(lax.axis_index("sec") > 0, value, jnp.zeros_like(value))


def from_above(value):
    last = lax.axis_size("sec") - 1
    return jnp.where(lax.axis_index("sec") < last, value, jnp.zeros_like(value))


def exchange(value, axis):
    count = lax.axis_size(axis)
    if count & (count - 1):
        return [lax.psum(value, axis)]
    parts, done = [value], 1
    while done < count:
        if len(parts) > 1:
            parts = [total(parts)]
        radix = 4 if count // done >= 4 else 2
        for digit in range(1, radix):
            pairs = [(source, source ^ (digit * done)) for source in range(count)]
            parts.append(lax.ppermute(parts[0], axis, pairs))
        done *= radix
    return parts


def pairwise(value, axis):
    count = lax.axis_size(axis)
    if count & (count - 1) or count == 1:
        return exchange(value, axis)
    stride, parts = 1, [value]
    while stride < count:
        if len(parts) > 1:
            parts = [total(parts)]
        pairs = [(source, source ^ stride) for source in range(count)]
        parts.append(lax.ppermute(parts[0], axis, pairs))
        stride *= 2
    return parts


def total(parts):
    while len(parts) > 1:
        parts = [parts[i] + parts[i + 1] for i in range(0, len(parts), 2)]
    return parts[0]


def fold(product):
    row = jnp.sum(product, axis=0, keepdims=True)
    width = row.shape[-1]
    out = row[:, :LANES]
    for start in range(LANES, width, LANES):
        out = out + row[:, start : start + LANES]
    return out


def scalars(refs, count):
    sums = jnp.sum(total([ref[...] for ref in refs]), axis=1, keepdims=True)
    return [sums[i : i + 1] for i in range(count)]


def sandwich(left, right, value, inner, first, last):
    size = value.shape[-1]
    for w in range(first, last):
        product = jnp.dot(left[w], value, preferred_element_type=F32)
        inner[:, w * size : (w + 1) * size] = product.astype(BF16)
    stacked = right[first:last].reshape((last - first) * size, size)
    return jnp.dot(inner[:, first * size : last * size], stacked, preferred_element_type=F32)


def cover_kernel(out):
    out[...] = jnp.zeros(out.shape, F32)


def mask_kernel(rows, _, mask_out):
    count = rows[...]
    shape = mask_out.shape
    idx_r = lax.broadcasted_iota(jnp.int32, shape, 0)
    idx_c = lax.broadcasted_iota(jnp.int32, shape, 1)
    mask_out[...] = jnp.where((idx_r < count) & (idx_c < count), 1.0, 0.0)


def start_kernel(scaled, behind, guess, mask, y_ref, yb_ref):
    size = mask.shape[-1]
    start = jnp.dot(scaled[...], behind[...], preferred_element_type=F32) + guess[...].astype(F32)
    y = mask[...] * start * (1.0 / (1 << (size - 1).bit_length()))
    y_ref[...] = y
    yb_ref[...] = y.astype(BF16)


def start_lower_kernel(left, right, y, yb, prec, low_ref, stat_ref, diag_ref, sent_ref, py_ref, inner):
    channels = left.shape[0]
    value = yb[...]
    low = sandwich(left, right, value, inner, WD, channels)
    low_ref[...] = low
    sent_ref[...] = low.astype(BF16)
    diag = sandwich(left, right, value, inner, 0, WD)
    diag_ref[...] = diag
    py_ref[...] = (prec[...].astype(F32) * y[...]).astype(BF16)
    write_sums(stat_ref, [(y, y), (y, diag)])


def terms_kernel(left, right, value, low_ref, diag_ref, inner):
    channels = left.shape[0]
    low_ref[...] = sandwich(left, right, value[...], inner, WD, channels)
    diag_ref[...] = sandwich(left, right, value[...], inner, 0, WD)


def write_sums(out, pairs):
    out[...] = jnp.zeros(out.shape, F32)
    for row, (one, two) in enumerate(pairs):
        out[row : row + 1] = fold(one[...] * two[...])


def add_cross(row, below, low, stat, out):
    out[...] = stat[...]
    out[row : row + 1] = stat[row : row + 1] + 2.0 * fold(from_below(below) * low[...])


def cross_kernel(below, low, stat, out):
    add_cross(1, below[...].astype(F32), low, stat, out)


def first_cross_kernel(parts, *refs):
    y, g, prec, low, stat, out, p_out = refs[parts:]
    yy, yhy = scalars(refs[:parts], 2)
    p = prec[...].astype(F32) * (g[...].astype(F32) - (yhy / yy) * y[...].astype(F32))
    p_out[...] = p.astype(BF16)
    add_cross(5, p, low, stat, out)


def second_cross_kernel(y, g, p, hp, prec, coefficients, low, stat, out):
    along_y, along_p, lam = [coefficients[i : i + 1, 0:1] for i in range(3)]
    x = along_y * y[...].astype(F32) + along_p * p[...].astype(F32)
    hx = along_y * g[...].astype(F32) + along_p * hp[...].astype(F32)
    add_cross(3, prec[...].astype(F32) * (hx - lam * x), low, stat, out)


def join_kernel(diag, up, above, mask, prec, out, out_b, weighted_b):
    joined = mask[...] * (diag[...] + up[...] + from_above(above[...].astype(F32)))
    out[...] = joined
    out_b[...] = joined.astype(BF16)
    weighted_b[...] = (prec[...].astype(F32) * joined).astype(BF16)


def raise_kernel(left, right, below, after, up_ref, inner):
    up_ref[...] = from_below(sandwich(left, right, below[...], inner, WD, left.shape[0]))


def first_kernel(parts, *refs):
    y, g, prec, low_g, low_y, diag_g, diag_y = refs[parts : parts + 7]
    p_ref, low_ref, sent_ref, diag_ref, stat_ref, weighted_b, shift_ref = refs[parts + 7 :]
    yy, yhy = scalars(refs[:parts], 2)
    a = yhy / yy
    shift_ref[...] = jnp.broadcast_to(a, shift_ref.shape)
    weights = prec[...].astype(F32)
    low = low_g[...] - a * low_y[...]
    low_ref[...] = low
    sent_ref[...] = low.astype(BF16)
    p = weights * (g[...] - a * y[...])
    p_ref[...] = p
    weighted_b[...] = (weights * p).astype(BF16)
    diag = diag_g[...] - a * diag_y[...]
    diag_ref[...] = diag
    write_sums(stat_ref, [(y, y), (y, g), (y, p), (p, p), (p, g), (p, diag)])


def ritz(a, b, c):
    lam = 0.5 * (a + c) - jnp.sqrt((0.5 * (a - c)) ** 2 + b * b)
    u, w = c - lam, -b
    n = jnp.sqrt(u * u + w * w)
    return lam, u / n, w / n


def second_kernel(parts, *refs):
    y_ref, g_ref, p_ref, hp_ref, prec, shift_ref = refs[parts : parts + 6]
    lows, diags = refs[parts + 6 : parts + 10], refs[parts + 10 : parts + 14]
    x_out, p_out, coefficients, low_ref, stat_ref = refs[parts + 14 :]
    yy, yg, yp, pp, pg, php = scalars(refs[:parts], 6)
    a = yg / yy
    s = yp / yy
    qq = pp - 2.0 * s * yp + s * s * yy
    b = (pg - s * yg) / jnp.sqrt(qq * yy)
    c = (php - 2.0 * s * pg + s * s * yg) / qq
    lam, u, w = ritz(a, b, c)
    along_p = w / jnp.sqrt(qq)
    along_y = u / jnp.sqrt(yy) - along_p * s
    factors = [along_y, along_y * (shift_ref[0:1, 0:1] - lam), along_p, -lam * along_p]
    low_ref[...] = total([factor * term[...] for factor, term in zip(factors, lows)])
    x = along_y * y_ref[...] + along_p * p_ref[...]
    g = along_y * g_ref[...] + along_p * hp_ref[...]
    p = prec[...].astype(F32) * (g - lam * x)
    x_out[...] = x
    p_out[...] = p
    diag = total([factor * term[...] for factor, term in zip(factors, diags)])
    write_sums(stat_ref, [(x, p), (p, p), (p, g), (p, diag)])
    for i, value in enumerate([along_y, along_p, lam]):
        coefficients[i : i + 1] = jnp.broadcast_to(value, (1, LANES))


def dot(one, two, over):
    dims = ((over[:1], over[1:]), ((), ()))
    return lax.dot_general(one, two, dims, preferred_element_type=F32)


def split(value):
    high = value.astype(BF16)
    return high, (value - high.astype(F32)).astype(BF16)


def product(one, two, over):
    (one_high, one_low), (two_high, two_low) = split(one), split(two)
    return dot(one_high, two_high, over) + (
        dot(one_high, two_low, over) + dot(one_low, two_high, over)
    )


def finish(sums, x_ref, p_ref, coefficients):
    xp, pp, pg, php = sums
    a = coefficients[2:3, 0:1]
    qq = pp - xp * xp
    b = (pg - xp * a) / jnp.sqrt(qq)
    c = (php - 2.0 * xp * pg + xp * xp * a) / qq
    lam, u, w = ritz(a, b, c)
    along_p = w / jnp.sqrt(qq)
    along_x = u - along_p * xp
    return lam, along_x * x_ref[...] + along_p * p_ref[...]


def polarise(x, polar_out, weight_out):
    frob = jnp.sum(jnp.sum(x * x, axis=0, keepdims=True), axis=1, keepdims=True)
    polar = x * lax.rsqrt(frob + 1e-06)
    for _ in range(NS_STEPS):
        narrow = polar.astype(BF16)
        gram = dot(narrow, narrow, (1, 1)).astype(BF16)
        polar = 1.5 * polar - 0.5 * dot(gram, narrow, (1, 0))
    polar_out[...] = polar
    weight_out[0, 0] = product(polar, x, (0, 0)).astype(BF16)


def odd_segment():
    return lax.rem(lax.axis_index("seg"), 2) == 1


def odd_kernel(parts, *refs):
    x_ref, p_ref, coefficients, polar_out, weight_out = refs[parts:]

    @pl.when(odd_segment())
    def _():
        _, x = finish(scalars(refs[:parts], 4), x_ref, p_ref, coefficients)
        polarise(x, polar_out, weight_out)

    @pl.when(jnp.logical_not(odd_segment()))
    def _():
        weight_out[...] = jnp.zeros_like(weight_out)


def even_kernel(parts, *refs):
    x_ref, p_ref, coefficients, _, polar_out, weight_out, lam_out = refs[parts:]

    @pl.when(jnp.logical_not(odd_segment()))
    def _():
        lam, x = finish(scalars(refs[:parts], 4), x_ref, p_ref, coefficients)
        lam_out[0] = lam[0, 0]
        polarise(x, polar_out, weight_out)

    @pl.when(odd_segment())
    def _():
        lam, _ = finish(scalars(refs[:parts], 4), x_ref, p_ref, coefficients)
        lam_out[0] = lam[0, 0]
        weight_out[...] = jnp.zeros_like(weight_out)


def hand_kernel(near, far, out):
    value = jnp.where(odd_segment(), near[...], far[...])
    out[...] = jnp.where(lax.axis_index("seg") > 0, value, jnp.zeros_like(value))


def store_kernel(value, out):
    out[0, 0] = value[...]


def inner_shards(
    left_env, right_env, left_piece, right_piece, guess, inverse_values, precond, sector_rows
):
    left, right, prec = left_env[0, 0], right_env[0, 0], precond[0, 0]
    channels, size = left.shape[0], left.shape[-1]
    matrix = jax.ShapeDtypeStruct((size, size), F32)
    narrow = jax.ShapeDtypeStruct((size, size), BF16)
    stats = jax.ShapeDtypeStruct((ROWS, LANES), F32)
    inner = pltpu.VMEM((size, channels * size), BF16)

    def call(kernel, outs, *operands, scratch=(), in_specs=None, out_specs=None, cost=None, aliases=None):
        return pl.pallas_call(
            kernel,
            out_shape=outs,
            in_specs=in_specs or [VMEM] * len(operands),
            out_specs=out_specs or [VMEM] * len(outs),
            scratch_shapes=list(scratch),
            cost_estimate=cost,
            input_output_aliases=aliases or {},
            compiler_params=pltpu.CompilerParams(vmem_limit_bytes=16 << 20),
        )(*operands)

    (cover,) = call(cover_kernel, [stats], cost=COVER)
    behind = shift(right_piece[0, 0], "seg", -1)
    prec_below = rotate(prec, "sec", 1)
    (mask,) = call(mask_kernel, [matrix], sector_rows, cover)
    scaled = (left_piece[0, 0].astype(F32) * inverse_values[0]).astype(BF16)

    y, yb = call(start_kernel, [matrix, narrow], scaled, behind, guess[0, 0], mask)

    def terms(value):
        return call(terms_kernel, [matrix, matrix], left, right, value, scratch=[inner])

    def joined(below, after, diag, above):
        (up,) = call(raise_kernel, [matrix], left, right, below, after, scratch=[inner])
        outs = [matrix, narrow, narrow]
        return call(join_kernel, outs, diag, up, above, mask, prec)

    y_below = rotate(yb, "sec", 1)
    low, stat, diag, sent, pyb = call(
        start_lower_kernel,
        [matrix, stats, matrix, narrow, narrow],
        left, right, y, yb, prec,
        scratch=[inner],
    )
    above = rotate(sent, "sec", -1)
    low_y, diag_y = terms(pyb)
    (stat,) = call(cross_kernel, [stats], y_below, low, stat)
    parts = pairwise(stat, "sec")
    g, gb, pgb = joined(y_below, stat, diag, above)
    g_below = rotate(gb, "sec", 1)
    low_g, diag_g = terms(pgb)
    p, low, sent, diag, stat, ppb, shifted = call(
        functools.partial(first_kernel, len(parts)),
        [matrix, matrix, narrow, matrix, stats, narrow, stats],
        *parts, y, g, prec, low_g, low_y, diag_g, diag_y,
    )
    above = rotate(sent, "sec", -1)
    stat, p_below = call(
        functools.partial(first_cross_kernel, len(parts)),
        [stats, narrow],
        *parts, y_below, g_below, prec_below, low, stat,
    )
    parts = pairwise(stat, "sec")
    hp, hpb, phpb = joined(p_below, stat, diag, above)
    low_p, diag_p = terms(ppb)
    hp_below = rotate(hpb, "sec", 1)
    low_hp, diag_hp = terms(phpb)
    x, p, coefficients, low, stat = call(
        functools.partial(second_kernel, len(parts)),
        [matrix, matrix, stats, matrix, stats],
        *parts, y, g, p, hp, prec, shifted,
        low, low_y, low_hp, low_p, diag, diag_y, diag_hp, diag_p,
    )
    (stat,) = call(
        second_cross_kernel,
        [stats],
        y_below, g_below, p_below, hp_below, prec_below, coefficients, low, stat,
    )
    parts = exchange(stat, "sec")
    block = (1, 1, size, size)
    weight = jax.ShapeDtypeStruct(block, BF16)
    energy = jax.ShapeDtypeStruct((1,), F32)
    operands = (*parts, x, p, coefficients)
    polar, far = call(functools.partial(odd_kernel, len(parts)), [matrix, weight], *operands)
    far = swap(far, "seg", 1)
    polar, near, energy = call(
        functools.partial(even_kernel, len(parts)),
        [matrix, weight, energy],
        *operands, polar,
        out_specs=[VMEM, VMEM, SMEM],
        aliases={len(operands): 0},
    )
    near = swap(near, "seg", 0)
    (handed,) = call(hand_kernel, [weight], near, far)
    (polar,) = call(store_kernel, [jax.ShapeDtypeStruct(block, F32)], polar, cost=SHORT)
    return polar, handed, energy


def solution(mesh):
    placed = (
        P("seg", "sec", None, None, None),
        P("seg", "sec", None, None, None),
        P("seg", "sec", None, None),
        P("seg", "sec", None, None),
        P("seg", "sec", None, None),
        P("seg", "sec", None),
        P("seg", "sec", None, None),
        P("seg", "sec"),
    )
    return jax.shard_map(
        inner_shards,
        mesh=mesh,
        in_specs=placed,
        out_specs=(P("seg", "sec", None, None), P("seg", "sec", None, None), P("seg")),
        check_vma=False,
    )
```

```python
import functools

import jax
import jax.numpy as jnp
from jax import lax
from jax.experimental import pallas as pl
from jax.experimental.pallas import tpu as pltpu
from jax.sharding import PartitionSpec as P


WD = 2
NS_STEPS = 3
ROWS = 8
LANES = 128
F32 = jnp.float32
BF16 = jnp.bfloat16
VMEM = pl.BlockSpec(memory_space=pltpu.VMEM)
SMEM = pl.BlockSpec(memory_space=pltpu.SMEM)
SHORT = pl.CostEstimate(flops=0, bytes_accessed=1 << 20, transcendentals=0)
COVER = pl.CostEstimate(flops=10**10, bytes_accessed=1 << 24, transcendentals=0)


def swap(value, axis, first, other):
    count, across = lax.axis_size(axis), lax.axis_size(other)
    partner = {}
    for i in range(first, count - 1, 2):
        partner[i], partner[i + 1] = i + 1, i
    pairs = []
    for i in range(count):
        for j in range(across):
            beside = min(j ^ 1, across - 1) if across % 2 == 0 else j
            target = (partner[i], j) if i in partner else (i, beside)
            pairs.append((i * across + j, target[0] * across + target[1]))
    return lax.ppermute(value, (axis, other), pairs)


def rotate(value, axis, steps):
    count = lax.axis_size(axis)
    return lax.ppermute(value, axis, [(source, (source + steps) % count) for source in range(count)])


def from_below(value):
    return jnp.where(lax.axis_index("sec") > 0, value, jnp.zeros_like(value))


def from_above(value):
    last = lax.axis_size("sec") - 1
    return jnp.where(lax.axis_index("sec") < last, value, jnp.zeros_like(value))


def exchange(value, axis):
    count = lax.axis_size(axis)
    if count & (count - 1):
        return [lax.psum(value, axis)]
    parts, done = [value], 1
    while done < count:
        if len(parts) > 1:
            parts = [total(parts)]
        radix = 4 if count // done >= 4 else 2
        for digit in range(1, radix):
            pairs = [(source, source ^ (digit * done)) for source in range(count)]
            parts.append(lax.ppermute(parts[0], axis, pairs))
        done *= radix
    return parts


def pairwise(value, axis):
    count = lax.axis_size(axis)
    if count & (count - 1) or count == 1:
        return exchange(value, axis)
    stride, parts = 1, [value]
    while stride < count:
        if len(parts) > 1:
            parts = [total(parts)]
        pairs = [(source, source ^ stride) for source in range(count)]
        parts.append(lax.ppermute(parts[0], axis, pairs))
        stride *= 2
    return parts


def total(parts):
    while len(parts) > 1:
        parts = [parts[i] + parts[i + 1] for i in range(0, len(parts), 2)]
    return parts[0]


def fold(product):
    row = jnp.sum(product, axis=0, keepdims=True)
    width = row.shape[-1]
    out = row[:, :LANES]
    for start in range(LANES, width, LANES):
        out = out + row[:, start : start + LANES]
    return out


def scalars(refs, count):
    sums = jnp.sum(total([ref[...] for ref in refs]), axis=1, keepdims=True)
    return [sums[i : i + 1] for i in range(count)]


def sandwich(left, right, value, inner, first, last):
    size = value.shape[-1]
    for w in range(first, last):
        product = jnp.dot(left[w], value, preferred_element_type=F32)
        inner[:, w * size : (w + 1) * size] = product.astype(BF16)
    stacked = right[first:last].reshape((last - first) * size, size)
    return jnp.dot(inner[:, first * size : last * size], stacked, preferred_element_type=F32)


def cover_kernel(out):
    out[...] = jnp.zeros(out.shape, F32)


def mask_kernel(rows, _, mask_out):
    count = rows[...]
    shape = mask_out.shape
    idx_r = lax.broadcasted_iota(jnp.int32, shape, 0)
    idx_c = lax.broadcasted_iota(jnp.int32, shape, 1)
    mask_out[...] = jnp.where((idx_r < count) & (idx_c < count), 1.0, 0.0)


def start_kernel(scaled, behind, guess, mask, y_ref, yb_ref):
    size = mask.shape[-1]
    inside = lax.axis_index("seg") < lax.axis_size("seg") - 1
    right = jnp.where(inside, behind[...], jnp.zeros_like(behind))
    start = jnp.dot(scaled[...], right, preferred_element_type=F32) + guess[...].astype(F32)
    y = mask[...] * start * (1.0 / (1 << (size - 1).bit_length()))
    y_ref[...] = y
    yb_ref[...] = y.astype(BF16)


def start_lower_kernel(left, right, yb, low_ref, sent_ref, inner):
    low = sandwich(left, right, yb[...], inner, WD, left.shape[0])
    low_ref[...] = low
    sent_ref[...] = low.astype(BF16)


def start_terms_kernel(left, right, y, yb, prec, stat_ref, diag_ref, low_ref, diag_py_ref, inner):
    channels = left.shape[0]
    diag = sandwich(left, right, yb[...], inner, 0, WD)
    diag_ref[...] = diag
    write_sums(stat_ref, [(y, y), (y, diag)])
    weighted = (prec[...].astype(F32) * y[...]).astype(BF16)
    low_ref[...] = sandwich(left, right, weighted, inner, WD, channels)
    diag_py_ref[...] = sandwich(left, right, weighted, inner, 0, WD)


def terms_kernel(left, right, value, low_ref, diag_ref, inner):
    channels = left.shape[0]
    low_ref[...] = sandwich(left, right, value[...], inner, WD, channels)
    diag_ref[...] = sandwich(left, right, value[...], inner, 0, WD)


def write_sums(out, pairs):
    out[...] = jnp.zeros(out.shape, F32)
    for row, (one, two) in enumerate(pairs):
        out[row : row + 1] = fold(one[...] * two[...])


def add_cross(row, below, low, stat, out):
    out[...] = stat[...]
    out[row : row + 1] = stat[row : row + 1] + 2.0 * fold(from_below(below) * low[...])


def cross_kernel(below, low, stat, out):
    add_cross(1, below[...].astype(F32), low, stat, out)


def first_cross_kernel(parts, *refs):
    y, g, prec, low, stat, out, p_out = refs[parts:]
    yy, yhy = scalars(refs[:parts], 2)
    p = prec[...].astype(F32) * (g[...].astype(F32) - (yhy / yy) * y[...].astype(F32))
    p_out[...] = p.astype(BF16)
    add_cross(5, p, low, stat, out)


def second_cross_kernel(y, g, p, hp, prec, coefficients, low, stat, out):
    along_y, along_p, lam = [coefficients[i : i + 1, 0:1] for i in range(3)]
    x = along_y * y[...].astype(F32) + along_p * p[...].astype(F32)
    hx = along_y * g[...].astype(F32) + along_p * hp[...].astype(F32)
    add_cross(3, prec[...].astype(F32) * (hx - lam * x), low, stat, out)


def join_kernel(diag, up, above, mask, prec, out, out_b, weighted_b):
    joined = mask[...] * (diag[...] + up[...] + from_above(above[...].astype(F32)))
    out[...] = joined
    out_b[...] = joined.astype(BF16)
    weighted_b[...] = (prec[...].astype(F32) * joined).astype(BF16)


def raise_kernel(left, right, below, after, up_ref, inner):
    up_ref[...] = from_below(sandwich(left, right, below[...], inner, WD, left.shape[0]))


def first_low_kernel(parts, *refs):
    low_g, low_y, low_ref, sent_ref = refs[parts:]
    yy, yhy = scalars(refs[:parts], 2)
    low = low_g[...] - (yhy / yy) * low_y[...]
    low_ref[...] = low
    sent_ref[...] = low.astype(BF16)


def first_kernel(parts, *refs):
    y, g, prec, diag_g, diag_y = refs[parts : parts + 5]
    p_ref, diag_ref, stat_ref, weighted_b, shift_ref = refs[parts + 5 :]
    yy, yhy = scalars(refs[:parts], 2)
    a = yhy / yy
    shift_ref[...] = jnp.broadcast_to(a, shift_ref.shape)
    weights = prec[...].astype(F32)
    p = weights * (g[...] - a * y[...])
    p_ref[...] = p
    weighted_b[...] = (weights * p).astype(BF16)
    diag = diag_g[...] - a * diag_y[...]
    diag_ref[...] = diag
    write_sums(stat_ref, [(y, y), (y, g), (y, p), (p, p), (p, g), (p, diag)])


def ritz(a, b, c):
    lam = 0.5 * (a + c) - jnp.sqrt((0.5 * (a - c)) ** 2 + b * b)
    u, w = c - lam, -b
    n = jnp.sqrt(u * u + w * w)
    return lam, u / n, w / n


def second_kernel(parts, *refs):
    y_ref, g_ref, p_ref, hp_ref, prec, shift_ref = refs[parts : parts + 6]
    lows, diags = refs[parts + 6 : parts + 10], refs[parts + 10 : parts + 14]
    x_out, p_out, coefficients, low_ref, stat_ref = refs[parts + 14 :]
    yy, yg, yp, pp, pg, php = scalars(refs[:parts], 6)
    a = yg / yy
    s = yp / yy
    qq = pp - 2.0 * s * yp + s * s * yy
    b = (pg - s * yg) / jnp.sqrt(qq * yy)
    c = (php - 2.0 * s * pg + s * s * yg) / qq
    lam, u, w = ritz(a, b, c)
    along_p = w / jnp.sqrt(qq)
    along_y = u / jnp.sqrt(yy) - along_p * s
    factors = [along_y, along_y * (shift_ref[0:1, 0:1] - lam), along_p, -lam * along_p]
    low_ref[...] = total([factor * term[...] for factor, term in zip(factors, lows)])
    x = along_y * y_ref[...] + along_p * p_ref[...]
    g = along_y * g_ref[...] + along_p * hp_ref[...]
    p = prec[...].astype(F32) * (g - lam * x)
    x_out[...] = x
    p_out[...] = p
    diag = total([factor * term[...] for factor, term in zip(factors, diags)])
    write_sums(stat_ref, [(x, p), (p, p), (p, g), (p, diag)])
    for i, value in enumerate([along_y, along_p, lam]):
        coefficients[i : i + 1] = jnp.broadcast_to(value, (1, LANES))


def dot(one, two, over):
    dims = ((over[:1], over[1:]), ((), ()))
    return lax.dot_general(one, two, dims, preferred_element_type=F32)


def split(value):
    high = value.astype(BF16)
    return high, (value - high.astype(F32)).astype(BF16)


def product(one, two, over):
    (one_high, one_low), (two_high, two_low) = split(one), split(two)
    return dot(one_high, two_high, over) + (
        dot(one_high, two_low, over) + dot(one_low, two_high, over)
    )


def finish(sums, x_ref, p_ref, coefficients):
    xp, pp, pg, php = sums
    a = coefficients[2:3, 0:1]
    qq = pp - xp * xp
    b = (pg - xp * a) / jnp.sqrt(qq)
    c = (php - 2.0 * xp * pg + xp * xp * a) / qq
    lam, u, w = ritz(a, b, c)
    along_p = w / jnp.sqrt(qq)
    along_x = u - along_p * xp
    return lam, along_x * x_ref[...] + along_p * p_ref[...]


def polarise(x, polar_out, weight_out):
    frob = jnp.sum(jnp.sum(x * x, axis=0, keepdims=True), axis=1, keepdims=True)
    polar = x * lax.rsqrt(frob + 1e-06)
    for _ in range(NS_STEPS):
        narrow = polar.astype(BF16)
        gram = dot(narrow, narrow, (1, 1)).astype(BF16)
        polar = 1.5 * polar - 0.5 * dot(gram, narrow, (1, 0))
    polar_out[...] = polar
    weight_out[0, 0] = product(polar, x, (0, 0)).astype(BF16)


def odd_segment():
    return lax.rem(lax.axis_index("seg"), 2) == 1


def odd_kernel(parts, *refs):
    x_ref, p_ref, coefficients, polar_out, weight_out = refs[parts:]

    @pl.when(odd_segment())
    def _():
        _, x = finish(scalars(refs[:parts], 4), x_ref, p_ref, coefficients)
        polarise(x, polar_out, weight_out)

    @pl.when(jnp.logical_not(odd_segment()))
    def _():
        weight_out[...] = jnp.zeros_like(weight_out)


def even_kernel(parts, *refs):
    x_ref, p_ref, coefficients, _, polar_out, weight_out, lam_out = refs[parts:]

    @pl.when(jnp.logical_not(odd_segment()))
    def _():
        lam, x = finish(scalars(refs[:parts], 4), x_ref, p_ref, coefficients)
        lam_out[0] = lam[0, 0]
        polarise(x, polar_out, weight_out)

    @pl.when(odd_segment())
    def _():
        lam, _ = finish(scalars(refs[:parts], 4), x_ref, p_ref, coefficients)
        lam_out[0] = lam[0, 0]
        weight_out[...] = jnp.zeros_like(weight_out)


def hand_kernel(near, far, out):
    value = jnp.where(odd_segment(), near[...], far[...])
    out[...] = jnp.where(lax.axis_index("seg") > 0, value, jnp.zeros_like(value))


def store_kernel(value, out):
    out[0, 0] = value[...]


def inner_shards(
    left_env, right_env, left_piece, right_piece, guess, inverse_values, precond, sector_rows
):
    left, right, prec = left_env[0, 0], right_env[0, 0], precond[0, 0]
    channels, size = left.shape[0], left.shape[-1]
    matrix = jax.ShapeDtypeStruct((size, size), F32)
    narrow = jax.ShapeDtypeStruct((size, size), BF16)
    stats = jax.ShapeDtypeStruct((ROWS, LANES), F32)
    inner = pltpu.VMEM((size, channels * size), BF16)

    def call(kernel, outs, *operands, scratch=(), in_specs=None, out_specs=None, cost=None, aliases=None):
        return pl.pallas_call(
            kernel,
            out_shape=outs,
            in_specs=in_specs or [VMEM] * len(operands),
            out_specs=out_specs or [VMEM] * len(outs),
            scratch_shapes=list(scratch),
            cost_estimate=cost,
            input_output_aliases=aliases or {},
            compiler_params=pltpu.CompilerParams(vmem_limit_bytes=16 << 20),
        )(*operands)

    (cover,) = call(cover_kernel, [stats], cost=COVER)
    behind = rotate(right_piece[0, 0], "seg", -1)
    prec_below = rotate(prec, "sec", 1)
    (mask,) = call(mask_kernel, [matrix], sector_rows, cover)
    scaled = (left_piece[0, 0].astype(F32) * inverse_values[0]).astype(BF16)

    y, yb = call(start_kernel, [matrix, narrow], scaled, behind, guess[0, 0], mask)

    def terms(value):
        return call(terms_kernel, [matrix, matrix], left, right, value, scratch=[inner])

    def joined(below, after, diag, above):
        (up,) = call(raise_kernel, [matrix], left, right, below, after, scratch=[inner])
        outs = [matrix, narrow, narrow]
        return call(join_kernel, outs, diag, up, above, mask, prec)

    y_below = rotate(yb, "sec", 1)
    low, sent = call(start_lower_kernel, [matrix, narrow], left, right, yb, scratch=[inner])
    above = rotate(sent, "sec", -1)
    stat, diag, low_y, diag_y = call(
        start_terms_kernel,
        [stats, matrix, matrix, matrix],
        left, right, y, yb, prec,
        scratch=[inner],
    )
    (stat,) = call(cross_kernel, [stats], y_below, low, stat)
    parts = pairwise(stat, "sec")
    g, gb, pgb = joined(y_below, stat, diag, above)
    g_below = rotate(gb, "sec", 1)
    low_g, diag_g = terms(pgb)
    low, sent = call(
        functools.partial(first_low_kernel, len(parts)),
        [matrix, narrow],
        *parts, low_g, low_y,
    )
    above = rotate(sent, "sec", -1)
    p, diag, stat, ppb, shifted = call(
        functools.partial(first_kernel, len(parts)),
        [matrix, matrix, stats, narrow, stats],
        *parts, y, g, prec, diag_g, diag_y,
    )
    stat, p_below = call(
        functools.partial(first_cross_kernel, len(parts)),
        [stats, narrow],
        *parts, y_below, g_below, prec_below, low, stat,
    )
    parts = pairwise(stat, "sec")
    hp, hpb, phpb = joined(p_below, stat, diag, above)
    low_p, diag_p = terms(ppb)
    hp_below = rotate(hpb, "sec", 1)
    low_hp, diag_hp = terms(phpb)
    x, p, coefficients, low, stat = call(
        functools.partial(second_kernel, len(parts)),
        [matrix, matrix, stats, matrix, stats],
        *parts, y, g, p, hp, prec, shifted,
        low, low_y, low_hp, low_p, diag, diag_y, diag_hp, diag_p,
    )
    (stat,) = call(
        second_cross_kernel,
        [stats],
        y_below, g_below, p_below, hp_below, prec_below, coefficients, low, stat,
    )
    parts = exchange(stat, "sec")
    block = (1, 1, size, size)
    weight = jax.ShapeDtypeStruct(block, BF16)
    energy = jax.ShapeDtypeStruct((1,), F32)
    operands = (*parts, x, p, coefficients)
    polar, far = call(functools.partial(odd_kernel, len(parts)), [matrix, weight], *operands)
    far = swap(far, "seg", 1, "sec")
    polar, near, energy = call(
        functools.partial(even_kernel, len(parts)),
        [matrix, weight, energy],
        *operands, polar,
        out_specs=[VMEM, VMEM, SMEM],
        aliases={len(operands): 0},
    )
    near = swap(near, "seg", 0, "sec")
    (handed,) = call(hand_kernel, [weight], near, far)
    (polar,) = call(store_kernel, [jax.ShapeDtypeStruct(block, F32)], polar, cost=SHORT)
    return polar, handed, energy


def solution(mesh):
    placed = (
        P("seg", "sec", None, None, None),
        P("seg", "sec", None, None, None),
        P("seg", "sec", None, None),
        P("seg", "sec", None, None),
        P("seg", "sec", None, None),
        P("seg", "sec", None),
        P("seg", "sec", None, None),
        P("seg", "sec"),
    )
    return jax.shard_map(
        inner_shards,
        mesh=mesh,
        in_specs=placed,
        out_specs=(P("seg", "sec", None, None), P("seg", "sec", None, None), P("seg")),
        check_vma=False,
    )
```

```python
import functools

import jax
import jax.numpy as jnp
from jax import lax
from jax.experimental import pallas as pl
from jax.experimental.pallas import tpu as pltpu
from jax.sharding import PartitionSpec as P


WD = 2
NS_STEPS = 3
ROWS = 8
LANES = 128
F32 = jnp.float32
BF16 = jnp.bfloat16
VMEM = pl.BlockSpec(memory_space=pltpu.VMEM)
SMEM = pl.BlockSpec(memory_space=pltpu.SMEM)
SHORT = pl.CostEstimate(flops=0, bytes_accessed=1 << 20, transcendentals=0)
COVER = pl.CostEstimate(flops=10**10, bytes_accessed=1 << 24, transcendentals=0)


def swap(value, axis, first, other):
    count, across = lax.axis_size(axis), lax.axis_size(other)
    partner = {}
    for i in range(first, count - 1, 2):
        partner[i], partner[i + 1] = i + 1, i
    pairs = []
    for i in range(count):
        for j in range(across):
            beside = min(j ^ 1, across - 1) if across % 2 == 0 else j
            target = (partner[i], j) if i in partner else (i, beside)
            pairs.append((i * across + j, target[0] * across + target[1]))
    return lax.ppermute(value, (axis, other), pairs)


def rotate(value, axis, steps):
    count = lax.axis_size(axis)
    return lax.ppermute(value, axis, [(source, (source + steps) % count) for source in range(count)])


def from_below(value):
    return jnp.where(lax.axis_index("sec") > 0, value, jnp.zeros_like(value))


def from_above(value):
    last = lax.axis_size("sec") - 1
    return jnp.where(lax.axis_index("sec") < last, value, jnp.zeros_like(value))


def exchange(value, axis):
    count = lax.axis_size(axis)
    if count & (count - 1):
        return [lax.psum(value, axis)]
    parts, done = [value], 1
    while done < count:
        if len(parts) > 1:
            parts = [total(parts)]
        radix = 4 if count // done >= 4 else 2
        for digit in range(1, radix):
            pairs = [(source, source ^ (digit * done)) for source in range(count)]
            parts.append(lax.ppermute(parts[0], axis, pairs))
        done *= radix
    return parts


def pairwise(value, axis):
    count = lax.axis_size(axis)
    if count & (count - 1) or count == 1:
        return exchange(value, axis)
    stride, parts = 1, [value]
    while stride < count:
        if len(parts) > 1:
            parts = [total(parts)]
        pairs = [(source, source ^ stride) for source in range(count)]
        parts.append(lax.ppermute(parts[0], axis, pairs))
        stride *= 2
    return parts


def total(parts):
    while len(parts) > 1:
        parts = [parts[i] + parts[i + 1] for i in range(0, len(parts), 2)]
    return parts[0]


def fold(product):
    row = jnp.sum(product, axis=0, keepdims=True)
    width = row.shape[-1]
    out = row[:, :LANES]
    for start in range(LANES, width, LANES):
        out = out + row[:, start : start + LANES]
    return out


def scalars(refs, count):
    sums = jnp.sum(total([ref[...] for ref in refs]), axis=1, keepdims=True)
    return [sums[i : i + 1] for i in range(count)]


def sandwich(left, right, value, inner, first, last):
    size = value.shape[-1]
    for w in range(first, last):
        product = jnp.dot(left[w], value, preferred_element_type=F32)
        inner[:, w * size : (w + 1) * size] = product.astype(BF16)
    stacked = right[first:last].reshape((last - first) * size, size)
    return jnp.dot(inner[:, first * size : last * size], stacked, preferred_element_type=F32)


def cover_kernel(out):
    out[...] = jnp.zeros(out.shape, F32)


def mask_kernel(rows, _, mask_out):
    count = rows[...]
    shape = mask_out.shape
    idx_r = lax.broadcasted_iota(jnp.int32, shape, 0)
    idx_c = lax.broadcasted_iota(jnp.int32, shape, 1)
    mask_out[...] = jnp.where((idx_r < count) & (idx_c < count), 1.0, 0.0)


def start_kernel(scaled, near, far, guess, mask, y_ref, yb_ref):
    size = mask.shape[-1]
    inside = lax.axis_index("seg") < lax.axis_size("seg") - 1
    behind = jnp.where(odd_segment(), far[...], near[...])
    right = jnp.where(inside, behind, jnp.zeros_like(behind))
    start = jnp.dot(scaled[...], right, preferred_element_type=F32) + guess[...].astype(F32)
    y = mask[...] * start * (1.0 / (1 << (size - 1).bit_length()))
    y_ref[...] = y
    yb_ref[...] = y.astype(BF16)


def start_lower_kernel(left, right, yb, low_ref, sent_ref, inner):
    low = sandwich(left, right, yb[...], inner, WD, left.shape[0])
    low_ref[...] = low
    sent_ref[...] = low.astype(BF16)


def start_terms_kernel(left, right, y, yb, prec, stat_ref, diag_ref, low_ref, diag_py_ref, inner):
    channels = left.shape[0]
    diag = sandwich(left, right, yb[...], inner, 0, WD)
    diag_ref[...] = diag
    write_sums(stat_ref, [(y, y), (y, diag)])
    weighted = (prec[...].astype(F32) * y[...]).astype(BF16)
    low_ref[...] = sandwich(left, right, weighted, inner, WD, channels)
    diag_py_ref[...] = sandwich(left, right, weighted, inner, 0, WD)


def terms_kernel(left, right, value, low_ref, diag_ref, inner):
    channels = left.shape[0]
    low_ref[...] = sandwich(left, right, value[...], inner, WD, channels)
    diag_ref[...] = sandwich(left, right, value[...], inner, 0, WD)


def write_sums(out, pairs):
    out[...] = jnp.zeros(out.shape, F32)
    for row, (one, two) in enumerate(pairs):
        out[row : row + 1] = fold(one[...] * two[...])


def add_cross(row, below, low, stat, out):
    out[...] = stat[...]
    out[row : row + 1] = stat[row : row + 1] + 2.0 * fold(from_below(below) * low[...])


def cross_kernel(below, low, stat, out):
    add_cross(1, below[...].astype(F32), low, stat, out)


def first_cross_kernel(parts, *refs):
    y, g, prec, low, stat, out, p_out = refs[parts:]
    yy, yhy = scalars(refs[:parts], 2)
    p = prec[...].astype(F32) * (g[...].astype(F32) - (yhy / yy) * y[...].astype(F32))
    p_out[...] = p.astype(BF16)
    add_cross(5, p, low, stat, out)


def second_cross_kernel(y, g, p, hp, prec, coefficients, low, stat, out):
    along_y, along_p, lam = [coefficients[i : i + 1, 0:1] for i in range(3)]
    x = along_y * y[...].astype(F32) + along_p * p[...].astype(F32)
    hx = along_y * g[...].astype(F32) + along_p * hp[...].astype(F32)
    add_cross(3, prec[...].astype(F32) * (hx - lam * x), low, stat, out)


def join_kernel(diag, up, above, mask, prec, out, out_b, weighted_b):
    joined = mask[...] * (diag[...] + up[...] + from_above(above[...].astype(F32)))
    out[...] = joined
    out_b[...] = joined.astype(BF16)
    weighted_b[...] = (prec[...].astype(F32) * joined).astype(BF16)


def raise_kernel(left, right, below, after, up_ref, inner):
    up_ref[...] = from_below(sandwich(left, right, below[...], inner, WD, left.shape[0]))


def first_low_kernel(parts, *refs):
    low_g, low_y, low_ref, sent_ref = refs[parts:]
    yy, yhy = scalars(refs[:parts], 2)
    low = low_g[...] - (yhy / yy) * low_y[...]
    low_ref[...] = low
    sent_ref[...] = low.astype(BF16)


def first_kernel(parts, *refs):
    y, g, prec, diag_g, diag_y = refs[parts : parts + 5]
    p_ref, diag_ref, stat_ref, weighted_b, shift_ref = refs[parts + 5 :]
    yy, yhy = scalars(refs[:parts], 2)
    a = yhy / yy
    shift_ref[...] = jnp.broadcast_to(a, shift_ref.shape)
    weights = prec[...].astype(F32)
    p = weights * (g[...] - a * y[...])
    p_ref[...] = p
    weighted_b[...] = (weights * p).astype(BF16)
    diag = diag_g[...] - a * diag_y[...]
    diag_ref[...] = diag
    write_sums(stat_ref, [(y, y), (y, g), (y, p), (p, p), (p, g), (p, diag)])


def ritz(a, b, c):
    lam = 0.5 * (a + c) - jnp.sqrt((0.5 * (a - c)) ** 2 + b * b)
    u, w = c - lam, -b
    n = jnp.sqrt(u * u + w * w)
    return lam, u / n, w / n


def second_kernel(parts, *refs):
    y_ref, g_ref, p_ref, hp_ref, prec, shift_ref = refs[parts : parts + 6]
    lows, diags = refs[parts + 6 : parts + 10], refs[parts + 10 : parts + 14]
    x_out, p_out, coefficients, low_ref, stat_ref = refs[parts + 14 :]
    yy, yg, yp, pp, pg, php = scalars(refs[:parts], 6)
    a = yg / yy
    s = yp / yy
    qq = pp - 2.0 * s * yp + s * s * yy
    b = (pg - s * yg) / jnp.sqrt(qq * yy)
    c = (php - 2.0 * s * pg + s * s * yg) / qq
    lam, u, w = ritz(a, b, c)
    along_p = w / jnp.sqrt(qq)
    along_y = u / jnp.sqrt(yy) - along_p * s
    factors = [along_y, along_y * (shift_ref[0:1, 0:1] - lam), along_p, -lam * along_p]
    low_ref[...] = total([factor * term[...] for factor, term in zip(factors, lows)])
    x = along_y * y_ref[...] + along_p * p_ref[...]
    g = along_y * g_ref[...] + along_p * hp_ref[...]
    p = prec[...].astype(F32) * (g - lam * x)
    x_out[...] = x
    p_out[...] = p
    diag = total([factor * term[...] for factor, term in zip(factors, diags)])
    write_sums(stat_ref, [(x, p), (p, p), (p, g), (p, diag)])
    for i, value in enumerate([along_y, along_p, lam]):
        coefficients[i : i + 1] = jnp.broadcast_to(value, (1, LANES))


def dot(one, two, over):
    dims = ((over[:1], over[1:]), ((), ()))
    return lax.dot_general(one, two, dims, preferred_element_type=F32)


def split(value):
    high = value.astype(BF16)
    return high, (value - high.astype(F32)).astype(BF16)


def product(one, two, over):
    (one_high, one_low), (two_high, two_low) = split(one), split(two)
    return dot(one_high, two_high, over) + (
        dot(one_high, two_low, over) + dot(one_low, two_high, over)
    )


def finish(sums, x_ref, p_ref, coefficients):
    xp, pp, pg, php = sums
    a = coefficients[2:3, 0:1]
    qq = pp - xp * xp
    b = (pg - xp * a) / jnp.sqrt(qq)
    c = (php - 2.0 * xp * pg + xp * xp * a) / qq
    lam, u, w = ritz(a, b, c)
    along_p = w / jnp.sqrt(qq)
    along_x = u - along_p * xp
    return lam, along_x * x_ref[...] + along_p * p_ref[...]


def polarise(x, polar_out, weight_out):
    frob = jnp.sum(jnp.sum(x * x, axis=0, keepdims=True), axis=1, keepdims=True)
    polar = x * lax.rsqrt(frob + 1e-06)
    for _ in range(NS_STEPS):
        narrow = polar.astype(BF16)
        gram = dot(narrow, narrow, (1, 1)).astype(BF16)
        polar = 1.5 * polar - 0.5 * dot(gram, narrow, (1, 0))
    polar_out[...] = polar
    weight_out[0, 0] = product(polar, x, (0, 0)).astype(BF16)


def odd_segment():
    return lax.rem(lax.axis_index("seg"), 2) == 1


def odd_kernel(parts, *refs):
    x_ref, p_ref, coefficients, polar_out, weight_out = refs[parts:]

    @pl.when(odd_segment())
    def _():
        _, x = finish(scalars(refs[:parts], 4), x_ref, p_ref, coefficients)
        polarise(x, polar_out, weight_out)

    @pl.when(jnp.logical_not(odd_segment()))
    def _():
        weight_out[...] = jnp.zeros_like(weight_out)


def even_kernel(parts, *refs):
    x_ref, p_ref, coefficients, _, polar_out, weight_out, lam_out = refs[parts:]

    @pl.when(jnp.logical_not(odd_segment()))
    def _():
        lam, x = finish(scalars(refs[:parts], 4), x_ref, p_ref, coefficients)
        lam_out[0] = lam[0, 0]
        polarise(x, polar_out, weight_out)

    @pl.when(odd_segment())
    def _():
        lam, _ = finish(scalars(refs[:parts], 4), x_ref, p_ref, coefficients)
        lam_out[0] = lam[0, 0]
        weight_out[...] = jnp.zeros_like(weight_out)


def hand_kernel(near, far, out):
    value = jnp.where(odd_segment(), near[...], far[...])
    out[...] = jnp.where(lax.axis_index("seg") > 0, value, jnp.zeros_like(value))


def store_kernel(value, out):
    out[0, 0] = value[...]


def inner_shards(
    left_env, right_env, left_piece, right_piece, guess, inverse_values, precond, sector_rows
):
    left, right, prec = left_env[0, 0], right_env[0, 0], precond[0, 0]
    channels, size = left.shape[0], left.shape[-1]
    matrix = jax.ShapeDtypeStruct((size, size), F32)
    narrow = jax.ShapeDtypeStruct((size, size), BF16)
    stats = jax.ShapeDtypeStruct((ROWS, LANES), F32)
    inner = pltpu.VMEM((size, channels * size), BF16)

    def call(kernel, outs, *operands, scratch=(), in_specs=None, out_specs=None, cost=None, aliases=None):
        return pl.pallas_call(
            kernel,
            out_shape=outs,
            in_specs=in_specs or [VMEM] * len(operands),
            out_specs=out_specs or [VMEM] * len(outs),
            scratch_shapes=list(scratch),
            cost_estimate=cost,
            input_output_aliases=aliases or {},
            compiler_params=pltpu.CompilerParams(vmem_limit_bytes=16 << 20),
        )(*operands)

    (cover,) = call(cover_kernel, [stats], cost=COVER)
    far = swap(right_piece[0, 0], "seg", 1, "sec")
    near = swap(right_piece[0, 0], "seg", 0, "sec")
    prec_below = rotate(prec, "sec", 1)
    (mask,) = call(mask_kernel, [matrix], sector_rows, cover)
    scaled = (left_piece[0, 0].astype(F32) * inverse_values[0]).astype(BF16)

    y, yb = call(start_kernel, [matrix, narrow], scaled, near, far, guess[0, 0], mask)

    def terms(value):
        return call(terms_kernel, [matrix, matrix], left, right, value, scratch=[inner])

    def joined(below, after, diag, above):
        (up,) = call(raise_kernel, [matrix], left, right, below, after, scratch=[inner])
        outs = [matrix, narrow, narrow]
        return call(join_kernel, outs, diag, up, above, mask, prec)

    y_below = rotate(yb, "sec", 1)
    low, sent = call(start_lower_kernel, [matrix, narrow], left, right, yb, scratch=[inner])
    above = rotate(sent, "sec", -1)
    stat, diag, low_y, diag_y = call(
        start_terms_kernel,
        [stats, matrix, matrix, matrix],
        left, right, y, yb, prec,
        scratch=[inner],
    )
    (stat,) = call(cross_kernel, [stats], y_below, low, stat)
    parts = pairwise(stat, "sec")
    g, gb, pgb = joined(y_below, stat, diag, above)
    g_below = rotate(gb, "sec", 1)
    low_g, diag_g = terms(pgb)
    low, sent = call(
        functools.partial(first_low_kernel, len(parts)),
        [matrix, narrow],
        *parts, low_g, low_y,
    )
    above = rotate(sent, "sec", -1)
    p, diag, stat, ppb, shifted = call(
        functools.partial(first_kernel, len(parts)),
        [matrix, matrix, stats, narrow, stats],
        *parts, y, g, prec, diag_g, diag_y,
    )
    stat, p_below = call(
        functools.partial(first_cross_kernel, len(parts)),
        [stats, narrow],
        *parts, y_below, g_below, prec_below, low, stat,
    )
    parts = pairwise(stat, "sec")
    hp, hpb, phpb = joined(p_below, stat, diag, above)
    low_p, diag_p = terms(ppb)
    hp_below = rotate(hpb, "sec", 1)
    low_hp, diag_hp = terms(phpb)
    x, p, coefficients, low, stat = call(
        functools.partial(second_kernel, len(parts)),
        [matrix, matrix, stats, matrix, stats],
        *parts, y, g, p, hp, prec, shifted,
        low, low_y, low_hp, low_p, diag, diag_y, diag_hp, diag_p,
    )
    (stat,) = call(
        second_cross_kernel,
        [stats],
        y_below, g_below, p_below, hp_below, prec_below, coefficients, low, stat,
    )
    parts = exchange(stat, "sec")
    block = (1, 1, size, size)
    weight = jax.ShapeDtypeStruct(block, BF16)
    energy = jax.ShapeDtypeStruct((1,), F32)
    operands = (*parts, x, p, coefficients)
    polar, far = call(functools.partial(odd_kernel, len(parts)), [matrix, weight], *operands)
    far = swap(far, "seg", 1, "sec")
    polar, near, energy = call(
        functools.partial(even_kernel, len(parts)),
        [matrix, weight, energy],
        *operands, polar,
        out_specs=[VMEM, VMEM, SMEM],
        aliases={len(operands): 0},
    )
    near = swap(near, "seg", 0, "sec")
    (handed,) = call(hand_kernel, [weight], near, far)
    (polar,) = call(store_kernel, [jax.ShapeDtypeStruct(block, F32)], polar, cost=SHORT)
    return polar, handed, energy


def solution(mesh):
    placed = (
        P("seg", "sec", None, None, None),
        P("seg", "sec", None, None, None),
        P("seg", "sec", None, None),
        P("seg", "sec", None, None),
        P("seg", "sec", None, None),
        P("seg", "sec", None),
        P("seg", "sec", None, None),
        P("seg", "sec"),
    )
    return jax.shard_map(
        inner_shards,
        mesh=mesh,
        in_specs=placed,
        out_specs=(P("seg", "sec", None, None), P("seg", "sec", None, None), P("seg")),
        check_vma=False,
    )
```

```python
import functools

import jax
import jax.numpy as jnp
from jax import lax
from jax.experimental import pallas as pl
from jax.experimental.pallas import tpu as pltpu
from jax.sharding import PartitionSpec as P


WD = 2
NS_STEPS = 3
ROWS = 8
LANES = 128
F32 = jnp.float32
BF16 = jnp.bfloat16
VMEM = pl.BlockSpec(memory_space=pltpu.VMEM)
SMEM = pl.BlockSpec(memory_space=pltpu.SMEM)
SHORT = pl.CostEstimate(flops=0, bytes_accessed=1 << 20, transcendentals=0)
COVER = pl.CostEstimate(flops=10**10, bytes_accessed=1 << 24, transcendentals=0)


def shift(value, axis, steps):
    count = lax.axis_size(axis)
    first, last = max(0, -steps), min(count, count - steps)
    return lax.ppermute(value, axis, [(source, source + steps) for source in range(first, last)])


def swap(value, axis, first, other):
    count, across = lax.axis_size(axis), lax.axis_size(other)
    partner = {}
    for i in range(first, count - 1, 2):
        partner[i], partner[i + 1] = i + 1, i
    pairs = []
    for i in range(count):
        for j in range(across):
            beside = min(j ^ 1, across - 1) if across % 2 == 0 else j
            target = (partner[i], j) if i in partner else (i, beside)
            pairs.append((i * across + j, target[0] * across + target[1]))
    return lax.ppermute(value, (axis, other), pairs)


def rotate(value, axis, steps):
    count = lax.axis_size(axis)
    return lax.ppermute(value, axis, [(source, (source + steps) % count) for source in range(count)])


def from_below(value):
    return jnp.where(lax.axis_index("sec") > 0, value, jnp.zeros_like(value))


def from_above(value):
    last = lax.axis_size("sec") - 1
    return jnp.where(lax.axis_index("sec") < last, value, jnp.zeros_like(value))


def exchange(value, axis):
    count = lax.axis_size(axis)
    if count & (count - 1):
        return [lax.psum(value, axis)]
    parts, done = [value], 1
    while done < count:
        if len(parts) > 1:
            parts = [total(parts)]
        radix = 4 if count // done >= 4 else 2
        for digit in range(1, radix):
            pairs = [(source, source ^ (digit * done)) for source in range(count)]
            parts.append(lax.ppermute(parts[0], axis, pairs))
        done *= radix
    return parts


def pairwise(value, axis):
    count = lax.axis_size(axis)
    if count & (count - 1) or count == 1:
        return exchange(value, axis)
    stride, parts = 1, [value]
    while stride < count:
        if len(parts) > 1:
            parts = [total(parts)]
        pairs = [(source, source ^ stride) for source in range(count)]
        parts.append(lax.ppermute(parts[0], axis, pairs))
        stride *= 2
    return parts


def total(parts):
    while len(parts) > 1:
        parts = [parts[i] + parts[i + 1] for i in range(0, len(parts), 2)]
    return parts[0]


def fold(product):
    row = jnp.sum(product, axis=0, keepdims=True)
    width = row.shape[-1]
    out = row[:, :LANES]
    for start in range(LANES, width, LANES):
        out = out + row[:, start : start + LANES]
    return out


def scalars(refs, count):
    sums = jnp.sum(total([ref[...] for ref in refs]), axis=1, keepdims=True)
    return [sums[i : i + 1] for i in range(count)]


def sandwich(left, right, value, inner, first, last):
    size = value.shape[-1]
    for w in range(first, last):
        product = jnp.dot(left[w], value, preferred_element_type=F32)
        inner[:, w * size : (w + 1) * size] = product.astype(BF16)
    stacked = right[first:last].reshape((last - first) * size, size)
    return jnp.dot(inner[:, first * size : last * size], stacked, preferred_element_type=F32)


def cover_kernel(out):
    out[...] = jnp.zeros(out.shape, F32)


def mask_kernel(rows, _, mask_out):
    count = rows[...]
    shape = mask_out.shape
    idx_r = lax.broadcasted_iota(jnp.int32, shape, 0)
    idx_c = lax.broadcasted_iota(jnp.int32, shape, 1)
    mask_out[...] = jnp.where((idx_r < count) & (idx_c < count), 1.0, 0.0)


def start_kernel(scaled, behind, guess, mask, y_ref, yb_ref):
    size = mask.shape[-1]
    start = jnp.dot(scaled[...], behind[...], preferred_element_type=F32) + guess[...].astype(F32)
    y = mask[...] * start * (1.0 / (1 << (size - 1).bit_length()))
    y_ref[...] = y
    yb_ref[...] = y.astype(BF16)


def start_lower_kernel(left, right, yb, low_ref, sent_ref, inner):
    low = sandwich(left, right, yb[...], inner, WD, left.shape[0])
    low_ref[...] = low
    sent_ref[...] = low.astype(BF16)


def start_terms_kernel(left, right, y, yb, prec, stat_ref, diag_ref, low_ref, diag_py_ref, inner):
    channels = left.shape[0]
    diag = sandwich(left, right, yb[...], inner, 0, WD)
    diag_ref[...] = diag
    write_sums(stat_ref, [(y, y), (y, diag)])
    weighted = (prec[...].astype(F32) * y[...]).astype(BF16)
    low_ref[...] = sandwich(left, right, weighted, inner, WD, channels)
    diag_py_ref[...] = sandwich(left, right, weighted, inner, 0, WD)


def terms_kernel(left, right, value, low_ref, diag_ref, inner):
    channels = left.shape[0]
    low_ref[...] = sandwich(left, right, value[...], inner, WD, channels)
    diag_ref[...] = sandwich(left, right, value[...], inner, 0, WD)


def write_sums(out, pairs):
    out[...] = jnp.zeros(out.shape, F32)
    for row, (one, two) in enumerate(pairs):
        out[row : row + 1] = fold(one[...] * two[...])


def add_cross(row, below, low, stat, out):
    out[...] = stat[...]
    out[row : row + 1] = stat[row : row + 1] + 2.0 * fold(from_below(below) * low[...])


def cross_kernel(below, low, stat, out):
    add_cross(1, below[...].astype(F32), low, stat, out)


def first_cross_kernel(parts, *refs):
    y, g, prec, low, stat, out, p_out = refs[parts:]
    yy, yhy = scalars(refs[:parts], 2)
    p = prec[...].astype(F32) * (g[...].astype(F32) - (yhy / yy) * y[...].astype(F32))
    p_out[...] = p.astype(BF16)
    add_cross(5, p, low, stat, out)


def second_cross_kernel(y, g, p, hp, prec, coefficients, low, stat, out):
    along_y, along_p, lam = [coefficients[i : i + 1, 0:1] for i in range(3)]
    x = along_y * y[...].astype(F32) + along_p * p[...].astype(F32)
    hx = along_y * g[...].astype(F32) + along_p * hp[...].astype(F32)
    add_cross(3, prec[...].astype(F32) * (hx - lam * x), low, stat, out)


def join_kernel(diag, up, above, mask, prec, out, out_b, weighted_b):
    joined = mask[...] * (diag[...] + up[...] + from_above(above[...].astype(F32)))
    out[...] = joined
    out_b[...] = joined.astype(BF16)
    weighted_b[...] = (prec[...].astype(F32) * joined).astype(BF16)


def raise_kernel(left, right, below, after, up_ref, inner):
    up_ref[...] = from_below(sandwich(left, right, below[...], inner, WD, left.shape[0]))


def first_low_kernel(parts, *refs):
    low_g, low_y, low_ref, sent_ref = refs[parts:]
    yy, yhy = scalars(refs[:parts], 2)
    low = low_g[...] - (yhy / yy) * low_y[...]
    low_ref[...] = low
    sent_ref[...] = low.astype(BF16)


def first_kernel(parts, *refs):
    y, g, prec, diag_g, diag_y = refs[parts : parts + 5]
    p_ref, diag_ref, stat_ref, weighted_b, shift_ref = refs[parts + 5 :]
    yy, yhy = scalars(refs[:parts], 2)
    a = yhy / yy
    shift_ref[...] = jnp.broadcast_to(a, shift_ref.shape)
    weights = prec[...].astype(F32)
    p = weights * (g[...] - a * y[...])
    p_ref[...] = p
    weighted_b[...] = (weights * p).astype(BF16)
    diag = diag_g[...] - a * diag_y[...]
    diag_ref[...] = diag
    write_sums(stat_ref, [(y, y), (y, g), (y, p), (p, p), (p, g), (p, diag)])


def ritz(a, b, c):
    lam = 0.5 * (a + c) - jnp.sqrt((0.5 * (a - c)) ** 2 + b * b)
    u, w = c - lam, -b
    n = jnp.sqrt(u * u + w * w)
    return lam, u / n, w / n


def second_kernel(parts, *refs):
    y_ref, g_ref, p_ref, hp_ref, prec, shift_ref = refs[parts : parts + 6]
    lows, diags = refs[parts + 6 : parts + 10], refs[parts + 10 : parts + 14]
    x_out, p_out, coefficients, low_ref, stat_ref = refs[parts + 14 :]
    yy, yg, yp, pp, pg, php = scalars(refs[:parts], 6)
    a = yg / yy
    s = yp / yy
    qq = pp - 2.0 * s * yp + s * s * yy
    b = (pg - s * yg) / jnp.sqrt(qq * yy)
    c = (php - 2.0 * s * pg + s * s * yg) / qq
    lam, u, w = ritz(a, b, c)
    along_p = w / jnp.sqrt(qq)
    along_y = u / jnp.sqrt(yy) - along_p * s
    factors = [along_y, along_y * (shift_ref[0:1, 0:1] - lam), along_p, -lam * along_p]
    low_ref[...] = total([factor * term[...] for factor, term in zip(factors, lows)])
    x = along_y * y_ref[...] + along_p * p_ref[...]
    g = along_y * g_ref[...] + along_p * hp_ref[...]
    p = prec[...].astype(F32) * (g - lam * x)
    x_out[...] = x
    p_out[...] = p
    diag = total([factor * term[...] for factor, term in zip(factors, diags)])
    write_sums(stat_ref, [(x, p), (p, p), (p, g), (p, diag)])
    for i, value in enumerate([along_y, along_p, lam]):
        coefficients[i : i + 1] = jnp.broadcast_to(value, (1, LANES))


def dot(one, two, over):
    dims = ((over[:1], over[1:]), ((), ()))
    return lax.dot_general(one, two, dims, preferred_element_type=F32)


def split(value):
    high = value.astype(BF16)
    return high, (value - high.astype(F32)).astype(BF16)


def product(one, two, over):
    (one_high, one_low), (two_high, two_low) = split(one), split(two)
    return dot(one_high, two_high, over) + (
        dot(one_high, two_low, over) + dot(one_low, two_high, over)
    )


def finish(sums, x_ref, p_ref, coefficients):
    xp, pp, pg, php = sums
    a = coefficients[2:3, 0:1]
    qq = pp - xp * xp
    b = (pg - xp * a) / jnp.sqrt(qq)
    c = (php - 2.0 * xp * pg + xp * xp * a) / qq
    lam, u, w = ritz(a, b, c)
    along_p = w / jnp.sqrt(qq)
    along_x = u - along_p * xp
    return lam, along_x * x_ref[...] + along_p * p_ref[...]


def polarise(x, polar_out, weight_out):
    frob = jnp.sum(jnp.sum(x * x, axis=0, keepdims=True), axis=1, keepdims=True)
    polar = x * lax.rsqrt(frob + 1e-06)
    for _ in range(NS_STEPS):
        narrow = polar.astype(BF16)
        gram = dot(narrow, narrow, (1, 1)).astype(BF16)
        polar = 1.5 * polar - 0.5 * dot(gram, narrow, (1, 0))
    polar_out[...] = polar
    weight_out[0, 0] = product(polar, x, (0, 0)).astype(BF16)


def odd_segment():
    return lax.rem(lax.axis_index("seg"), 2) == 1


def odd_kernel(parts, *refs):
    x_ref, p_ref, coefficients, polar_out, weight_out = refs[parts:]

    @pl.when(odd_segment())
    def _():
        _, x = finish(scalars(refs[:parts], 4), x_ref, p_ref, coefficients)
        polarise(x, polar_out, weight_out)

    @pl.when(jnp.logical_not(odd_segment()))
    def _():
        weight_out[...] = jnp.zeros_like(weight_out)


def even_kernel(parts, *refs):
    x_ref, p_ref, coefficients, _, polar_out, weight_out, lam_out = refs[parts:]

    @pl.when(jnp.logical_not(odd_segment()))
    def _():
        lam, x = finish(scalars(refs[:parts], 4), x_ref, p_ref, coefficients)
        lam_out[0] = lam[0, 0]
        polarise(x, polar_out, weight_out)

    @pl.when(odd_segment())
    def _():
        lam, _ = finish(scalars(refs[:parts], 4), x_ref, p_ref, coefficients)
        lam_out[0] = lam[0, 0]
        weight_out[...] = jnp.zeros_like(weight_out)


def hand_kernel(near, far, out):
    value = jnp.where(odd_segment(), near[...], far[...])
    out[...] = jnp.where(lax.axis_index("seg") > 0, value, jnp.zeros_like(value))


def store_kernel(value, out):
    out[0, 0] = value[...]


def inner_shards(
    left_env, right_env, left_piece, right_piece, guess, inverse_values, precond, sector_rows
):
    left, right, prec = left_env[0, 0], right_env[0, 0], precond[0, 0]
    channels, size = left.shape[0], left.shape[-1]
    matrix = jax.ShapeDtypeStruct((size, size), F32)
    narrow = jax.ShapeDtypeStruct((size, size), BF16)
    stats = jax.ShapeDtypeStruct((ROWS, LANES), F32)
    inner = pltpu.VMEM((size, channels * size), BF16)

    def call(kernel, outs, *operands, scratch=(), in_specs=None, out_specs=None, cost=None, aliases=None):
        return pl.pallas_call(
            kernel,
            out_shape=outs,
            in_specs=in_specs or [VMEM] * len(operands),
            out_specs=out_specs or [VMEM] * len(outs),
            scratch_shapes=list(scratch),
            cost_estimate=cost,
            input_output_aliases=aliases or {},
            compiler_params=pltpu.CompilerParams(vmem_limit_bytes=16 << 20),
        )(*operands)

    (cover,) = call(cover_kernel, [stats], cost=COVER)
    behind = shift(right_piece[0, 0], "seg", -1)
    prec_below = rotate(prec, "sec", 1)
    (mask,) = call(mask_kernel, [matrix], sector_rows, cover)
    scaled = (left_piece[0, 0].astype(F32) * inverse_values[0]).astype(BF16)

    y, yb = call(start_kernel, [matrix, narrow], scaled, behind, guess[0, 0], mask)

    def terms(value):
        return call(terms_kernel, [matrix, matrix], left, right, value, scratch=[inner])

    def joined(below, after, diag, above):
        (up,) = call(raise_kernel, [matrix], left, right, below, after, scratch=[inner])
        outs = [matrix, narrow, narrow]
        return call(join_kernel, outs, diag, up, above, mask, prec)

    y_below = rotate(yb, "sec", 1)
    low, sent = call(start_lower_kernel, [matrix, narrow], left, right, yb, scratch=[inner])
    above = rotate(sent, "sec", -1)
    stat, diag, low_y, diag_y = call(
        start_terms_kernel,
        [stats, matrix, matrix, matrix],
        left, right, y, yb, prec,
        scratch=[inner],
    )
    (stat,) = call(cross_kernel, [stats], y_below, low, stat)
    parts = pairwise(stat, "sec")
    g, gb, pgb = joined(y_below, stat, diag, above)
    g_below = rotate(gb, "sec", 1)
    low_g, diag_g = terms(pgb)
    low, sent = call(
        functools.partial(first_low_kernel, len(parts)),
        [matrix, narrow],
        *parts, low_g, low_y,
    )
    above = rotate(sent, "sec", -1)
    p, diag, stat, ppb, shifted = call(
        functools.partial(first_kernel, len(parts)),
        [matrix, matrix, stats, narrow, stats],
        *parts, y, g, prec, diag_g, diag_y,
    )
    stat, p_below = call(
        functools.partial(first_cross_kernel, len(parts)),
        [stats, narrow],
        *parts, y_below, g_below, prec_below, low, stat,
    )
    parts = pairwise(stat, "sec")
    hp, hpb, phpb = joined(p_below, stat, diag, above)
    low_p, diag_p = terms(ppb)
    hp_below = rotate(hpb, "sec", 1)
    low_hp, diag_hp = terms(phpb)
    x, p, coefficients, low, stat = call(
        functools.partial(second_kernel, len(parts)),
        [matrix, matrix, stats, matrix, stats],
        *parts, y, g, p, hp, prec, shifted,
        low, low_y, low_hp, low_p, diag, diag_y, diag_hp, diag_p,
    )
    (stat,) = call(
        second_cross_kernel,
        [stats],
        y_below, g_below, p_below, hp_below, prec_below, coefficients, low, stat,
    )
    parts = exchange(stat, "sec")
    block = (1, 1, size, size)
    weight = jax.ShapeDtypeStruct(block, BF16)
    energy = jax.ShapeDtypeStruct((1,), F32)
    operands = (*parts, x, p, coefficients)
    polar, far = call(functools.partial(odd_kernel, len(parts)), [matrix, weight], *operands)
    far = swap(far, "seg", 1, "sec")
    polar, near, energy = call(
        functools.partial(even_kernel, len(parts)),
        [matrix, weight, energy],
        *operands, polar,
        out_specs=[VMEM, VMEM, SMEM],
        aliases={len(operands): 0},
    )
    near = swap(near, "seg", 0, "sec")
    (handed,) = call(hand_kernel, [weight], near, far)
    (polar,) = call(store_kernel, [jax.ShapeDtypeStruct(block, F32)], polar, cost=SHORT)
    return polar, handed, energy


def solution(mesh):
    placed = (
        P("seg", "sec", None, None, None),
        P("seg", "sec", None, None, None),
        P("seg", "sec", None, None),
        P("seg", "sec", None, None),
        P("seg", "sec", None, None),
        P("seg", "sec", None),
        P("seg", "sec", None, None),
        P("seg", "sec"),
    )
    return jax.shard_map(
        inner_shards,
        mesh=mesh,
        in_specs=placed,
        out_specs=(P("seg", "sec", None, None), P("seg", "sec", None, None), P("seg")),
        check_vma=False,
    )
```

```python
import functools

import jax
import jax.numpy as jnp
from jax import lax
from jax.experimental import pallas as pl
from jax.experimental.pallas import tpu as pltpu
from jax.sharding import PartitionSpec as P


WD = 2
NS_STEPS = 3
ROWS = 8
LANES = 128
F32 = jnp.float32
BF16 = jnp.bfloat16
VMEM = pl.BlockSpec(memory_space=pltpu.VMEM)
SMEM = pl.BlockSpec(memory_space=pltpu.SMEM)
SHORT = pl.CostEstimate(flops=0, bytes_accessed=1 << 20, transcendentals=0)
COVER = pl.CostEstimate(flops=10**10, bytes_accessed=1 << 24, transcendentals=0)


def shift(value, axis, steps):
    count = lax.axis_size(axis)
    first, last = max(0, -steps), min(count, count - steps)
    return lax.ppermute(value, axis, [(source, source + steps) for source in range(first, last)])


def swap(value, axis, first, other):
    count, across = lax.axis_size(axis), lax.axis_size(other)
    partner = {}
    for i in range(first, count - 1, 2):
        partner[i], partner[i + 1] = i + 1, i
    pairs = []
    for i in range(count):
        for j in range(across):
            beside = min(j ^ 1, across - 1) if across % 2 == 0 else j
            target = (partner[i], j) if i in partner else (i, beside)
            pairs.append((i * across + j, target[0] * across + target[1]))
    return lax.ppermute(value, (axis, other), pairs)


def rotate(value, axis, steps):
    count = lax.axis_size(axis)
    return lax.ppermute(value, axis, [(source, (source + steps) % count) for source in range(count)])


def from_below(value):
    return jnp.where(lax.axis_index("sec") > 0, value, jnp.zeros_like(value))


def from_above(value):
    last = lax.axis_size("sec") - 1
    return jnp.where(lax.axis_index("sec") < last, value, jnp.zeros_like(value))


def exchange(value, axis):
    count = lax.axis_size(axis)
    if count & (count - 1):
        return [lax.psum(value, axis)]
    parts, done = [value], 1
    while done < count:
        if len(parts) > 1:
            parts = [total(parts)]
        radix = 4 if count // done >= 4 else 2
        for digit in range(1, radix):
            pairs = [(source, source ^ (digit * done)) for source in range(count)]
            parts.append(lax.ppermute(parts[0], axis, pairs))
        done *= radix
    return parts


def pairwise(value, axis):
    count = lax.axis_size(axis)
    if count & (count - 1) or count == 1:
        return exchange(value, axis)
    stride, parts = 1, [value]
    while stride < count:
        if len(parts) > 1:
            parts = [total(parts)]
        pairs = [(source, source ^ stride) for source in range(count)]
        parts.append(lax.ppermute(parts[0], axis, pairs))
        stride *= 2
    return parts


def total(parts):
    while len(parts) > 1:
        parts = [parts[i] + parts[i + 1] for i in range(0, len(parts), 2)]
    return parts[0]


def fold(product):
    row = jnp.sum(product, axis=0, keepdims=True)
    width = row.shape[-1]
    out = row[:, :LANES]
    for start in range(LANES, width, LANES):
        out = out + row[:, start : start + LANES]
    return out


def scalars(refs, count):
    sums = jnp.sum(total([ref[...] for ref in refs]), axis=1, keepdims=True)
    return [sums[i : i + 1] for i in range(count)]


def sandwich(left, right, value, inner, first, last):
    size = value.shape[-1]
    for w in range(first, last):
        product = jnp.dot(left[w], value, preferred_element_type=F32)
        inner[:, w * size : (w + 1) * size] = product.astype(BF16)
    stacked = right[first:last].reshape((last - first) * size, size)
    return jnp.dot(inner[:, first * size : last * size], stacked, preferred_element_type=F32)


def cover_kernel(out):
    out[...] = jnp.zeros(out.shape, F32)


def mask_kernel(rows, _, mask_out):
    count = rows[...]
    shape = mask_out.shape
    idx_r = lax.broadcasted_iota(jnp.int32, shape, 0)
    idx_c = lax.broadcasted_iota(jnp.int32, shape, 1)
    mask_out[...] = jnp.where((idx_r < count) & (idx_c < count), 1.0, 0.0)


def start_kernel(scaled, behind, guess, mask, y_ref, yb_ref):
    size = mask.shape[-1]
    start = jnp.dot(scaled[...], behind[...], preferred_element_type=F32) + guess[...].astype(F32)
    y = mask[...] * start * (1.0 / (1 << (size - 1).bit_length()))
    y_ref[...] = y
    yb_ref[...] = y.astype(BF16)


def start_lower_kernel(left, right, yb, low_ref, sent_ref, inner):
    low = sandwich(left, right, yb[...], inner, WD, left.shape[0])
    low_ref[...] = low
    sent_ref[...] = low.astype(BF16)


def start_terms_kernel(left, right, y, yb, prec, stat_ref, diag_ref, low_ref, diag_py_ref, inner):
    channels = left.shape[0]
    diag = sandwich(left, right, yb[...], inner, 0, WD)
    diag_ref[...] = diag
    write_sums(stat_ref, [(y, y), (y, diag)])
    weighted = (prec[...].astype(F32) * y[...]).astype(BF16)
    low_ref[...] = sandwich(left, right, weighted, inner, WD, channels)
    diag_py_ref[...] = sandwich(left, right, weighted, inner, 0, WD)


def terms_kernel(left, right, value, low_ref, diag_ref, inner):
    channels = left.shape[0]
    low_ref[...] = sandwich(left, right, value[...], inner, WD, channels)
    diag_ref[...] = sandwich(left, right, value[...], inner, 0, WD)


def write_sums(out, pairs):
    out[...] = jnp.zeros(out.shape, F32)
    for row, (one, two) in enumerate(pairs):
        out[row : row + 1] = fold(one[...] * two[...])


def add_cross(row, below, low, stat, out):
    out[...] = stat[...]
    out[row : row + 1] = stat[row : row + 1] + 2.0 * fold(from_below(below) * low[...])


def cross_kernel(below, low, stat, out):
    add_cross(1, below[...].astype(F32), low, stat, out)


def first_cross_kernel(parts, *refs):
    y, g, prec, low, stat, out, p_out = refs[parts:]
    yy, yhy = scalars(refs[:parts], 2)
    p = prec[...].astype(F32) * (g[...].astype(F32) - (yhy / yy) * y[...].astype(F32))
    p_out[...] = p.astype(BF16)
    add_cross(5, p, low, stat, out)


def second_cross_kernel(y, g, p, hp, prec, coefficients, low, stat, out):
    along_y, along_p, lam = [coefficients[i : i + 1, 0:1] for i in range(3)]
    x = along_y * y[...].astype(F32) + along_p * p[...].astype(F32)
    hx = along_y * g[...].astype(F32) + along_p * hp[...].astype(F32)
    add_cross(3, prec[...].astype(F32) * (hx - lam * x), low, stat, out)


def join_kernel(diag, up, above, mask, prec, out, out_b, weighted_b):
    joined = mask[...] * (diag[...] + up[...] + from_above(above[...].astype(F32)))
    out[...] = joined
    out_b[...] = joined.astype(BF16)
    weighted_b[...] = (prec[...].astype(F32) * joined).astype(BF16)


def raise_kernel(left, right, below, after, up_ref, inner):
    up_ref[...] = from_below(sandwich(left, right, below[...], inner, WD, left.shape[0]))


def first_kernel(parts, *refs):
    y, g, prec, low_g, low_y, diag_g, diag_y = refs[parts : parts + 7]
    p_ref, low_ref, sent_ref, diag_ref, stat_ref, weighted_b, shift_ref = refs[parts + 7 :]
    yy, yhy = scalars(refs[:parts], 2)
    a = yhy / yy
    shift_ref[...] = jnp.broadcast_to(a, shift_ref.shape)
    weights = prec[...].astype(F32)
    low = low_g[...] - a * low_y[...]
    low_ref[...] = low
    sent_ref[...] = low.astype(BF16)
    p = weights * (g[...] - a * y[...])
    p_ref[...] = p
    weighted_b[...] = (weights * p).astype(BF16)
    diag = diag_g[...] - a * diag_y[...]
    diag_ref[...] = diag
    write_sums(stat_ref, [(y, y), (y, g), (y, p), (p, p), (p, g), (p, diag)])


def ritz(a, b, c):
    half = 0.5 * (a - c)
    root = jnp.sqrt(half * half + b * b)
    u, w = root - half, -b
    inverse = lax.rsqrt(u * u + w * w)
    return 0.5 * (a + c) - root, u * inverse, w * inverse


def second_kernel(parts, *refs):
    y_ref, g_ref, p_ref, hp_ref, prec, shift_ref = refs[parts : parts + 6]
    lows, diags = refs[parts + 6 : parts + 10], refs[parts + 10 : parts + 14]
    x_out, p_out, coefficients, low_ref, stat_ref = refs[parts + 14 :]
    yy, yg, yp, pp, pg, php = scalars(refs[:parts], 6)
    inverse_y = lax.rsqrt(yy)
    per_y = inverse_y * inverse_y
    a = yg * per_y
    s = yp * per_y
    inverse_q = lax.rsqrt(pp - 2.0 * s * yp + s * s * yy)
    b = (pg - s * yg) * (inverse_q * inverse_y)
    c = (php - 2.0 * s * pg + s * s * yg) * (inverse_q * inverse_q)
    lam, u, w = ritz(a, b, c)
    along_p = w * inverse_q
    along_y = u * inverse_y - along_p * s
    factors = [along_y, along_y * (shift_ref[0:1, 0:1] - lam), along_p, -lam * along_p]
    low_ref[...] = total([factor * term[...] for factor, term in zip(factors, lows)])
    x = along_y * y_ref[...] + along_p * p_ref[...]
    g = along_y * g_ref[...] + along_p * hp_ref[...]
    p = prec[...].astype(F32) * (g - lam * x)
    x_out[...] = x
    p_out[...] = p
    diag = total([factor * term[...] for factor, term in zip(factors, diags)])
    write_sums(stat_ref, [(x, p), (p, p), (p, g), (p, diag)])
    for i, value in enumerate([along_y, along_p, lam]):
        coefficients[i : i + 1] = jnp.broadcast_to(value, (1, LANES))


def dot(one, two, over):
    dims = ((over[:1], over[1:]), ((), ()))
    return lax.dot_general(one, two, dims, preferred_element_type=F32)


def split(value):
    high = value.astype(BF16)
    return high, (value - high.astype(F32)).astype(BF16)


def product(one, two, over):
    (one_high, one_low), (two_high, two_low) = split(one), split(two)
    return dot(one_high, two_high, over) + (
        dot(one_high, two_low, over) + dot(one_low, two_high, over)
    )


def finish(sums, x_ref, p_ref, coefficients):
    xp, pp, pg, php = sums
    a = coefficients[2:3, 0:1]
    inverse_q = lax.rsqrt(pp - xp * xp)
    b = (pg - xp * a) * inverse_q
    c = (php - 2.0 * xp * pg + xp * xp * a) * (inverse_q * inverse_q)
    lam, u, w = ritz(a, b, c)
    along_p = w * inverse_q
    along_x = u - along_p * xp
    return lam, along_x * x_ref[...] + along_p * p_ref[...]


def polarise(x, polar_out, weight_out):
    frob = jnp.sum(jnp.sum(x * x, axis=0, keepdims=True), axis=1, keepdims=True)
    polar = x * lax.rsqrt(frob + 1e-06)
    for _ in range(NS_STEPS):
        narrow = polar.astype(BF16)
        gram = dot(narrow, narrow, (1, 1)).astype(BF16)
        polar = 1.5 * polar - 0.5 * dot(gram, narrow, (1, 0))
    polar_out[...] = polar
    weight_out[0, 0] = product(polar, x, (0, 0)).astype(BF16)


def odd_segment():
    return lax.rem(lax.axis_index("seg"), 2) == 1


def odd_kernel(parts, *refs):
    x_ref, p_ref, coefficients, polar_out, weight_out = refs[parts:]

    @pl.when(odd_segment())
    def _():
        _, x = finish(scalars(refs[:parts], 4), x_ref, p_ref, coefficients)
        polarise(x, polar_out, weight_out)

    @pl.when(jnp.logical_not(odd_segment()))
    def _():
        weight_out[...] = jnp.zeros_like(weight_out)


def even_kernel(parts, *refs):
    x_ref, p_ref, coefficients, _, polar_out, weight_out, lam_out = refs[parts:]

    @pl.when(jnp.logical_not(odd_segment()))
    def _():
        lam, x = finish(scalars(refs[:parts], 4), x_ref, p_ref, coefficients)
        polarise(x, polar_out, weight_out)
        lam_out[0] = lam[0, 0]

    @pl.when(odd_segment())
    def _():
        lam, _ = finish(scalars(refs[:parts], 4), x_ref, p_ref, coefficients)
        lam_out[0] = lam[0, 0]
        weight_out[...] = jnp.zeros_like(weight_out)


def hand_kernel(near, far, out):
    value = jnp.where(odd_segment(), near[...], far[...])
    out[...] = jnp.where(lax.axis_index("seg") > 0, value, jnp.zeros_like(value))


def store_kernel(value, out):
    out[0, 0] = value[...]


def inner_shards(
    left_env, right_env, left_piece, right_piece, guess, inverse_values, precond, sector_rows
):
    left, right, prec = left_env[0, 0], right_env[0, 0], precond[0, 0]
    channels, size = left.shape[0], left.shape[-1]
    matrix = jax.ShapeDtypeStruct((size, size), F32)
    narrow = jax.ShapeDtypeStruct((size, size), BF16)
    stats = jax.ShapeDtypeStruct((ROWS, LANES), F32)
    inner = pltpu.VMEM((size, channels * size), BF16)

    def call(kernel, outs, *operands, scratch=(), in_specs=None, out_specs=None, cost=None, aliases=None):
        return pl.pallas_call(
            kernel,
            out_shape=outs,
            in_specs=in_specs or [VMEM] * len(operands),
            out_specs=out_specs or [VMEM] * len(outs),
            scratch_shapes=list(scratch),
            cost_estimate=cost,
            input_output_aliases=aliases or {},
            compiler_params=pltpu.CompilerParams(vmem_limit_bytes=16 << 20),
        )(*operands)

    (cover,) = call(cover_kernel, [stats], cost=COVER)
    behind = shift(right_piece[0, 0], "seg", -1)
    prec_below = rotate(prec, "sec", 1)
    (mask,) = call(mask_kernel, [matrix], sector_rows, cover)
    scaled = (left_piece[0, 0].astype(F32) * inverse_values[0]).astype(BF16)

    y, yb = call(start_kernel, [matrix, narrow], scaled, behind, guess[0, 0], mask)

    def terms(value):
        return call(terms_kernel, [matrix, matrix], left, right, value, scratch=[inner])

    def joined(below, after, diag, above):
        (up,) = call(raise_kernel, [matrix], left, right, below, after, scratch=[inner])
        outs = [matrix, narrow, narrow]
        return call(join_kernel, outs, diag, up, above, mask, prec)

    y_below = rotate(yb, "sec", 1)
    low, sent = call(start_lower_kernel, [matrix, narrow], left, right, yb, scratch=[inner])
    above = rotate(sent, "sec", -1)
    stat, diag, low_y, diag_y = call(
        start_terms_kernel,
        [stats, matrix, matrix, matrix],
        left, right, y, yb, prec,
        scratch=[inner],
    )
    (stat,) = call(cross_kernel, [stats], y_below, low, stat)
    parts = pairwise(stat, "sec")
    g, gb, pgb = joined(y_below, stat, diag, above)
    g_below = rotate(gb, "sec", 1)
    low_g, diag_g = terms(pgb)
    p, low, sent, diag, stat, ppb, shifted = call(
        functools.partial(first_kernel, len(parts)),
        [matrix, matrix, narrow, matrix, stats, narrow, stats],
        *parts, y, g, prec, low_g, low_y, diag_g, diag_y,
    )
    above = rotate(sent, "sec", -1)
    stat, p_below = call(
        functools.partial(first_cross_kernel, len(parts)),
        [stats, narrow],
        *parts, y_below, g_below, prec_below, low, stat,
    )
    parts = pairwise(stat, "sec")
    hp, hpb, phpb = joined(p_below, stat, diag, above)
    low_p, diag_p = terms(ppb)
    hp_below = rotate(hpb, "sec", 1)
    low_hp, diag_hp = terms(phpb)
    x, p, coefficients, low, stat = call(
        functools.partial(second_kernel, len(parts)),
        [matrix, matrix, stats, matrix, stats],
        *parts, y, g, p, hp, prec, shifted,
        low, low_y, low_hp, low_p, diag, diag_y, diag_hp, diag_p,
    )
    (stat,) = call(
        second_cross_kernel,
        [stats],
        y_below, g_below, p_below, hp_below, prec_below, coefficients, low, stat,
    )
    parts = exchange(stat, "sec")
    block = (1, 1, size, size)
    weight = jax.ShapeDtypeStruct(block, BF16)
    energy = jax.ShapeDtypeStruct((1,), F32)
    operands = (*parts, x, p, coefficients)
    polar, far = call(functools.partial(odd_kernel, len(parts)), [matrix, weight], *operands)
    far = swap(far, "seg", 1, "sec")
    polar, near, energy = call(
        functools.partial(even_kernel, len(parts)),
        [matrix, weight, energy],
        *operands, polar,
        out_specs=[VMEM, VMEM, SMEM],
        aliases={len(operands): 0},
    )
    near = swap(near, "seg", 0, "sec")
    (handed,) = call(hand_kernel, [weight], near, far)
    (polar,) = call(store_kernel, [jax.ShapeDtypeStruct(block, F32)], polar, cost=SHORT)
    return polar, handed, energy


def solution(mesh):
    placed = (
        P("seg", "sec", None, None, None),
        P("seg", "sec", None, None, None),
        P("seg", "sec", None, None),
        P("seg", "sec", None, None),
        P("seg", "sec", None, None),
        P("seg", "sec", None),
        P("seg", "sec", None, None),
        P("seg", "sec"),
    )
    return jax.shard_map(
        inner_shards,
        mesh=mesh,
        in_specs=placed,
        out_specs=(P("seg", "sec", None, None), P("seg", "sec", None, None), P("seg")),
        check_vma=False,
    )
```

```python
import functools

import jax
import jax.numpy as jnp
from jax import lax
from jax.experimental import pallas as pl
from jax.experimental.pallas import tpu as pltpu
from jax.sharding import PartitionSpec as P


WD = 2
NS_STEPS = 3
ROWS = 8
LANES = 128
F32 = jnp.float32
BF16 = jnp.bfloat16
VMEM = pl.BlockSpec(memory_space=pltpu.VMEM)
SMEM = pl.BlockSpec(memory_space=pltpu.SMEM)
SHORT = pl.CostEstimate(flops=0, bytes_accessed=1 << 20, transcendentals=0)
COVER = pl.CostEstimate(flops=10**10, bytes_accessed=1 << 24, transcendentals=0)


def shift(value, axis, steps):
    count = lax.axis_size(axis)
    first, last = max(0, -steps), min(count, count - steps)
    return lax.ppermute(value, axis, [(source, source + steps) for source in range(first, last)])


def swap(value, axis, first, other):
    count, across = lax.axis_size(axis), lax.axis_size(other)
    partner = {}
    for i in range(first, count - 1, 2):
        partner[i], partner[i + 1] = i + 1, i
    pairs = []
    for i in range(count):
        for j in range(across):
            beside = min(j ^ 1, across - 1) if across % 2 == 0 else j
            target = (partner[i], j) if i in partner else (i, beside)
            pairs.append((i * across + j, target[0] * across + target[1]))
    return lax.ppermute(value, (axis, other), pairs)


def rotate(value, axis, steps):
    count = lax.axis_size(axis)
    return lax.ppermute(value, axis, [(source, (source + steps) % count) for source in range(count)])


def from_below(value):
    return jnp.where(lax.axis_index("sec") > 0, value, jnp.zeros_like(value))


def from_above(value):
    last = lax.axis_size("sec") - 1
    return jnp.where(lax.axis_index("sec") < last, value, jnp.zeros_like(value))


def exchange(value, axis):
    count = lax.axis_size(axis)
    if count & (count - 1):
        return [lax.psum(value, axis)]
    parts, done = [value], 1
    while done < count:
        if len(parts) > 1:
            parts = [total(parts)]
        radix = 4 if count // done >= 4 else 2
        for digit in range(1, radix):
            pairs = [(source, source ^ (digit * done)) for source in range(count)]
            parts.append(lax.ppermute(parts[0], axis, pairs))
        done *= radix
    return parts


def pairwise(value, axis):
    count = lax.axis_size(axis)
    if count & (count - 1) or count == 1:
        return exchange(value, axis)
    stride, parts = 1, [value]
    while stride < count:
        if len(parts) > 1:
            parts = [total(parts)]
        pairs = [(source, source ^ stride) for source in range(count)]
        parts.append(lax.ppermute(parts[0], axis, pairs))
        stride *= 2
    return parts


def total(parts):
    while len(parts) > 1:
        parts = [parts[i] + parts[i + 1] for i in range(0, len(parts), 2)]
    return parts[0]


def fold(product):
    row = jnp.sum(product, axis=0, keepdims=True)
    width = row.shape[-1]
    out = row[:, :LANES]
    for start in range(LANES, width, LANES):
        out = out + row[:, start : start + LANES]
    return out


def scalars(refs, count):
    sums = jnp.sum(total([ref[...] for ref in refs]), axis=1, keepdims=True)
    return [sums[i : i + 1] for i in range(count)]


def sandwich(left, right, value, inner, first, last):
    size = value.shape[-1]
    for w in range(first, last):
        product = jnp.dot(left[w], value, preferred_element_type=F32)
        inner[:, w * size : (w + 1) * size] = product.astype(BF16)
    stacked = right[first:last].reshape((last - first) * size, size)
    return jnp.dot(inner[:, first * size : last * size], stacked, preferred_element_type=F32)


def cover_kernel(out):
    out[...] = jnp.zeros(out.shape, F32)


def mask_kernel(rows, _, mask_out):
    count = rows[...]
    shape = mask_out.shape
    idx_r = lax.broadcasted_iota(jnp.int32, shape, 0)
    idx_c = lax.broadcasted_iota(jnp.int32, shape, 1)
    mask_out[...] = jnp.where((idx_r < count) & (idx_c < count), 1.0, 0.0)


def start_kernel(scaled, behind, guess, mask, y_ref, yb_ref):
    size = mask.shape[-1]
    start = jnp.dot(scaled[...], behind[...], preferred_element_type=F32) + guess[...].astype(F32)
    y = mask[...] * start * (1.0 / (1 << (size - 1).bit_length()))
    y_ref[...] = y
    yb_ref[...] = y.astype(BF16)


def start_lower_kernel(left, right, yb, low_ref, sent_ref, inner):
    low = sandwich(left, right, yb[...], inner, WD, left.shape[0])
    low_ref[...] = low
    sent_ref[...] = low.astype(BF16)


def start_terms_kernel(left, right, y, yb, prec, stat_ref, diag_ref, low_ref, diag_py_ref, inner):
    channels = left.shape[0]
    diag = sandwich(left, right, yb[...], inner, 0, WD)
    diag_ref[...] = diag
    write_sums(stat_ref, [(y, y), (y, diag)])
    weighted = (prec[...].astype(F32) * y[...]).astype(BF16)
    low_ref[...] = sandwich(left, right, weighted, inner, WD, channels)
    diag_py_ref[...] = sandwich(left, right, weighted, inner, 0, WD)


def terms_kernel(left, right, value, low_ref, diag_ref, inner):
    channels = left.shape[0]
    low_ref[...] = sandwich(left, right, value[...], inner, WD, channels)
    diag_ref[...] = sandwich(left, right, value[...], inner, 0, WD)


def write_sums(out, pairs):
    out[...] = jnp.zeros(out.shape, F32)
    for row, (one, two) in enumerate(pairs):
        out[row : row + 1] = fold(one[...] * two[...])


def add_cross(row, below, low, stat, out):
    out[...] = stat[...]
    out[row : row + 1] = stat[row : row + 1] + 2.0 * fold(from_below(below) * low[...])


def cross_kernel(below, low, stat, out):
    add_cross(1, below[...].astype(F32), low, stat, out)


def first_cross_kernel(parts, *refs):
    y, g, prec, low, stat, out, p_out = refs[parts:]
    yy, yhy = scalars(refs[:parts], 2)
    p = prec[...].astype(F32) * (g[...].astype(F32) - (yhy / yy) * y[...].astype(F32))
    p_out[...] = p.astype(BF16)
    add_cross(5, p, low, stat, out)


def second_cross_kernel(y, g, p, hp, prec, coefficients, low, stat, out):
    along_y, along_p, lam = [coefficients[i : i + 1, 0:1] for i in range(3)]
    x = along_y * y[...].astype(F32) + along_p * p[...].astype(F32)
    hx = along_y * g[...].astype(F32) + along_p * hp[...].astype(F32)
    add_cross(3, prec[...].astype(F32) * (hx - lam * x), low, stat, out)


def join_kernel(diag, up, above, mask, prec, out, out_b, weighted_b):
    joined = mask[...] * (diag[...] + up[...] + from_above(above[...].astype(F32)))
    out[...] = joined
    out_b[...] = joined.astype(BF16)
    weighted_b[...] = (prec[...].astype(F32) * joined).astype(BF16)


def raise_kernel(left, right, below, after, up_ref, inner):
    up_ref[...] = from_below(sandwich(left, right, below[...], inner, WD, left.shape[0]))


def first_kernel(parts, *refs):
    y, g, prec, low_g, low_y, diag_g, diag_y = refs[parts : parts + 7]
    p_ref, low_ref, sent_ref, diag_ref, stat_ref, weighted_b, shift_ref = refs[parts + 7 :]
    yy, yhy = scalars(refs[:parts], 2)
    a = yhy / yy
    shift_ref[...] = jnp.broadcast_to(a, shift_ref.shape)
    weights = prec[...].astype(F32)
    low = low_g[...] - a * low_y[...]
    low_ref[...] = low
    sent_ref[...] = low.astype(BF16)
    p = weights * (g[...] - a * y[...])
    p_ref[...] = p
    weighted_b[...] = (weights * p).astype(BF16)
    diag = diag_g[...] - a * diag_y[...]
    diag_ref[...] = diag
    write_sums(stat_ref, [(y, y), (y, g), (y, p), (p, p), (p, g), (p, diag)])


def ritz(a, b, c):
    lam = 0.5 * (a + c) - jnp.sqrt((0.5 * (a - c)) ** 2 + b * b)
    u, w = c - lam, -b
    n = jnp.sqrt(u * u + w * w)
    return lam, u / n, w / n


def second_kernel(parts, *refs):
    y_ref, g_ref, p_ref, hp_ref, prec, shift_ref = refs[parts : parts + 6]
    lows, diags = refs[parts + 6 : parts + 10], refs[parts + 10 : parts + 14]
    x_out, p_out, coefficients, low_ref, stat_ref = refs[parts + 14 :]
    yy, yg, yp, pp, pg, php = scalars(refs[:parts], 6)
    a = yg / yy
    s = yp / yy
    qq = pp - 2.0 * s * yp + s * s * yy
    b = (pg - s * yg) / jnp.sqrt(qq * yy)
    c = (php - 2.0 * s * pg + s * s * yg) / qq
    lam, u, w = ritz(a, b, c)
    along_p = w / jnp.sqrt(qq)
    along_y = u / jnp.sqrt(yy) - along_p * s
    factors = [along_y, along_y * (shift_ref[0:1, 0:1] - lam), along_p, -lam * along_p]
    low_ref[...] = total([factor * term[...] for factor, term in zip(factors, lows)])
    x = along_y * y_ref[...] + along_p * p_ref[...]
    g = along_y * g_ref[...] + along_p * hp_ref[...]
    p = prec[...].astype(F32) * (g - lam * x)
    x_out[...] = x
    p_out[...] = p
    diag = total([factor * term[...] for factor, term in zip(factors, diags)])
    write_sums(stat_ref, [(x, p), (p, p), (p, g), (p, diag)])
    for i, value in enumerate([along_y, along_p, lam]):
        coefficients[i : i + 1] = jnp.broadcast_to(value, (1, LANES))


def dot(one, two, over):
    dims = ((over[:1], over[1:]), ((), ()))
    return lax.dot_general(one, two, dims, preferred_element_type=F32)


def split(value):
    high = value.astype(BF16)
    return high, (value - high.astype(F32)).astype(BF16)


def product(one, two, over):
    (one_high, one_low), (two_high, two_low) = split(one), split(two)
    return dot(one_high, two_high, over) + (
        dot(one_high, two_low, over) + dot(one_low, two_high, over)
    )


def finish(sums, x_ref, p_ref, coefficients):
    xp, pp, pg, php = sums
    a = coefficients[2:3, 0:1]
    qq = pp - xp * xp
    b = (pg - xp * a) / jnp.sqrt(qq)
    c = (php - 2.0 * xp * pg + xp * xp * a) / qq
    lam, u, w = ritz(a, b, c)
    along_p = w / jnp.sqrt(qq)
    along_x = u - along_p * xp
    return lam, along_x * x_ref[...] + along_p * p_ref[...]


def polarise(x, polar_out, weight_out):
    frob = jnp.sum(jnp.sum(x * x, axis=0, keepdims=True), axis=1, keepdims=True)
    polar = x * lax.rsqrt(frob + 1e-06)
    for _ in range(NS_STEPS):
        narrow = polar.astype(BF16)
        gram = dot(narrow, narrow, (1, 1)).astype(BF16)
        polar = 1.5 * polar - 0.5 * dot(gram, narrow, (1, 0))
    polar_out[...] = polar
    weight_out[0, 0] = product(polar, x, (0, 0)).astype(BF16)


def odd_segment():
    return lax.rem(lax.axis_index("seg"), 2) == 1


def odd_kernel(parts, *refs):
    x_ref, p_ref, coefficients, polar_out, weight_out = refs[parts:]

    @pl.when(odd_segment())
    def _():
        _, x = finish(scalars(refs[:parts], 4), x_ref, p_ref, coefficients)
        polarise(x, polar_out, weight_out)

    @pl.when(jnp.logical_not(odd_segment()))
    def _():
        weight_out[...] = jnp.zeros_like(weight_out)


def even_kernel(parts, *refs):
    x_ref, p_ref, coefficients, _, polar_out, weight_out, lam_out = refs[parts:]

    @pl.when(jnp.logical_not(odd_segment()))
    def _():
        lam, x = finish(scalars(refs[:parts], 4), x_ref, p_ref, coefficients)
        lam_out[0] = lam[0, 0]
        polarise(x, polar_out, weight_out)

    @pl.when(odd_segment())
    def _():
        lam, _ = finish(scalars(refs[:parts], 4), x_ref, p_ref, coefficients)
        lam_out[0] = lam[0, 0]
        weight_out[...] = jnp.zeros_like(weight_out)


def hand_kernel(near, far, out):
    value = jnp.where(odd_segment(), near[...], far[...])
    out[...] = jnp.where(lax.axis_index("seg") > 0, value, jnp.zeros_like(value))


def store_kernel(value, out):
    out[0, 0] = value[...]


def inner_shards(
    left_env, right_env, left_piece, right_piece, guess, inverse_values, precond, sector_rows
):
    left, right, prec = left_env[0, 0], right_env[0, 0], precond[0, 0]
    channels, size = left.shape[0], left.shape[-1]
    matrix = jax.ShapeDtypeStruct((size, size), F32)
    narrow = jax.ShapeDtypeStruct((size, size), BF16)
    stats = jax.ShapeDtypeStruct((ROWS, LANES), F32)
    inner = pltpu.VMEM((size, channels * size), BF16)

    def call(kernel, outs, *operands, scratch=(), in_specs=None, out_specs=None, cost=None, aliases=None):
        return pl.pallas_call(
            kernel,
            out_shape=outs,
            in_specs=in_specs or [VMEM] * len(operands),
            out_specs=out_specs or [VMEM] * len(outs),
            scratch_shapes=list(scratch),
            cost_estimate=cost,
            input_output_aliases=aliases or {},
            compiler_params=pltpu.CompilerParams(vmem_limit_bytes=16 << 20),
        )(*operands)

    (cover,) = call(cover_kernel, [stats], cost=COVER)
    behind = shift(right_piece[0, 0], "seg", -1)
    prec_below = rotate(prec, "sec", 1)
    (mask,) = call(mask_kernel, [matrix], sector_rows, cover)
    scaled = (left_piece[0, 0].astype(F32) * inverse_values[0]).astype(BF16)

    y, yb = call(start_kernel, [matrix, narrow], scaled, behind, guess[0, 0], mask)

    def terms(value):
        return call(terms_kernel, [matrix, matrix], left, right, value, scratch=[inner])

    def joined(below, after, diag, above):
        (up,) = call(raise_kernel, [matrix], left, right, below, after, scratch=[inner])
        outs = [matrix, narrow, narrow]
        return call(join_kernel, outs, diag, up, above, mask, prec)

    y_below = rotate(yb, "sec", 1)
    low, sent = call(start_lower_kernel, [matrix, narrow], left, right, yb, scratch=[inner])
    above = rotate(sent, "sec", -1)
    stat, diag, low_y, diag_y = call(
        start_terms_kernel,
        [stats, matrix, matrix, matrix],
        left, right, y, yb, prec,
        scratch=[inner],
    )
    (stat,) = call(cross_kernel, [stats], y_below, low, stat)
    parts = exchange(stat, "sec")
    g, gb, pgb = joined(y_below, stat, diag, above)
    g_below = rotate(gb, "sec", 1)
    low_g, diag_g = terms(pgb)
    p, low, sent, diag, stat, ppb, shifted = call(
        functools.partial(first_kernel, len(parts)),
        [matrix, matrix, narrow, matrix, stats, narrow, stats],
        *parts, y, g, prec, low_g, low_y, diag_g, diag_y,
    )
    above = rotate(sent, "sec", -1)
    stat, p_below = call(
        functools.partial(first_cross_kernel, len(parts)),
        [stats, narrow],
        *parts, y_below, g_below, prec_below, low, stat,
    )
    parts = pairwise(stat, "sec")
    hp, hpb, phpb = joined(p_below, stat, diag, above)
    low_p, diag_p = terms(ppb)
    hp_below = rotate(hpb, "sec", 1)
    low_hp, diag_hp = terms(phpb)
    x, p, coefficients, low, stat = call(
        functools.partial(second_kernel, len(parts)),
        [matrix, matrix, stats, matrix, stats],
        *parts, y, g, p, hp, prec, shifted,
        low, low_y, low_hp, low_p, diag, diag_y, diag_hp, diag_p,
    )
    (stat,) = call(
        second_cross_kernel,
        [stats],
        y_below, g_below, p_below, hp_below, prec_below, coefficients, low, stat,
    )
    parts = exchange(stat, "sec")
    block = (1, 1, size, size)
    weight = jax.ShapeDtypeStruct(block, BF16)
    energy = jax.ShapeDtypeStruct((1,), F32)
    operands = (*parts, x, p, coefficients)
    polar, far = call(functools.partial(odd_kernel, len(parts)), [matrix, weight], *operands)
    far = swap(far, "seg", 1, "sec")
    polar, near, energy = call(
        functools.partial(even_kernel, len(parts)),
        [matrix, weight, energy],
        *operands, polar,
        out_specs=[VMEM, VMEM, SMEM],
        aliases={len(operands): 0},
    )
    near = swap(near, "seg", 0, "sec")
    (handed,) = call(hand_kernel, [weight], near, far)
    (polar,) = call(store_kernel, [jax.ShapeDtypeStruct(block, F32)], polar, cost=SHORT)
    return polar, handed, energy


def solution(mesh):
    placed = (
        P("seg", "sec", None, None, None),
        P("seg", "sec", None, None, None),
        P("seg", "sec", None, None),
        P("seg", "sec", None, None),
        P("seg", "sec", None, None),
        P("seg", "sec", None),
        P("seg", "sec", None, None),
        P("seg", "sec"),
    )
    return jax.shard_map(
        inner_shards,
        mesh=mesh,
        in_specs=placed,
        out_specs=(P("seg", "sec", None, None), P("seg", "sec", None, None), P("seg")),
        check_vma=False,
    )
```

```python
import functools

import jax
import jax.numpy as jnp
from jax import lax
from jax.experimental import pallas as pl
from jax.experimental.pallas import tpu as pltpu
from jax.sharding import PartitionSpec as P


WD = 2
NS_STEPS = 3
ROWS = 8
BAND = 32
LANES = 128
F32 = jnp.float32
BF16 = jnp.bfloat16
VMEM = pl.BlockSpec(memory_space=pltpu.VMEM)
SMEM = pl.BlockSpec(memory_space=pltpu.SMEM)
SHORT = pl.CostEstimate(flops=0, bytes_accessed=1 << 20, transcendentals=0)
COVER = pl.CostEstimate(flops=10**10, bytes_accessed=1 << 24, transcendentals=0)


def shift(value, axis, steps):
    count = lax.axis_size(axis)
    first, last = max(0, -steps), min(count, count - steps)
    return lax.ppermute(value, axis, [(source, source + steps) for source in range(first, last)])


def swap(value, axis, first, other):
    count, across = lax.axis_size(axis), lax.axis_size(other)
    partner = {}
    for i in range(first, count - 1, 2):
        partner[i], partner[i + 1] = i + 1, i
    pairs = []
    for i in range(count):
        for j in range(across):
            beside = min(j ^ 1, across - 1) if across % 2 == 0 else j
            target = (partner[i], j) if i in partner else (i, beside)
            pairs.append((i * across + j, target[0] * across + target[1]))
    return lax.ppermute(value, (axis, other), pairs)


def rotate(value, axis, steps):
    count = lax.axis_size(axis)
    return lax.ppermute(value, axis, [(source, (source + steps) % count) for source in range(count)])


def from_below(value):
    return jnp.where(lax.axis_index("sec") > 0, value, jnp.zeros_like(value))


def from_above(value):
    last = lax.axis_size("sec") - 1
    return jnp.where(lax.axis_index("sec") < last, value, jnp.zeros_like(value))


def exchange(value, axis):
    count = lax.axis_size(axis)
    if count & (count - 1):
        return [lax.psum(value, axis)]
    parts, done = [value], 1
    while done < count:
        if len(parts) > 1:
            parts = [total(parts)]
        radix = 4 if count // done >= 4 else 2
        for digit in range(1, radix):
            pairs = [(source, source ^ (digit * done)) for source in range(count)]
            parts.append(lax.ppermute(parts[0], axis, pairs))
        done *= radix
    return parts


def pairwise(value, axis):
    count = lax.axis_size(axis)
    if count & (count - 1) or count == 1:
        return exchange(value, axis)
    stride, parts = 1, [value]
    while stride < count:
        if len(parts) > 1:
            parts = [total(parts)]
        pairs = [(source, source ^ stride) for source in range(count)]
        parts.append(lax.ppermute(parts[0], axis, pairs))
        stride *= 2
    return parts


def total(parts):
    while len(parts) > 1:
        parts = [parts[i] + parts[i + 1] for i in range(0, len(parts), 2)]
    return parts[0]


def fold(product):
    row = jnp.sum(product, axis=0, keepdims=True)
    width = row.shape[-1]
    out = row[:, :LANES]
    for start in range(LANES, width, LANES):
        out = out + row[:, start : start + LANES]
    return out


def scalars(refs, count):
    sums = jnp.sum(total([ref[...] for ref in refs]), axis=1, keepdims=True)
    return [sums[i : i + 1] for i in range(count)]


def sandwich(left, right, value, inner, first, last):
    size = value.shape[-1]
    for w in range(first, last):
        product = jnp.dot(left[w], value, preferred_element_type=F32)
        inner[:, w * size : (w + 1) * size] = product.astype(BF16)
    stacked = right[first:last].reshape((last - first) * size, size)
    return jnp.dot(inner[:, first * size : last * size], stacked, preferred_element_type=F32)


def cover_kernel(out):
    out[...] = jnp.zeros(out.shape, F32)


def mask_kernel(rows, _, mask_out):
    count = rows[...]
    shape = mask_out.shape
    idx_r = lax.broadcasted_iota(jnp.int32, shape, 0)
    idx_c = lax.broadcasted_iota(jnp.int32, shape, 1)
    mask_out[...] = jnp.where((idx_r < count) & (idx_c < count), 1.0, 0.0)


def start_kernel(scaled, behind, guess, mask, y_ref, yb_ref):
    size = mask.shape[-1]
    start = jnp.dot(scaled[...], behind[...], preferred_element_type=F32) + guess[...].astype(F32)
    y = mask[...] * start * (1.0 / (1 << (size - 1).bit_length()))
    y_ref[...] = y
    yb_ref[...] = y.astype(BF16)


def start_lower_kernel(left, right, yb, low_ref, sent_ref, inner):
    low = sandwich(left, right, yb[...], inner, WD, left.shape[0])
    low_ref[...] = low
    sent_ref[...] = low.astype(BF16)


def start_terms_kernel(left, right, y, yb, prec, stat_ref, diag_ref, low_ref, diag_py_ref, inner):
    channels = left.shape[0]
    diag = sandwich(left, right, yb[...], inner, 0, WD)
    diag_ref[...] = diag
    write_sums(stat_ref, [(y, y), (y, diag)])
    weighted = (prec[...].astype(F32) * y[...]).astype(BF16)
    low_ref[...] = sandwich(left, right, weighted, inner, WD, channels)
    diag_py_ref[...] = sandwich(left, right, weighted, inner, 0, WD)


def terms_kernel(left, right, value, low_ref, diag_ref, inner):
    channels = left.shape[0]
    low_ref[...] = sandwich(left, right, value[...], inner, WD, channels)
    diag_ref[...] = sandwich(left, right, value[...], inner, 0, WD)


def write_sums(out, pairs):
    out[...] = jnp.zeros(out.shape, F32)
    for row, (one, two) in enumerate(pairs):
        out[row : row + 1] = fold(one[...] * two[...])


def add_cross(row, below, low, stat, out):
    out[...] = stat[...]
    out[row : row + 1] = stat[row : row + 1] + 2.0 * fold(from_below(below) * low[...])


def cross_kernel(below, low, stat, out):
    add_cross(1, below[...].astype(F32), low, stat, out)


def first_cross_kernel(parts, *refs):
    y, g, prec, low, stat, out, p_out = refs[parts:]
    yy, yhy = scalars(refs[:parts], 2)
    p = prec[...].astype(F32) * (g[...].astype(F32) - (yhy / yy) * y[...].astype(F32))
    p_out[...] = p.astype(BF16)
    add_cross(5, p, low, stat, out)


def second_cross_kernel(y, g, p, hp, prec, coefficients, low, stat, out):
    along_y, along_p, lam = [coefficients[i : i + 1, 0:1] for i in range(3)]
    x = along_y * y[...].astype(F32) + along_p * p[...].astype(F32)
    hx = along_y * g[...].astype(F32) + along_p * hp[...].astype(F32)
    add_cross(3, prec[...].astype(F32) * (hx - lam * x), low, stat, out)


def join_kernel(diag, up, above, mask, prec, out, out_b, weighted_b):
    joined = mask[...] * (diag[...] + up[...] + from_above(above[...].astype(F32)))
    out[...] = joined
    out_b[...] = joined.astype(BF16)
    weighted_b[...] = (prec[...].astype(F32) * joined).astype(BF16)


def raise_kernel(left, right, below, after, up_ref, inner):
    up_ref[...] = from_below(sandwich(left, right, below[...], inner, WD, left.shape[0]))


def first_kernel(parts, *refs):
    y, g, prec, low_g, low_y, diag_g, diag_y = refs[parts : parts + 7]
    p_ref, low_ref, sent_ref, diag_ref, stat_ref, weighted_b, shift_ref = refs[parts + 7 :]
    yy, yhy = scalars(refs[:parts], 2)
    a = yhy / yy
    shift_ref[...] = jnp.broadcast_to(a, shift_ref.shape)
    weights = prec[...].astype(F32)
    low = low_g[...] - a * low_y[...]
    low_ref[...] = low
    sent_ref[...] = low.astype(BF16)
    p = weights * (g[...] - a * y[...])
    p_ref[...] = p
    weighted_b[...] = (weights * p).astype(BF16)
    diag = diag_g[...] - a * diag_y[...]
    diag_ref[...] = diag
    write_sums(stat_ref, [(y, y), (y, g), (y, p), (p, p), (p, g), (p, diag)])


def ritz(a, b, c):
    half = 0.5 * (a - c)
    root = jnp.sqrt(half * half + b * b)
    u, w = root - half, -b
    inverse = lax.rsqrt(u * u + w * w)
    return 0.5 * (a + c) - root, u * inverse, w * inverse


def second_kernel(parts, *refs):
    y_ref, g_ref, p_ref, hp_ref, prec, shift_ref = refs[parts : parts + 6]
    lows, diags = refs[parts + 6 : parts + 10], refs[parts + 10 : parts + 14]
    x_out, p_out, coefficients, low_ref, stat_ref = refs[parts + 14 :]
    yy, yg, yp, pp, pg, php = scalars(refs[:parts], 6)
    inverse_y = lax.rsqrt(yy)
    per_y = inverse_y * inverse_y
    a = yg * per_y
    s = yp * per_y
    inverse_q = lax.rsqrt(pp - 2.0 * s * yp + s * s * yy)
    b = (pg - s * yg) * (inverse_q * inverse_y)
    c = (php - 2.0 * s * pg + s * s * yg) * (inverse_q * inverse_q)
    lam, u, w = ritz(a, b, c)
    along_p = w * inverse_q
    along_y = u * inverse_y - along_p * s
    factors = [along_y, along_y * (shift_ref[0:1, 0:1] - lam), along_p, -lam * along_p]
    size = low_ref.shape[0]
    step = BAND if size % BAND == 0 else size
    sums = None
    for start in range(0, size, step):
        band = slice(start, start + step)
        low_ref[band] = total([factor * term[band] for factor, term in zip(factors, lows)])
        x = along_y * y_ref[band] + along_p * p_ref[band]
        g = along_y * g_ref[band] + along_p * hp_ref[band]
        p = prec[band].astype(F32) * (g - lam * x)
        x_out[band] = x
        p_out[band] = p
        diag = total([factor * term[band] for factor, term in zip(factors, diags)])
        products = [x * p, p * p, p * g, p * diag]
        parts_of = [jnp.sum(value.reshape(-1, ROWS, size), axis=0) for value in products]
        sums = parts_of if sums is None else [one + two for one, two in zip(sums, parts_of)]
    stat_ref[...] = jnp.zeros(stat_ref.shape, F32)
    for row, value in enumerate(sums):
        stat_ref[row : row + 1] = fold(value)
    for i, value in enumerate([along_y, along_p, lam]):
        coefficients[i : i + 1] = jnp.broadcast_to(value, (1, LANES))


def dot(one, two, over):
    dims = ((over[:1], over[1:]), ((), ()))
    return lax.dot_general(one, two, dims, preferred_element_type=F32)


def split(value):
    high = value.astype(BF16)
    return high, (value - high.astype(F32)).astype(BF16)


def product(one, two, over):
    (one_high, one_low), (two_high, two_low) = split(one), split(two)
    return dot(one_high, two_high, over) + (
        dot(one_high, two_low, over) + dot(one_low, two_high, over)
    )


def finish(sums, x_ref, p_ref, coefficients):
    xp, pp, pg, php = sums
    a = coefficients[2:3, 0:1]
    inverse_q = lax.rsqrt(pp - xp * xp)
    b = (pg - xp * a) * inverse_q
    c = (php - 2.0 * xp * pg + xp * xp * a) * (inverse_q * inverse_q)
    lam, u, w = ritz(a, b, c)
    along_p = w * inverse_q
    along_x = u - along_p * xp
    return lam, along_x * x_ref[...] + along_p * p_ref[...]


def polarise(x, polar_out, weight_out):
    frob = jnp.sum(jnp.sum(x * x, axis=0, keepdims=True), axis=1, keepdims=True)
    polar = x * lax.rsqrt(frob + 1e-06)
    for _ in range(NS_STEPS):
        narrow = polar.astype(BF16)
        gram = dot(narrow, narrow, (1, 1)).astype(BF16)
        polar = 1.5 * polar - 0.5 * dot(gram, narrow, (1, 0))
    polar_out[...] = polar
    weight_out[0, 0] = product(polar, x, (0, 0)).astype(BF16)


def odd_segment():
    return lax.rem(lax.axis_index("seg"), 2) == 1


def odd_kernel(parts, *refs):
    x_ref, p_ref, coefficients, polar_out, weight_out = refs[parts:]

    @pl.when(odd_segment())
    def _():
        _, x = finish(scalars(refs[:parts], 4), x_ref, p_ref, coefficients)
        polarise(x, polar_out, weight_out)

    @pl.when(jnp.logical_not(odd_segment()))
    def _():
        weight_out[...] = jnp.zeros_like(weight_out)


def even_kernel(parts, *refs):
    x_ref, p_ref, coefficients, _, polar_out, weight_out, lam_out = refs[parts:]

    @pl.when(jnp.logical_not(odd_segment()))
    def _():
        lam, x = finish(scalars(refs[:parts], 4), x_ref, p_ref, coefficients)
        lam_out[0] = lam[0, 0]
        polarise(x, polar_out, weight_out)

    @pl.when(odd_segment())
    def _():
        lam, _ = finish(scalars(refs[:parts], 4), x_ref, p_ref, coefficients)
        lam_out[0] = lam[0, 0]
        weight_out[...] = jnp.zeros_like(weight_out)


def hand_kernel(near, far, out):
    value = jnp.where(odd_segment(), near[...], far[...])
    out[...] = jnp.where(lax.axis_index("seg") > 0, value, jnp.zeros_like(value))


def store_kernel(value, out):
    out[0, 0] = value[...]


def inner_shards(
    left_env, right_env, left_piece, right_piece, guess, inverse_values, precond, sector_rows
):
    left, right, prec = left_env[0, 0], right_env[0, 0], precond[0, 0]
    channels, size = left.shape[0], left.shape[-1]
    matrix = jax.ShapeDtypeStruct((size, size), F32)
    narrow = jax.ShapeDtypeStruct((size, size), BF16)
    stats = jax.ShapeDtypeStruct((ROWS, LANES), F32)
    inner = pltpu.VMEM((size, channels * size), BF16)

    def call(kernel, outs, *operands, scratch=(), in_specs=None, out_specs=None, cost=None, aliases=None):
        return pl.pallas_call(
            kernel,
            out_shape=outs,
            in_specs=in_specs or [VMEM] * len(operands),
            out_specs=out_specs or [VMEM] * len(outs),
            scratch_shapes=list(scratch),
            cost_estimate=cost,
            input_output_aliases=aliases or {},
            compiler_params=pltpu.CompilerParams(vmem_limit_bytes=16 << 20),
        )(*operands)

    (cover,) = call(cover_kernel, [stats], cost=COVER)
    behind = shift(right_piece[0, 0], "seg", -1)
    prec_below = rotate(prec, "sec", 1)
    (mask,) = call(mask_kernel, [matrix], sector_rows, cover)
    scaled = (left_piece[0, 0].astype(F32) * inverse_values[0]).astype(BF16)

    y, yb = call(start_kernel, [matrix, narrow], scaled, behind, guess[0, 0], mask)

    def terms(value):
        return call(terms_kernel, [matrix, matrix], left, right, value, scratch=[inner])

    def joined(below, after, diag, above):
        (up,) = call(raise_kernel, [matrix], left, right, below, after, scratch=[inner])
        outs = [matrix, narrow, narrow]
        return call(join_kernel, outs, diag, up, above, mask, prec)

    y_below = rotate(yb, "sec", 1)
    low, sent = call(start_lower_kernel, [matrix, narrow], left, right, yb, scratch=[inner])
    above = rotate(sent, "sec", -1)
    stat, diag, low_y, diag_y = call(
        start_terms_kernel,
        [stats, matrix, matrix, matrix],
        left, right, y, yb, prec,
        scratch=[inner],
    )
    (stat,) = call(cross_kernel, [stats], y_below, low, stat)
    parts = pairwise(stat, "sec")
    g, gb, pgb = joined(y_below, stat, diag, above)
    g_below = rotate(gb, "sec", 1)
    low_g, diag_g = terms(pgb)
    p, low, sent, diag, stat, ppb, shifted = call(
        functools.partial(first_kernel, len(parts)),
        [matrix, matrix, narrow, matrix, stats, narrow, stats],
        *parts, y, g, prec, low_g, low_y, diag_g, diag_y,
    )
    above = rotate(sent, "sec", -1)
    stat, p_below = call(
        functools.partial(first_cross_kernel, len(parts)),
        [stats, narrow],
        *parts, y_below, g_below, prec_below, low, stat,
    )
    parts = pairwise(stat, "sec")
    hp, hpb, phpb = joined(p_below, stat, diag, above)
    low_p, diag_p = terms(ppb)
    hp_below = rotate(hpb, "sec", 1)
    low_hp, diag_hp = terms(phpb)
    x, p, coefficients, low, stat = call(
        functools.partial(second_kernel, len(parts)),
        [matrix, matrix, stats, matrix, stats],
        *parts, y, g, p, hp, prec, shifted,
        low, low_y, low_hp, low_p, diag, diag_y, diag_hp, diag_p,
    )
    (stat,) = call(
        second_cross_kernel,
        [stats],
        y_below, g_below, p_below, hp_below, prec_below, coefficients, low, stat,
    )
    parts = exchange(stat, "sec")
    block = (1, 1, size, size)
    weight = jax.ShapeDtypeStruct(block, BF16)
    energy = jax.ShapeDtypeStruct((1,), F32)
    operands = (*parts, x, p, coefficients)
    polar, far = call(functools.partial(odd_kernel, len(parts)), [matrix, weight], *operands)
    far = swap(far, "seg", 1, "sec")
    polar, near, energy = call(
        functools.partial(even_kernel, len(parts)),
        [matrix, weight, energy],
        *operands, polar,
        out_specs=[VMEM, VMEM, SMEM],
        aliases={len(operands): 0},
    )
    near = swap(near, "seg", 0, "sec")
    (handed,) = call(hand_kernel, [weight], near, far)
    (polar,) = call(store_kernel, [jax.ShapeDtypeStruct(block, F32)], polar, cost=SHORT)
    return polar, handed, energy


def solution(mesh):
    placed = (
        P("seg", "sec", None, None, None),
        P("seg", "sec", None, None, None),
        P("seg", "sec", None, None),
        P("seg", "sec", None, None),
        P("seg", "sec", None, None),
        P("seg", "sec", None),
        P("seg", "sec", None, None),
        P("seg", "sec"),
    )
    return jax.shard_map(
        inner_shards,
        mesh=mesh,
        in_specs=placed,
        out_specs=(P("seg", "sec", None, None), P("seg", "sec", None, None), P("seg")),
        check_vma=False,
    )
```

```python
import functools

import jax
import jax.numpy as jnp
from jax import lax
from jax.experimental import pallas as pl
from jax.experimental.pallas import tpu as pltpu
from jax.sharding import PartitionSpec as P


WD = 2
NS_STEPS = 3
ROWS = 8
BAND = 32
LANES = 128
F32 = jnp.float32
BF16 = jnp.bfloat16
VMEM = pl.BlockSpec(memory_space=pltpu.VMEM)
SMEM = pl.BlockSpec(memory_space=pltpu.SMEM)
SHORT = pl.CostEstimate(flops=0, bytes_accessed=1 << 20, transcendentals=0)
COVER = pl.CostEstimate(flops=10**10, bytes_accessed=1 << 24, transcendentals=0)


def shift(value, axis, steps):
    count = lax.axis_size(axis)
    first, last = max(0, -steps), min(count, count - steps)
    return lax.ppermute(value, axis, [(source, source + steps) for source in range(first, last)])


def swap(value, axis, first, other):
    count, across = lax.axis_size(axis), lax.axis_size(other)
    partner = {}
    for i in range(first, count - 1, 2):
        partner[i], partner[i + 1] = i + 1, i
    pairs = []
    for i in range(count):
        for j in range(across):
            beside = min(j ^ 1, across - 1) if across % 2 == 0 else j
            target = (partner[i], j) if i in partner else (i, beside)
            pairs.append((i * across + j, target[0] * across + target[1]))
    return lax.ppermute(value, (axis, other), pairs)


def rotate(value, axis, steps):
    count = lax.axis_size(axis)
    return lax.ppermute(value, axis, [(source, (source + steps) % count) for source in range(count)])


def from_below(value):
    return jnp.where(lax.axis_index("sec") > 0, value, jnp.zeros_like(value))


def from_above(value):
    last = lax.axis_size("sec") - 1
    return jnp.where(lax.axis_index("sec") < last, value, jnp.zeros_like(value))


def exchange(value, axis):
    count = lax.axis_size(axis)
    if count & (count - 1):
        return [lax.psum(value, axis)]
    parts, done = [value], 1
    while done < count:
        if len(parts) > 1:
            parts = [total(parts)]
        radix = 4 if count // done >= 4 else 2
        for digit in range(1, radix):
            pairs = [(source, source ^ (digit * done)) for source in range(count)]
            parts.append(lax.ppermute(parts[0], axis, pairs))
        done *= radix
    return parts


def pairwise(value, axis):
    count = lax.axis_size(axis)
    if count & (count - 1) or count == 1:
        return exchange(value, axis)
    stride, parts = 1, [value]
    while stride < count:
        if len(parts) > 1:
            parts = [total(parts)]
        pairs = [(source, source ^ stride) for source in range(count)]
        parts.append(lax.ppermute(parts[0], axis, pairs))
        stride *= 2
    return parts


def total(parts):
    while len(parts) > 1:
        parts = [parts[i] + parts[i + 1] for i in range(0, len(parts), 2)]
    return parts[0]


def fold(product):
    row = jnp.sum(product, axis=0, keepdims=True)
    width = row.shape[-1]
    out = row[:, :LANES]
    for start in range(LANES, width, LANES):
        out = out + row[:, start : start + LANES]
    return out


def scalars(refs, count):
    sums = jnp.sum(total([ref[...] for ref in refs]), axis=1, keepdims=True)
    return [sums[i : i + 1] for i in range(count)]


def sandwich(left, right, value, inner, first, last):
    size = value.shape[-1]
    for w in range(first, last):
        product = jnp.dot(left[w], value, preferred_element_type=F32)
        inner[:, w * size : (w + 1) * size] = product.astype(BF16)
    stacked = right[first:last].reshape((last - first) * size, size)
    return jnp.dot(inner[:, first * size : last * size], stacked, preferred_element_type=F32)


def cover_kernel(out):
    out[...] = jnp.zeros(out.shape, F32)


def mask_kernel(rows, _, mask_out):
    count = rows[...]
    shape = mask_out.shape
    idx_r = lax.broadcasted_iota(jnp.int32, shape, 0)
    idx_c = lax.broadcasted_iota(jnp.int32, shape, 1)
    mask_out[...] = jnp.where((idx_r < count) & (idx_c < count), 1.0, 0.0)


def start_kernel(scaled, behind, guess, mask, y_ref, yb_ref):
    size = mask.shape[-1]
    start = jnp.dot(scaled[...], behind[...], preferred_element_type=F32) + guess[...].astype(F32)
    y = mask[...] * start * (1.0 / (1 << (size - 1).bit_length()))
    y_ref[...] = y
    yb_ref[...] = y.astype(BF16)


def start_lower_kernel(left, right, yb, low_ref, sent_ref, inner):
    low = sandwich(left, right, yb[...], inner, WD, left.shape[0])
    low_ref[...] = low
    sent_ref[...] = low.astype(BF16)


def start_terms_kernel(left, right, y, yb, prec, stat_ref, diag_ref, low_ref, diag_py_ref, inner):
    channels = left.shape[0]
    diag = sandwich(left, right, yb[...], inner, 0, WD)
    diag_ref[...] = diag
    write_sums(stat_ref, [(y, y), (y, diag)])
    weighted = (prec[...].astype(F32) * y[...]).astype(BF16)
    low_ref[...] = sandwich(left, right, weighted, inner, WD, channels)
    diag_py_ref[...] = sandwich(left, right, weighted, inner, 0, WD)


def terms_kernel(left, right, value, low_ref, diag_ref, inner):
    channels = left.shape[0]
    low_ref[...] = sandwich(left, right, value[...], inner, WD, channels)
    diag_ref[...] = sandwich(left, right, value[...], inner, 0, WD)


def write_sums(out, pairs):
    out[...] = jnp.zeros(out.shape, F32)
    for row, (one, two) in enumerate(pairs):
        out[row : row + 1] = fold(one[...] * two[...])


def add_cross(row, below, low, stat, out):
    out[...] = stat[...]
    out[row : row + 1] = stat[row : row + 1] + 2.0 * fold(from_below(below) * low[...])


def cross_kernel(below, low, stat, out):
    add_cross(1, below[...].astype(F32), low, stat, out)


def first_cross_kernel(parts, *refs):
    y, g, prec, low, stat, out, p_out = refs[parts:]
    yy, yhy = scalars(refs[:parts], 2)
    p = prec[...].astype(F32) * (g[...].astype(F32) - (yhy / yy) * y[...].astype(F32))
    p_out[...] = p.astype(BF16)
    add_cross(5, p, low, stat, out)


def second_cross_kernel(y, g, p, hp, prec, coefficients, low, stat, out):
    along_y, along_p, lam = [coefficients[i : i + 1, 0:1] for i in range(3)]
    x = along_y * y[...].astype(F32) + along_p * p[...].astype(F32)
    hx = along_y * g[...].astype(F32) + along_p * hp[...].astype(F32)
    add_cross(3, prec[...].astype(F32) * (hx - lam * x), low, stat, out)


def join_kernel(diag, up, above, mask, prec, out, out_b, weighted_b):
    joined = mask[...] * (diag[...] + up[...] + from_above(above[...].astype(F32)))
    out[...] = joined
    out_b[...] = joined.astype(BF16)
    weighted_b[...] = (prec[...].astype(F32) * joined).astype(BF16)


def raise_kernel(left, right, below, after, up_ref, inner):
    up_ref[...] = from_below(sandwich(left, right, below[...], inner, WD, left.shape[0]))


def first_kernel(parts, *refs):
    y, g, prec, low_g, low_y, diag_g, diag_y = refs[parts : parts + 7]
    p_ref, low_ref, sent_ref, diag_ref, stat_ref, weighted_b, shift_ref = refs[parts + 7 :]
    yy, yhy = scalars(refs[:parts], 2)
    a = yhy / yy
    shift_ref[...] = jnp.broadcast_to(a, shift_ref.shape)
    weights = prec[...].astype(F32)
    low = low_g[...] - a * low_y[...]
    low_ref[...] = low
    sent_ref[...] = low.astype(BF16)
    p = weights * (g[...] - a * y[...])
    p_ref[...] = p
    weighted_b[...] = (weights * p).astype(BF16)
    diag = diag_g[...] - a * diag_y[...]
    diag_ref[...] = diag
    write_sums(stat_ref, [(y, y), (y, g), (y, p), (p, p), (p, g), (p, diag)])


def ritz(a, b, c):
    lam = 0.5 * (a + c) - jnp.sqrt((0.5 * (a - c)) ** 2 + b * b)
    u, w = c - lam, -b
    n = jnp.sqrt(u * u + w * w)
    return lam, u / n, w / n


def second_kernel(parts, *refs):
    y_ref, g_ref, p_ref, hp_ref, prec, shift_ref = refs[parts : parts + 6]
    lows, diags = refs[parts + 6 : parts + 10], refs[parts + 10 : parts + 14]
    x_out, p_out, coefficients, low_ref, stat_ref = refs[parts + 14 :]
    yy, yg, yp, pp, pg, php = scalars(refs[:parts], 6)
    a = yg / yy
    s = yp / yy
    qq = pp - 2.0 * s * yp + s * s * yy
    b = (pg - s * yg) / jnp.sqrt(qq * yy)
    c = (php - 2.0 * s * pg + s * s * yg) / qq
    lam, u, w = ritz(a, b, c)
    along_p = w / jnp.sqrt(qq)
    along_y = u / jnp.sqrt(yy) - along_p * s
    factors = [along_y, along_y * (shift_ref[0:1, 0:1] - lam), along_p, -lam * along_p]
    size = low_ref.shape[0]
    step = BAND if size % BAND == 0 else size
    sums = None
    for start in range(0, size, step):
        band = slice(start, start + step)
        low_ref[band] = total([factor * term[band] for factor, term in zip(factors, lows)])
        x = along_y * y_ref[band] + along_p * p_ref[band]
        g = along_y * g_ref[band] + along_p * hp_ref[band]
        p = prec[band].astype(F32) * (g - lam * x)
        x_out[band] = x
        p_out[band] = p
        diag = total([factor * term[band] for factor, term in zip(factors, diags)])
        products = [x * p, p * p, p * g, p * diag]
        parts_of = [jnp.sum(value.reshape(-1, ROWS, size), axis=0) for value in products]
        sums = parts_of if sums is None else [one + two for one, two in zip(sums, parts_of)]
    stat_ref[...] = jnp.zeros(stat_ref.shape, F32)
    for row, value in enumerate(sums):
        stat_ref[row : row + 1] = fold(value)
    for i, value in enumerate([along_y, along_p, lam]):
        coefficients[i : i + 1] = jnp.broadcast_to(value, (1, LANES))


def dot(one, two, over):
    dims = ((over[:1], over[1:]), ((), ()))
    return lax.dot_general(one, two, dims, preferred_element_type=F32)


def split(value):
    high = value.astype(BF16)
    return high, (value - high.astype(F32)).astype(BF16)


def product(one, two, over):
    (one_high, one_low), (two_high, two_low) = split(one), split(two)
    return dot(one_high, two_high, over) + (
        dot(one_high, two_low, over) + dot(one_low, two_high, over)
    )


def finish(sums, x_ref, p_ref, coefficients):
    xp, pp, pg, php = sums
    a = coefficients[2:3, 0:1]
    qq = pp - xp * xp
    b = (pg - xp * a) / jnp.sqrt(qq)
    c = (php - 2.0 * xp * pg + xp * xp * a) / qq
    lam, u, w = ritz(a, b, c)
    along_p = w / jnp.sqrt(qq)
    along_x = u - along_p * xp
    return lam, along_x * x_ref[...] + along_p * p_ref[...]


def polarise(x, polar_out, weight_out):
    frob = jnp.sum(jnp.sum(x * x, axis=0, keepdims=True), axis=1, keepdims=True)
    polar = x * lax.rsqrt(frob + 1e-06)
    for _ in range(NS_STEPS):
        narrow = polar.astype(BF16)
        gram = dot(narrow, narrow, (1, 1)).astype(BF16)
        polar = 1.5 * polar - 0.5 * dot(gram, narrow, (1, 0))
    polar_out[...] = polar
    weight_out[0, 0] = product(polar, x, (0, 0)).astype(BF16)


def odd_segment():
    return lax.rem(lax.axis_index("seg"), 2) == 1


def odd_kernel(parts, *refs):
    x_ref, p_ref, coefficients, polar_out, weight_out = refs[parts:]

    @pl.when(odd_segment())
    def _():
        _, x = finish(scalars(refs[:parts], 4), x_ref, p_ref, coefficients)
        polarise(x, polar_out, weight_out)

    @pl.when(jnp.logical_not(odd_segment()))
    def _():
        weight_out[...] = jnp.zeros_like(weight_out)


def even_kernel(parts, *refs):
    x_ref, p_ref, coefficients, _, polar_out, weight_out, lam_out = refs[parts:]

    @pl.when(jnp.logical_not(odd_segment()))
    def _():
        lam, x = finish(scalars(refs[:parts], 4), x_ref, p_ref, coefficients)
        lam_out[0] = lam[0, 0]
        polarise(x, polar_out, weight_out)

    @pl.when(odd_segment())
    def _():
        lam, _ = finish(scalars(refs[:parts], 4), x_ref, p_ref, coefficients)
        lam_out[0] = lam[0, 0]
        weight_out[...] = jnp.zeros_like(weight_out)


def hand_kernel(near, far, out):
    value = jnp.where(odd_segment(), near[...], far[...])
    out[...] = jnp.where(lax.axis_index("seg") > 0, value, jnp.zeros_like(value))


def store_kernel(value, out):
    out[0, 0] = value[...]


def inner_shards(
    left_env, right_env, left_piece, right_piece, guess, inverse_values, precond, sector_rows
):
    left, right, prec = left_env[0, 0], right_env[0, 0], precond[0, 0]
    channels, size = left.shape[0], left.shape[-1]
    matrix = jax.ShapeDtypeStruct((size, size), F32)
    narrow = jax.ShapeDtypeStruct((size, size), BF16)
    stats = jax.ShapeDtypeStruct((ROWS, LANES), F32)
    inner = pltpu.VMEM((size, channels * size), BF16)

    def call(kernel, outs, *operands, scratch=(), in_specs=None, out_specs=None, cost=None, aliases=None):
        return pl.pallas_call(
            kernel,
            out_shape=outs,
            in_specs=in_specs or [VMEM] * len(operands),
            out_specs=out_specs or [VMEM] * len(outs),
            scratch_shapes=list(scratch),
            cost_estimate=cost,
            input_output_aliases=aliases or {},
            compiler_params=pltpu.CompilerParams(vmem_limit_bytes=16 << 20),
        )(*operands)

    (cover,) = call(cover_kernel, [stats], cost=COVER)
    behind = shift(right_piece[0, 0], "seg", -1)
    prec_below = rotate(prec, "sec", 1)
    (mask,) = call(mask_kernel, [matrix], sector_rows, cover)
    scaled = (left_piece[0, 0].astype(F32) * inverse_values[0]).astype(BF16)

    y, yb = call(start_kernel, [matrix, narrow], scaled, behind, guess[0, 0], mask)

    def terms(value):
        return call(terms_kernel, [matrix, matrix], left, right, value, scratch=[inner])

    def joined(below, after, diag, above):
        (up,) = call(raise_kernel, [matrix], left, right, below, after, scratch=[inner])
        outs = [matrix, narrow, narrow]
        return call(join_kernel, outs, diag, up, above, mask, prec)

    y_below = rotate(yb, "sec", 1)
    low, sent = call(start_lower_kernel, [matrix, narrow], left, right, yb, scratch=[inner])
    above = rotate(sent, "sec", -1)
    stat, diag, low_y, diag_y = call(
        start_terms_kernel,
        [stats, matrix, matrix, matrix],
        left, right, y, yb, prec,
        scratch=[inner],
    )
    (stat,) = call(cross_kernel, [stats], y_below, low, stat)
    parts = pairwise(stat, "sec")
    g, gb, pgb = joined(y_below, stat, diag, above)
    g_below = rotate(gb, "sec", 1)
    low_g, diag_g = terms(pgb)
    p, low, sent, diag, stat, ppb, shifted = call(
        functools.partial(first_kernel, len(parts)),
        [matrix, matrix, narrow, matrix, stats, narrow, stats],
        *parts, y, g, prec, low_g, low_y, diag_g, diag_y,
    )
    above = rotate(sent, "sec", -1)
    stat, p_below = call(
        functools.partial(first_cross_kernel, len(parts)),
        [stats, narrow],
        *parts, y_below, g_below, prec_below, low, stat,
    )
    parts = pairwise(stat, "sec")
    hp, hpb, phpb = joined(p_below, stat, diag, above)
    low_p, diag_p = terms(ppb)
    hp_below = rotate(hpb, "sec", 1)
    low_hp, diag_hp = terms(phpb)
    x, p, coefficients, low, stat = call(
        functools.partial(second_kernel, len(parts)),
        [matrix, matrix, stats, matrix, stats],
        *parts, y, g, p, hp, prec, shifted,
        low, low_y, low_hp, low_p, diag, diag_y, diag_hp, diag_p,
    )
    (stat,) = call(
        second_cross_kernel,
        [stats],
        y_below, g_below, p_below, hp_below, prec_below, coefficients, low, stat,
    )
    parts = exchange(stat, "sec")
    block = (1, 1, size, size)
    weight = jax.ShapeDtypeStruct(block, BF16)
    energy = jax.ShapeDtypeStruct((1,), F32)
    operands = (*parts, x, p, coefficients)
    polar, far = call(functools.partial(odd_kernel, len(parts)), [matrix, weight], *operands)
    far = swap(far, "seg", 1, "sec")
    polar, near, energy = call(
        functools.partial(even_kernel, len(parts)),
        [matrix, weight, energy],
        *operands, polar,
        out_specs=[VMEM, VMEM, SMEM],
        aliases={len(operands): 0},
    )
    near = swap(near, "seg", 0, "sec")
    (handed,) = call(hand_kernel, [weight], near, far)
    (polar,) = call(store_kernel, [jax.ShapeDtypeStruct(block, F32)], polar, cost=SHORT)
    return polar, handed, energy


def solution(mesh):
    placed = (
        P("seg", "sec", None, None, None),
        P("seg", "sec", None, None, None),
        P("seg", "sec", None, None),
        P("seg", "sec", None, None),
        P("seg", "sec", None, None),
        P("seg", "sec", None),
        P("seg", "sec", None, None),
        P("seg", "sec"),
    )
    return jax.shard_map(
        inner_shards,
        mesh=mesh,
        in_specs=placed,
        out_specs=(P("seg", "sec", None, None), P("seg", "sec", None, None), P("seg")),
        check_vma=False,
    )
```
